32 devices in a mesh: beam: 8 (over y, x, core), freq: 4 (over z).
Axes of the slice: x: 2, y: 2, z: 4, core: 2. Of those that a mesh axis runs over, the one named last changes fastest.
Arguments:
- intensity: bfloat16 [8, 16384, 256], P(None, ('freq', 'beam')), may hold values from -600 to 600, as said below
- channel_mask: int32 [16384], P('freq'), may hold values 0 or 1
- box_widths: int32 [9], replicated, may hold values from 1 to 64
Outputs:
- snr_peak: float32 [8, 4096], P('beam', 'freq')
The draws below stay inside these ranges and needn't reach their ends.
Inputs may be any that keep to these rules, and one draw needn't show every extreme that they name: `intensity`: filterbank intensities of every beam and channel, of any sign.
All inputs are finite; a program needn't handle non-finite values. No bound on the sum of `channel_mask` on one device may be relied on, other than what follows from the above.
Results may differ from the reference program's by a relative error of at most 0.002.
Values may be sent and summed in bfloat16 or wider, within the bound.
A program may use at most 64 MiB of HBM per device.

```python
import jax
import jax.numpy as jnp
from jax import lax

CHANS = 16384
NDM = 4096
SAMP = 256
NWIDTH = 9
BEAMS = 8


def draw_intensity(key, part):
    key_gain, key_offset, key_noise = jax.random.split(key, 3)
    beam_pos = jnp.arange(BEAMS, dtype=jnp.float32) / max(BEAMS - 1, 1)
    beam_ramp = 3.0 ** beam_pos
    gain_field = beam_ramp[:, None] * jnp.exp(jax.random.uniform(key_gain, (BEAMS, CHANS), jnp.float32, 0.0, 2.302585))
    offsets = jax.random.uniform(key_offset, (BEAMS, CHANS), jnp.float32, -3.0, 3.0) * gain_field
    noise_field = jax.random.normal(key_noise, (BEAMS, CHANS, SAMP), jnp.float32)
    return (offsets[:, :, None] + gain_field[:, :, None] * noise_field).astype(jnp.bfloat16)


def touch_ends(entries, stream_key, low, top_value):
    spot = [jax.random.randint(jax.random.fold_in(stream_key, axis), (), 0, length) for axis, length in enumerate(entries.shape)]
    widest = entries.shape.index(max(entries.shape))
    next_to = spot[:widest] + [(spot[widest] + 1) % entries.shape[widest]] + spot[widest + 1:]
    return entries.at[tuple(spot)].set(low).at[tuple(next_to)].set(top_value)


def setup_inputs(seed: int = 0) -> dict:
    keys = jax.random.split(jax.random.key(seed), 4)
    intensity = draw_intensity(jax.random.fold_in(keys[3], 71), 0)
    channel_mask = touch_ends((jax.random.randint(keys[1], (CHANS,), 0, 8) < 7).astype(jnp.int32), jax.random.fold_in(keys[1], 1), 0, 1)
    box_widths = touch_ends(jax.random.randint(keys[2], (NWIDTH,), 1, 65), jax.random.fold_in(keys[2], 1), 1, 64).astype(jnp.int32)
    return dict(intensity=intensity, channel_mask=channel_mask, box_widths=box_widths)


epsilon = 1e-05

def statistics(channel_sum, squares, channel_mask, row_total):
    channel_mean = channel_sum / row_total
    channel_var = squares / row_total - channel_mean * channel_mean
    channel_scale = lax.rsqrt(channel_var + epsilon) * channel_mask.astype(jnp.float32)
    return (channel_scale, channel_mean)

def advance_ref(row_block, shift_rows):
    samples = row_block.shape[-1]
    padded = jnp.concatenate([row_block, jnp.zeros_like(row_block)], axis=-1)
    time_index = jnp.arange(samples, dtype=jnp.int32)
    gather_index = jnp.minimum(time_index[None, :] + shift_rows[:, None], 2 * samples - 1)
    gather_index = jnp.broadcast_to(gather_index, row_block.shape)
    return jnp.take_along_axis(padded, gather_index, axis=-1)

def dedisperse(band_rows):
    tree_rows = band_rows[:, None, :]
    band_width = 1
    trial_count = 1
    while band_width < CHANS:
        band_width = band_width * 2
        grown = max(1, band_width * NDM // CHANS)
        low_part = tree_rows[0::2]
        high_part = tree_rows[1::2]
        if grown == trial_count:
            tree_rows = low_part + high_part
        else:
            shift_rows = jnp.arange(trial_count, dtype=jnp.int32)
            even_rows = low_part + advance_ref(high_part, shift_rows)
            odd_rows = low_part + advance_ref(high_part, shift_rows + 1)
            tree_rows = jnp.stack([even_rows, odd_rows], axis=2).reshape(low_part.shape[0], 2 * trial_count, SAMP)
        trial_count = grown
    return tree_rows[0]

def boxcar_peaks(series, box_widths):
    samples = series.shape[-1]
    lead_dims = series.shape[:-1]
    prefix = jnp.concatenate([jnp.zeros(lead_dims + (1,), series.dtype), jnp.cumsum(series, axis=-1), jnp.zeros(lead_dims + (samples,), series.dtype)], axis=-1)
    time_index = jnp.arange(samples, dtype=jnp.int32)
    best_peak = None
    for number in range(box_widths.shape[0]):
        box_span = box_widths[number]
        ahead_sum = lax.dynamic_slice_in_dim(prefix, box_span, samples, axis=series.ndim - 1)
        norm_factor = lax.rsqrt((box_span * CHANS).astype(jnp.float32))
        box_sum = (ahead_sum - prefix[..., :samples]) * norm_factor
        box_sum = jnp.where(time_index <= samples - box_span, box_sum, -jnp.inf)
        width_peak = lax.optimization_barrier(jnp.max(box_sum, axis=-1))
        best_peak = width_peak if best_peak is None else jnp.maximum(best_peak, width_peak)
    return best_peak

def reference(intensity, channel_mask, box_widths):
    row_total = float(BEAMS * SAMP)
    channel_sum = lax.optimization_barrier(jnp.sum(intensity.astype(jnp.float32), axis=(0, 2)))
    squares = lax.optimization_barrier(jnp.sum(jnp.square(intensity.astype(jnp.float32)), axis=(0, 2)))
    channel_scale, channel_mean = statistics(channel_sum, squares, channel_mask, row_total)

    def one_beam(beam_rows):
        normed = ((beam_rows.astype(jnp.float32) - channel_mean[:, None]) * channel_scale[:, None]).astype(jnp.bfloat16)
        series = dedisperse(normed.astype(jnp.float32))
        return boxcar_peaks(series, box_widths)
    return lax.map(one_beam, intensity)
```

```python
import jax
import jax.numpy as jnp
from jax import lax
from jax.experimental import pallas as pl
from jax.experimental.pallas import tpu as pltpu
from jax.sharding import PartitionSpec as P

CHANS = 16384
NDM = 4096
LANE_ROWS = 8
LANES = 128
WIDEST = 64

epsilon = 1e-05


def reverse_bits(number, count):
    result = 0
    for _ in range(count):
        result = result << 1 | number & 1
        number >>= 1
    return result


def lane_index(shape):
    return lax.broadcasted_iota(jnp.int32, shape, len(shape) - 1)


def earlier(block, amount):
    if amount == 0:
        return block
    samples = block.shape[-1]
    return jnp.where(lane_index(block.shape) < samples - amount, pltpu.roll(block, samples - amount, 1), 0.0)


def folds(trial_dev, samples):
    return trial_dev >= 4 * samples


def channel_limits(trial_dev, blocks, samples):
    limits = []
    for block in range(blocks):
        limit, rows = CHANS, NDM
        while (block * trial_dev * rows // NDM + 1) // 2 >= samples:
            limit, rows = limit // 2, rows // 2
        limits.append(limit)
    return limits


def entry_kernel(x_hbm, mask_ref, out_ref, x_ref, in_sem, send, send_sem, recv_sem, own_sem):
    blocks, beams, bands, samples = send.shape
    groups = lax.axis_size("beam")
    beam_dev = beams // groups
    width = x_ref.shape[1]
    group = width // (bands * blocks)
    trial_dev = NDM // blocks
    row_total = float(beams * samples)
    fold = folds(trial_dev, samples)
    limits = channel_limits(trial_dev, blocks, samples)
    my_block = lax.axis_index("freq")
    my_group = lax.axis_index("beam")
    my_place = my_block * groups + my_group
    devices = blocks * groups

    barrier = pltpu.get_barrier_semaphore()
    for step in range(1, devices):
        peer = (my_place + step) % devices
        pl.semaphore_signal(
            barrier, inc=1, device_id={"freq": peer // groups, "beam": peer % groups},
            device_id_type=pl.DeviceIdType.MESH,
        )

    chunks = in_sem.shape[0]
    span = width // chunks
    loads = [
        pltpu.make_async_copy(
            x_hbm.at[:, pl.ds(c * span, span)], x_ref.at[:, pl.ds(c * span, span)], in_sem.at[c]
        )
        for c in range(chunks)
    ]
    for load in loads:
        load.start()
    means, scales = [], []
    for c in range(chunks):
        loads[c].wait()
        total = jnp.zeros((span, samples), jnp.float32)
        squares = jnp.zeros((span, samples), jnp.float32)
        for beam in range(beams):
            wide = x_ref[beam, c * span:(c + 1) * span].astype(jnp.float32)
            total = total + wide
            squares = squares + wide * wide
        mean = jnp.sum(total, axis=1, keepdims=True) / row_total
        var = jnp.sum(squares, axis=1, keepdims=True) / row_total - mean * mean
        means.append(mean)
        scales.append(lax.rsqrt(var + epsilon))
    channel_mean = jnp.concatenate(means, axis=0)
    channel_scale = jnp.concatenate(scales, axis=0)
    out_row = lax.broadcasted_iota(jnp.int32, (blocks * bands, width), 0)
    channel = lax.broadcasted_iota(jnp.int32, (blocks * bands, width), 1)
    band = out_row % bands
    if fold:
        half = bands // 2
        band = (band % half) * 2 + band // half
    wanted = band * blocks + out_row // bands
    clean = mask_ref[:, pl.ds(pl.multiple_of(my_group * width, width), width)].astype(jnp.float32)
    chosen = jnp.where(channel // group == wanted, clean, 0.0).astype(jnp.bfloat16)
    upper = my_block * 2 >= blocks

    def message(block, slot, beam, rows):
        return pltpu.make_async_remote_copy(
            src_ref=send.at[block, slot, pl.ds(0, rows)],
            dst_ref=out_ref.at[beam % beam_dev, my_place, pl.ds(0, rows)],
            send_sem=send_sem.at[block, slot],
            recv_sem=recv_sem.at[beam % beam_dev, my_place],
            device_id={"freq": block, "beam": beam // beam_dev},
            device_id_type=pl.DeviceIdType.MESH,
        )

    def own_copy(slot, part):
        return pltpu.make_async_copy(
            send.at[my_block, slot], out_ref.at[part, my_place], own_sem.at[part]
        )

    def every_message(action, slot):
        beam = (my_group * beam_dev + slot) % beams
        for block in range(blocks):
            goes = my_place * width < limits[block]
            if slot < beam_dev:
                goes = goes & (my_block != block)
            if fold:
                @pl.when(goes & upper)
                def _(block=block):
                    action(message(block, slot, beam, bands // 2))
                goes = goes & jnp.logical_not(upper)

            @pl.when(goes)
            def _(block=block):
                action(message(block, slot, beam, bands))

    for slot in range(beams):
        beam = (my_group * beam_dev + slot) % beams
        wide = x_ref[beam].astype(jnp.float32)
        normed = ((wide - channel_mean) * channel_scale).astype(jnp.bfloat16)
        sums = jnp.dot(chosen, normed, preferred_element_type=jnp.float32)
        tree = [[sums[i * bands:(i + 1) * bands]] for i in range(blocks)]
        while len(tree) > 1:
            merged = []
            for low, high in zip(tree[0::2], tree[1::2]):
                merged.append(
                    [low[m // 2] + earlier(high[m // 2], (m + 1) // 2) for m in range(2 * len(low))]
                )
            tree = merged
        for number, row in enumerate(tree[0]):
            if fold:
                both = row[:half] + row[half:]
                row = jnp.concatenate([jnp.where(upper, both, row[:half]), row[half:]], axis=0)
            send[number, slot] = row.astype(jnp.bfloat16)
        if slot == 0:
            pl.semaphore_wait(barrier, devices - 1)
        every_message(lambda copy: copy.start(), slot)
        if slot < beam_dev:
            own_copy(slot, slot).start()

    for slot in range(beam_dev):
        own_copy(slot, slot).wait()
    limit = sum(jnp.where(my_block == block, limits[block], 0) for block in range(blocks))
    for place in range(devices):
        for part in range(beam_dev):
            rows = bands // 2 if fold and 2 * place >= devices else bands
            target = out_ref.at[part, place, pl.ds(0, rows)]
            @pl.when((place * width < limit) & (place != my_place))
            def _(target=target, place=place, part=part):
                pltpu.make_async_remote_copy(
                    src_ref=target, dst_ref=target, send_sem=send_sem.at[0, 0],
                    recv_sem=recv_sem.at[part, place],
                    device_id={"freq": my_block, "beam": my_group},
                    device_id_type=pl.DeviceIdType.MESH,
                ).wait_recv()
    for slot in range(beams):
        every_message(lambda copy: copy.wait_send(), slot)


def entry_rows(intensity, channel_mask):
    beams, width, samples = intensity.shape
    blocks, groups = lax.axis_size("freq"), lax.axis_size("beam")
    bands = width * NDM // (CHANS * blocks)
    beam_dev, devices = beams // groups, blocks * groups
    return pl.pallas_call(
        entry_kernel,
        in_specs=[pl.BlockSpec(memory_space=pl.ANY), pl.BlockSpec(memory_space=pltpu.VMEM)],
        out_specs=pl.BlockSpec(memory_space=pl.ANY),
        scratch_shapes=[
            pltpu.VMEM((beams, width, samples), jnp.bfloat16),
            pltpu.SemaphoreType.DMA((4,)),
            pltpu.VMEM((blocks, beams, bands, samples), jnp.bfloat16),
            pltpu.SemaphoreType.DMA((blocks, beams)),
            pltpu.SemaphoreType.DMA((beam_dev, devices)),
            pltpu.SemaphoreType.DMA((beam_dev,)),
        ],
        out_shape=jax.ShapeDtypeStruct((beam_dev, devices, bands, samples), jnp.bfloat16),
        compiler_params=pltpu.CompilerParams(collective_id=0, has_side_effects=True),
    )(intensity, channel_mask.reshape(1, -1))


def advanced(pieces, amount):
    lanes = pieces[0].shape[-1]
    position = lane_index(pieces[0].shape)
    turn = (lanes - amount) & (lanes - 1)
    turned = [pltpu.roll(piece, turn, 1) for piece in pieces]
    return joined(turned, lambda limit: position < limit - amount)


def advanced_rows(pieces, amounts):
    lanes = pieces[0].shape[-1]
    position = lane_index(pieces[0].shape) + amounts
    picks = position & (lanes - 1)
    turned = [jnp.take_along_axis(piece, picks, axis=1, mode="promise_in_bounds") for piece in pieces]
    return joined(turned, lambda limit: position < limit)


def joined(turned, below):
    lanes = turned[0].shape[-1]
    near = [below((k + 1) * lanes) for k in range(len(turned))]
    result = []
    for number in range(len(turned)):
        value = jnp.zeros_like(turned[0])
        for ahead in reversed(range(len(turned) - number)):
            value = jnp.where(near[ahead], turned[number + ahead], value)
        result.append(value)
    return result


def trial_kernel(place_ref, widths_ref, x_ref, out_ref, first, even, odd, series, prefix):
    total, samples = out_ref.shape[2], x_ref.shape[3]
    tiles = total // LANE_ROWS
    tile_bits = tiles.bit_length() - 1
    lanes = prefix.shape[2]
    parts = samples // lanes
    pitch = first.shape[1] // LANE_ROWS
    block = place_ref[0]
    bands = x_ref.shape[2]
    fold = folds(total, samples)
    half_bands = bands // 2
    sources = x_ref.shape[1]
    for number in range(sources):
        high, start = divmod(number * bands, tiles)
        start += reverse_bits(high, LANE_ROWS.bit_length() - 1) * pitch
        for part in range(parts):
            cut = slice(part * lanes, (part + 1) * lanes)
            if fold and 2 * number >= sources:
                first[part, start:start + half_bands] = x_ref[0, number, :half_bands, cut].astype(jnp.float32)
                first[part, start + half_bands:start + bands] = jnp.zeros((half_bands, lanes), jnp.float32)
            else:
                first[part, start:start + bands] = x_ref[0, number, :, cut].astype(jnp.float32)
    for tile in range(tiles):
        spot = tile
        if fold:
            band = tile % bands
            spot = tile - band + (band % 2) * half_bands + band // 2
        for part in range(parts):
            even[reverse_bits(tile, tile_bits), :, part * lanes:(part + 1) * lanes] = first[
                part, pl.ds(spot, LANE_ROWS, stride=pitch)
            ]

    source, target = even, odd
    count = 1
    while count < tiles:
        half = tiles // count // 2

        def merge(j, source=source, target=target, count=count, half=half):
            flat = (half * LANE_ROWS, lanes)
            cut = [slice(part * lanes, (part + 1) * lanes) for part in range(parts)]
            low = [source[pl.ds(j * 2 * half, half), :, c].reshape(flat) for c in cut]
            high = [source[pl.ds(j * 2 * half + half, half), :, c].reshape(flat) for c in cut]
            for side in range(2):
                moved = advanced(high, block * count + j + side)
                for c, base, extra in zip(cut, low, moved):
                    target[pl.ds((2 * j + side) * half, half), :, c] = (base + extra).reshape(
                        half, LANE_ROWS, lanes
                    )

        if count <= 16:
            for j in range(count):
                merge(j)
        else:
            def step(i, carry, merge=merge):
                for k in range(32):
                    merge(i * 32 + k)
                return carry
            lax.fori_loop(0, count // 32, step, 0)
        source, target = target, source
        count = count * 2

    spot = lax.broadcasted_iota(jnp.int32, (LANE_ROWS, lanes), 0)
    bits = [spot >> 2 & 1, spot >> 1 & 1, spot & 1]
    clear = [bit == 0 for bit in bits]

    def final_rows(j):
        pieces = [source[j, :, part * lanes:(part + 1) * lanes] for part in range(parts)]
        row = spot * 0 + (block * tiles + j)
        for level, reach in enumerate((4, 2, 1)):
            low, high = [], []
            for piece in pieces:
                down = pltpu.roll(piece, reach, 0)
                up = down if 2 * reach == LANE_ROWS else pltpu.roll(piece, LANE_ROWS - reach, 0)
                low.append(jnp.where(clear[level], piece, down))
                high.append(jnp.where(clear[level], up, piece))
            moved = advanced_rows(high, row + bits[level])
            pieces = [base + extra for base, extra in zip(low, moved)]
            row = 2 * row + bits[level]
        return jnp.concatenate(pieces, axis=1)

    def finish(i, carry):
        for k in range(16):
            pair = i * 16 + k
            rows = jnp.concatenate([final_rows(2 * pair), final_rows(2 * pair + 1)], axis=0)
            coarse = rows.astype(jnp.bfloat16)
            place = pl.ds(pl.multiple_of(pair * 16, 16), 16)
            series[place, :samples] = coarse
            series[place, samples:] = (rows - coarse.astype(jnp.float32)).astype(jnp.bfloat16)
        return carry

    lax.fori_loop(0, tiles // 32, finish, 0)

    until = lax.broadcasted_iota(jnp.int32, (samples, 2 * samples), 0)
    time = lax.broadcasted_iota(jnp.int32, (samples, 2 * samples), 1) & (samples - 1)
    ladder = jnp.where(time <= until, 1.0, 0.0).astype(jnp.bfloat16)
    margin = prefix.shape[1] - samples - LANE_ROWS
    piece = 2 * lanes
    for part in range(total // piece):
        sums = lax.dot_general(
            ladder, series[part * piece:(part + 1) * piece], (((1,), (1,)), ((), ())),
            preferred_element_type=jnp.float32,
        )
        for side in range(2):
            column = 2 * part + side
            prefix[column, :LANE_ROWS] = jnp.zeros((LANE_ROWS, lanes), jnp.float32)
            prefix[column, LANE_ROWS:LANE_ROWS + samples] = sums[:, side * lanes:(side + 1) * lanes]
            prefix[column, LANE_ROWS + samples:] = jnp.full((margin, lanes), -jnp.inf, jnp.float32)
    for column in range(total // lanes):
        best = None
        for number in range(widths_ref.shape[0]):
            width = widths_ref[number]
            sums = (
                prefix[column, pl.ds(LANE_ROWS - 1 + width, samples)]
                - prefix[column, LANE_ROWS - 1:LANE_ROWS - 1 + samples]
            )
            norm = lax.rsqrt(jnp.full((1, lanes), width * CHANS, jnp.int32).astype(jnp.float32))
            peak = jnp.max(sums, axis=0, keepdims=True) * norm
            best = peak if best is None else jnp.maximum(best, peak)
        out_ref[0, :, column * lanes:(column + 1) * lanes] = best


def trial_peaks(rows, box_widths, place):
    beams, devices, bands, samples = rows.shape
    total = devices * bands
    tiles = total // LANE_ROWS
    return pl.pallas_call(
        trial_kernel,
        grid_spec=pltpu.PrefetchScalarGridSpec(
            num_scalar_prefetch=2,
            grid=(beams,),
            in_specs=[pl.BlockSpec((1, devices, bands, samples), lambda b, p, w: (b, 0, 0, 0))],
            out_specs=pl.BlockSpec((1, 1, total), lambda b, p, w: (b, 0, 0)),
            scratch_shapes=[
                pltpu.VMEM((samples // LANES, total + LANE_ROWS * LANE_ROWS, LANES), jnp.float32),
                pltpu.VMEM((tiles, LANE_ROWS, samples), jnp.float32),
                pltpu.VMEM((tiles, LANE_ROWS, samples), jnp.float32),
                pltpu.VMEM((total, 2 * samples), jnp.bfloat16),
                pltpu.VMEM((total // LANES, LANE_ROWS + samples + WIDEST, LANES), jnp.float32),
            ],
        ),
        out_shape=jax.ShapeDtypeStruct((beams, 1, total), jnp.float32),
    )(place, box_widths, rows)[:, 0]


def compact(samples, devices, blocks, groups, beams, width):
    return (
        samples == 2 * LANES and NDM == 16 * samples and blocks == 4 and beams == groups
        and devices * LANE_ROWS == samples and width * devices == CHANS
    )


LAYERS = (3, 2, 1, 0)
ORDER = (0, 2, 1, 3)


def device_kind(block, group, groups):
    lower = jnp.where(group * 2 < groups, 0, 1)
    return jnp.where(block == 0, lower, jnp.where(block == 1, 2, 3))


def kind_span(kind):
    return ((0, 8), (0, 8), (2, 8), (3, 6))[kind]


def late_span(place, whole):
    return (0, 8) if place < whole else (4, 8)


def band_mask(kind, width):
    depth = LAYERS[kind]
    rows = LANE_ROWS * (2 << depth)
    row = lax.broadcasted_iota(jnp.int32, (rows, width), 0)
    channel = lax.broadcasted_iota(jnp.int32, (rows, width), 1)
    inner, tile = row % LANE_ROWS, row // LANE_ROWS
    if kind == 3:
        wanted = inner * 2 + tile
    else:
        quarter = tile % 4
        band = inner * 4 + (quarter % 2) * 2 + quarter // 2
        wanted = band * (rows // (4 * LANE_ROWS)) + tile // 4
    return channel // (width * LANE_ROWS // (rows * LANE_ROWS)) == wanted


def stepped(pair, amount):
    if amount == 0:
        return list(pair)
    lane = lane_index(pair[0].shape)
    near = lane < LANES - amount
    turned = [pltpu.roll(piece, LANES - amount, 1) for piece in pair]
    return [jnp.where(near, turned[0], turned[1]), jnp.where(near, turned[1], 0.0)]


def plus(low, high):
    return [a + b for a, b in zip(low, high)]


def leaf_rows(kind, tiles):
    if kind == 3:
        wide = tiles
    else:
        per = len(tiles) // 4
        quarters = [tiles[q] for q in range(4)]
        parts = [[tiles[u * 4 + q] for q in range(4)] for u in range(per)]
        if per == 4:
            one = [plus(parts[0][q], stepped(parts[1][q], 1)) for q in range(4)]
            two = [plus(parts[2][q], stepped(parts[3][q], 1)) for q in range(4)]
            halves = [
                [plus(parts[0][q], parts[1][q]) for q in range(4)],
                [plus(parts[2][q], parts[3][q]) for q in range(4)],
            ]
        elif per == 2:
            halves = parts
        if per >= 2:
            quarters = [plus(halves[0][q], halves[1][q]) for q in range(4)]
        wide = [plus(quarters[0], quarters[2]), plus(quarters[1], quarters[3])]
    zero = plus(wide[0], wide[1])
    first = plus(wide[0], stepped(wide[1], 1))
    message = [None, None, first[0], first[1], zero[0], zero[1], None, None]
    out = {0: message}
    if kind != 3:
        second = [plus(quarters[a], stepped(quarters[2 + a], 1)) for a in range(2)]
        message[0], message[1] = second[0][0], second[1][0]
        message[6], message[7] = second[0][1], second[1][1]
        if per >= 2:
            third = [plus(halves[0][q], stepped(halves[1][q], 1)) for q in range(4)]
            out[1] = [tile[0] for tile in third] + [tile[1] for tile in third]
        if per == 4:
            for block in (2, 3):
                fourth = [plus(one[q], stepped(two[q], block - 1)) for q in range(4)]
                out[block] = [tile[0] for tile in fourth] + [tile[1] for tile in fourth]
    return out


def spread_kernel(x_hbm, mask_ref, out_ref, x_ref, in_sem, send, send_sem, recv_sem, own_sem):
    beams, width, samples = x_ref.shape
    blocks, groups = lax.axis_size("freq"), lax.axis_size("beam")
    devices = blocks * groups
    row_total = float(beams * samples)
    my_block = lax.axis_index("freq")
    my_group = lax.axis_index("beam")
    my_place = my_block * groups + my_group
    kind_here = device_kind(my_block, my_group, groups)
    sources = (devices, groups, groups // 2, groups // 2)

    chunks = in_sem.shape[0]
    span = width // chunks
    loads = [
        pltpu.make_async_copy(
            x_hbm.at[:, pl.ds(c * span, span)], x_ref.at[:, pl.ds(c * span, span)], in_sem.at[c]
        )
        for c in range(chunks)
    ]
    for load in loads:
        load.start()

    barrier = pltpu.get_barrier_semaphore()
    for block in range(blocks):
        @pl.when(my_block == block)
        def _(block=block):
            for step in range(1, devices):
                place = (my_place + step) % devices
                if sources[block] == devices:
                    pl.semaphore_signal(
                        barrier, inc=1, device_id={"freq": place // groups, "beam": place % groups},
                        device_id_type=pl.DeviceIdType.MESH,
                    )
            if sources[block] < devices:
                for place in range(sources[block]):
                    pl.semaphore_signal(
                        barrier, inc=1, device_id={"freq": place // groups, "beam": place % groups},
                        device_id_type=pl.DeviceIdType.MESH,
                    )

    lane = lax.broadcasted_iota(jnp.int32, (LANE_ROWS, LANES), 1)
    inner = lax.broadcasted_iota(jnp.int32, (LANE_ROWS, LANES), 0)
    ones = jnp.ones((2 * LANE_ROWS, samples), jnp.bfloat16)
    dims = (((1,), (1,)), ((), ()))
    means, scales = [], []
    for c in range(chunks):
        loads[c].wait()
        rows = slice(c * span, (c + 1) * span)
        dotted = beams // 2
        flat = jnp.concatenate([x_ref[b, rows] for b in range(dotted)], axis=1)
        rest = jnp.concatenate([x_ref[b, rows] for b in range(dotted, beams)], axis=1)
        gram = lax.dot_general(flat, flat, dims, preferred_element_type=jnp.float32)
        total = lax.dot_general(
            jnp.concatenate([ones] * beams, axis=1), jnp.concatenate([flat, rest], axis=1), dims,
            preferred_element_type=jnp.float32,
        )[:1]
        squares = []
        for column in range(span // LANES):
            sums = jnp.zeros((LANE_ROWS, LANES), jnp.float32)
            for tile in range(LANES // LANE_ROWS):
                at = column * LANES + tile * LANE_ROWS
                own = jnp.zeros((LANE_ROWS, samples), jnp.float32)
                for b in range(dotted, beams):
                    wide = x_ref[b, c * span + at:c * span + at + LANE_ROWS].astype(jnp.float32)
                    own = own + wide * wide
                own = jnp.sum(own, axis=1, keepdims=True)
                both = gram[at:at + LANE_ROWS, column * LANES:(column + 1) * LANES] + own
                sums = sums + jnp.where(lane == inner + tile * LANE_ROWS, both, 0.0)
            squares.append(jnp.sum(sums, axis=0, keepdims=True))
        mean = total / row_total
        var = jnp.concatenate(squares, axis=1) / row_total - mean * mean
        place = pl.multiple_of(my_group * width + c * span, span)
        clean = mask_ref[:, pl.ds(place, span)].astype(jnp.float32)
        means.append(mean)
        scales.append(lax.rsqrt(var + epsilon) * clean)
    channel_mean = jnp.concatenate(means, axis=1)
    channel_scale = jnp.concatenate(scales, axis=1)
    coarse = channel_scale.astype(jnp.bfloat16).astype(jnp.float32)
    fine = (channel_scale - coarse).astype(jnp.bfloat16).astype(jnp.float32)
    offset = channel_mean * (coarse + fine)

    def message(block, slot, first, last):
        beam = (my_group + slot) % beams
        return pltpu.make_async_remote_copy(
            src_ref=send.at[block, slot, pl.ds(first, last - first)],
            dst_ref=out_ref.at[0, my_place, pl.ds(first, last - first)],
            send_sem=send_sem.at[block, slot],
            recv_sem=recv_sem.at[my_place],
            device_id={"freq": block, "beam": beam},
            device_id_type=pl.DeviceIdType.MESH,
        )

    def own_copy():
        return pltpu.make_async_copy(send.at[0, 0], out_ref.at[0, my_place], own_sem.at[0])

    def outgoing(action, kind, slot):
        if kind < 2 and slot == 0:
            pass
        else:
            action(message(0, slot, *kind_span(kind)))
        if kind == 0:
            action(message(1, slot, 0, 8))
            for half in range(2):
                @pl.when((my_group * 4 >= groups) if half else (my_group * 4 < groups))
                def _(half=half):
                    for block in (2, 3):
                        action(message(block, slot, 4 * half, 8))
        if kind == 1:
            action(message(1, slot, 4, 8))

    targets = (devices - 1, 2 * groups - 1, groups, groups)
    for kind in range(4):
        @pl.when(kind_here == kind)
        def _(kind=kind):
            chosen = band_mask(kind, width)
            rows = chosen.shape[0]
            matrix = jnp.concatenate(
                [jnp.where(chosen, coarse, 0.0), jnp.where(chosen, fine, 0.0)], axis=0
            ).astype(jnp.bfloat16)
            shift = jnp.sum(jnp.where(chosen, offset, 0.0), axis=1, keepdims=True)
            for slot in range(beams):
                beam = (my_group + slot) % beams
                both = jnp.dot(matrix, x_ref[beam], preferred_element_type=jnp.float32)
                sums = both[:rows] + both[rows:] - shift
                tiles = [
                    [sums[t * LANE_ROWS:(t + 1) * LANE_ROWS, p * LANES:(p + 1) * LANES] for p in range(2)]
                    for t in range(rows // LANE_ROWS)
                ]
                for block, leaves in leaf_rows(kind, tiles).items():
                    for number, leaf in enumerate(leaves):
                        if leaf is not None:
                            send[block, slot, number] = leaf.astype(jnp.bfloat16)
                if slot == 0:
                    pl.semaphore_wait(barrier, targets[kind])
                outgoing(lambda copy: copy.start(), kind, slot)
                if kind < 2 and slot == 0:
                    own_copy().start()

    def arrival(place, first, last):
        target = out_ref.at[0, place, pl.ds(first, last - first)]
        pltpu.make_async_remote_copy(
            src_ref=target, dst_ref=target, send_sem=send_sem.at[0, 0], recv_sem=recv_sem.at[place],
            device_id={"freq": my_block, "beam": my_group}, device_id_type=pl.DeviceIdType.MESH,
        ).wait_recv()

    @pl.when(my_block == 0)
    def _():
        own_copy().wait()
        for place in range(devices):
            kind = max(place // groups, 0)
            extent = kind_span(0 if kind == 0 else min(kind + 1, 3))

            @pl.when(place != my_place)
            def _(place=place, extent=extent):
                arrival(place, *extent)

    @pl.when(my_block == 1)
    def _():
        for place in range(groups):
            arrival(place, *late_span(place, groups // 2))

    @pl.when(my_block > 1)
    def _():
        for place in range(groups // 2):
            arrival(place, *late_span(place, groups // 4))

    for kind in range(4):
        @pl.when(kind_here == kind)
        def _(kind=kind):
            for slot in range(beams):
                outgoing(lambda copy: copy.wait_send(), kind, slot)


def spread_rows(intensity, channel_mask):
    beams, width, samples = intensity.shape
    blocks, groups = lax.axis_size("freq"), lax.axis_size("beam")
    devices = blocks * groups
    return pl.pallas_call(
        spread_kernel,
        in_specs=[pl.BlockSpec(memory_space=pl.ANY), pl.BlockSpec(memory_space=pltpu.VMEM)],
        out_specs=pl.BlockSpec(memory_space=pl.ANY),
        scratch_shapes=[
            pltpu.VMEM((beams, width, samples), jnp.bfloat16),
            pltpu.SemaphoreType.DMA((2,)),
            pltpu.VMEM((blocks, beams, 8, LANE_ROWS, LANES), jnp.bfloat16),
            pltpu.SemaphoreType.DMA((blocks, beams)),
            pltpu.SemaphoreType.DMA((devices,)),
            pltpu.SemaphoreType.DMA((1,)),
        ],
        out_shape=jax.ShapeDtypeStruct((1, devices, 8, LANE_ROWS, LANES), jnp.bfloat16),
        compiler_params=pltpu.CompilerParams(collective_id=0, has_side_effects=True),
    )(intensity, channel_mask.reshape(1, -1))


def ramped(pair, start, stride, far, only_late=False):
    shape = pair[1].shape
    place = lane_index(shape) + (lax.broadcasted_iota(jnp.int32, shape, 0) * stride + start)
    picks = place & (LANES - 1)
    late = jnp.take_along_axis(pair[1], picks, axis=1, mode="promise_in_bounds")
    if far:
        return [jnp.where(place < 2 * LANES, late, 0.0), None]
    near = place < LANES
    moved = [None, jnp.where(near, late, 0.0)]
    if not only_late:
        early = jnp.take_along_axis(pair[0], picks, axis=1, mode="promise_in_bounds")
        moved[0] = jnp.where(near, early, late)
    return moved


def joined_pair(low, high):
    return [a if b is None else (None if a is None else a + b) for a, b in zip(low, high)]


def unit_rows(x_ref, first, work, mid, series, base, root, leaves, kinds, found):
    tiles = leaves // LANE_ROWS
    pitch = first.shape[1] // LANE_ROWS
    for address, place, numbers in found:
        for part in range(2):
            if numbers[part] is not None:
                first[part, address:address + LANE_ROWS] = x_ref[0, place, numbers[part]].astype(jnp.float32)

    def leaf(tile, part):
        outer, kind = tile >> kinds, tile & ((1 << kinds) - 1)
        if leaves == LANE_ROWS * (pitch - LANE_ROWS):
            spot, step = ((outer >> 3 << kinds) + kind) * LANE_ROWS + (outer & 7), pitch
        else:
            spot, step = kind * pitch + outer, LANE_ROWS // 2
        return first[part, pl.ds(spot, LANE_ROWS, stride=step)]

    chunk = 8
    for c in range(tiles // chunk):
        tree = [[[leaf(c * chunk + k, part) for part in range(2)]] for k in range(chunk)]
        level_root = root
        while len(tree) > 1:
            tree = [
                [
                    plus(low[r // 2], stepped(high[r // 2], level_root + r // 2 + r % 2))
                    for r in range(2 * len(low))
                ]
                for low, high in zip(tree[0::2], tree[1::2])
            ]
            level_root = level_root * 2
        for j in range(chunk):
            for part in range(2):
                at = (j * (tiles // chunk) + c) * LANE_ROWS
                work[part, at:at + LANE_ROWS] = tree[0][j][part]
    chunks = tiles // chunk
    for j in range(chunk):
        tree = []
        for c in range(chunks):
            at = (j * chunks + c) * LANE_ROWS
            tree.append([[work[part, at:at + LANE_ROWS] for part in range(2)]])
        level_root = root * chunk + j
        while len(tree) > 1:
            tree = [
                [
                    plus(low[r // 2], stepped(high[r // 2], level_root + r // 2 + r % 2))
                    for r in range(2 * len(low))
                ]
                for low, high in zip(tree[0::2], tree[1::2])
            ]
            level_root = level_root * 2
        for k in range(chunks):
            for part in range(2):
                at = (j * chunks + k) * LANE_ROWS
                mid[part, at:at + LANE_ROWS] = tree[0][k][part]
    far = root > 0
    for g in range(tiles // LANE_ROWS):
        tree = []
        for s in range(LANE_ROWS):
            pair = [
                None if far and 2 * s >= LANE_ROWS and part == 0
                else mid[part, pl.ds(g * LANE_ROWS * LANE_ROWS + s, LANE_ROWS, stride=LANE_ROWS)]
                for part in range(2)
            ]
            tree.append([pair])
        start, stride = root * tiles + g * LANE_ROWS, 1
        while len(tree) > 1:
            last = len(tree) == 2
            merged = []
            for number in range(len(tree) // 2):
                low, high = tree[2 * number], tree[2 * number + 1]
                rows = []
                for r in range(2 * len(low)):
                    source = r // 2
                    begin = start + source + r % 2
                    missing = high[source][0] is None
                    moved = ramped(high[source], begin, stride, far and last, missing)
                    rows.append(joined_pair(low[source], moved))
                merged.append(rows)
            tree = merged
            start, stride = start * 2, stride * 2
        for k in range(0, LANE_ROWS, 2):
            rows = jnp.concatenate(
                [jnp.concatenate(tree[0][k + half], axis=1) for half in range(2)], axis=0
            )
            coarse = rows.astype(jnp.bfloat16)
            at = base + g * 64 + k * LANE_ROWS
            samples = rows.shape[1]
            series[at:at + 2 * LANE_ROWS, :samples] = coarse
            series[at:at + 2 * LANE_ROWS, samples:] = (rows - coarse.astype(jnp.float32)).astype(jnp.bfloat16)


def boxcar_rows(widths_ref, series, prefix, columns):
    lanes = prefix.shape[2]
    samples = series.shape[1] // 2
    until = lax.broadcasted_iota(jnp.int32, (samples, 2 * samples), 0)
    time = lax.broadcasted_iota(jnp.int32, (samples, 2 * samples), 1) & (samples - 1)
    ladder = jnp.where(time <= until, 1.0, 0.0).astype(jnp.bfloat16)
    margin = prefix.shape[1] - samples - LANE_ROWS
    piece = min(2, columns)
    for part in range(columns // piece):
        sums = lax.dot_general(
            ladder, series[part * piece * lanes:(part + 1) * piece * lanes], (((1,), (1,)), ((), ())),
            preferred_element_type=jnp.float32,
        )
        for side in range(piece):
            column = piece * part + side
            prefix[column, :LANE_ROWS] = jnp.zeros((LANE_ROWS, lanes), jnp.float32)
            prefix[column, LANE_ROWS:LANE_ROWS + samples] = sums[:, side * lanes:(side + 1) * lanes]
            prefix[column, LANE_ROWS + samples:] = jnp.full((margin, lanes), -jnp.inf, jnp.float32)
    result = []
    for column in range(columns):
        best = None
        for number in range(widths_ref.shape[0]):
            width = widths_ref[number]
            sums = (
                prefix[column, pl.ds(LANE_ROWS - 1 + width, samples)]
                - prefix[column, LANE_ROWS - 1:LANE_ROWS - 1 + samples]
            )
            norm = lax.rsqrt(jnp.full((1, lanes), width * CHANS, jnp.int32).astype(jnp.float32))
            peak = jnp.max(sums, axis=0, keepdims=True) * norm
            best = peak if best is None else jnp.maximum(best, peak)
        result.append(jnp.broadcast_to(best, (LANE_ROWS, lanes)))
    return result


def unpermuted(columns, out_ref, offset, repeat_bits):
    lane = lane_index((LANE_ROWS, LANES))
    for number in range(len(columns) << repeat_bits):
        row = (lane + number * LANES) >> repeat_bits
        row = row & (LANES - 1)
        picks = (row & 64) + (row & 7) * LANE_ROWS + ((row >> 3) & 7)
        column = columns[number >> repeat_bits]
        spread = jnp.take_along_axis(column, picks, axis=1, mode="promise_in_bounds")
        at = offset + number * LANES
        out_ref[0, :, at:at + LANES] = spread[:1]


def peaks_kernel(widths_ref, x_ref, out_ref, first, work, mid, series, prefix):
    block = lax.axis_index("freq")
    groups = lax.axis_size("beam")
    pitch = first.shape[1] // LANE_ROWS
    args = (x_ref, first, work, mid, series)

    def wide_places(devices, numbers_of):
        found = []
        per = devices // LANE_ROWS
        for place in range(devices):
            s, b = divmod(place, per)
            for address, numbers in numbers_of(place):
                found.append((s * pitch + b * (pitch - LANE_ROWS) // per + address, place, numbers))
        return found

    @pl.when(block == 0)
    def _():
        unit_rows(*args, 512, 1, 256, 1, wide_places(
            2 * groups,
            lambda place: [(8 * a, (a if place < groups else None, 6 + a)) for a in range(2)],
        ))
        unit_rows(*args, 256, 1, 256, 0, wide_places(
            4 * groups, lambda place: [(0, (2 if place < 2 * groups else None, 3))],
        ))
        unit_rows(*args, 0, 0, 256, 0, wide_places(4 * groups, lambda place: [(0, (4, 5))]))
        result = boxcar_rows(widths_ref, series, prefix, 6)
        unpermuted(result[:4], out_ref, 0, 0)
        unpermuted(result[4:], out_ref, 512, 1)

    @pl.when(block == 1)
    def _():
        unit_rows(*args, 0, 1, 256, 2, wide_places(
            groups,
            lambda place: [
                (8 * (2 * (q % 2) + q // 2), (q if 2 * place < groups else None, 4 + q)) for q in range(4)
            ],
        ))
        unpermuted(boxcar_rows(widths_ref, series, prefix, 2), out_ref, 0, 2)

    for late in (2, 3):
        @pl.when(block == late)
        def _(late=late):
            found = []
            for place in range(groups // 2):
                for q in range(4):
                    found.append((
                        (2 * (q % 2) + q // 2) * pitch + place * LANE_ROWS, place,
                        (q if 4 * place < groups else None, 4 + q),
                    ))
            unit_rows(*args, 0, late, 128, 2, found)
            unpermuted(boxcar_rows(widths_ref, series, prefix, 1), out_ref, 0, 3)


def beam_peaks(rows, box_widths):
    samples = 2 * LANES
    total = 4 * samples
    return pl.pallas_call(
        peaks_kernel,
        grid_spec=pltpu.PrefetchScalarGridSpec(
            num_scalar_prefetch=1,
            grid=(1,),
            in_specs=[pl.BlockSpec(rows.shape, lambda b, w: (0, 0, 0, 0, 0))],
            out_specs=pl.BlockSpec((1, 1, total), lambda b, w: (0, 0, 0)),
            scratch_shapes=[
                pltpu.VMEM((2, samples + LANE_ROWS * LANE_ROWS, LANES), jnp.float32),
                pltpu.VMEM((2, samples, LANES), jnp.float32),
                pltpu.VMEM((2, samples, LANES), jnp.float32),
                pltpu.VMEM((3 * samples, 2 * samples), jnp.bfloat16),
                pltpu.VMEM((6, LANE_ROWS + samples + WIDEST, LANES), jnp.float32),
            ],
        ),
        out_shape=jax.ShapeDtypeStruct((1, 1, total), jnp.float32),
    )(box_widths, rows)[:, 0]


def shards(intensity, channel_mask, box_widths):
    beams, width, samples = intensity.shape
    blocks, groups = lax.axis_size("freq"), lax.axis_size("beam")
    if compact(samples, blocks * groups, blocks, groups, beams, width):
        return beam_peaks(spread_rows(intensity, channel_mask), box_widths)
    rows = entry_rows(intensity, channel_mask)
    return trial_peaks(rows, box_widths, lax.axis_index("freq").reshape(1))


def solution(mesh):
    in_specs = (P(None, ("freq", "beam"), None), P("freq"), P())
    out_specs = P("beam", "freq")
    return jax.shard_map(shards, mesh=mesh, in_specs=in_specs, out_specs=out_specs, check_vma=False)
```

```python
import jax
import jax.numpy as jnp
from jax import lax
from jax.experimental import pallas as pl
from jax.experimental.pallas import tpu as pltpu
from jax.sharding import PartitionSpec as P

CHANS = 16384
NDM = 4096
LANE_ROWS = 8
LANES = 128
WIDEST = 64

epsilon = 1e-05


def reverse_bits(number, count):
    result = 0
    for _ in range(count):
        result = result << 1 | number & 1
        number >>= 1
    return result


def lane_index(shape):
    return lax.broadcasted_iota(jnp.int32, shape, len(shape) - 1)


def earlier(block, amount):
    if amount == 0:
        return block
    samples = block.shape[-1]
    return jnp.where(lane_index(block.shape) < samples - amount, pltpu.roll(block, samples - amount, 1), 0.0)


def folds(trial_dev, samples):
    return trial_dev >= 4 * samples


def channel_limits(trial_dev, blocks, samples):
    limits = []
    for block in range(blocks):
        limit, rows = CHANS, NDM
        while (block * trial_dev * rows // NDM + 1) // 2 >= samples:
            limit, rows = limit // 2, rows // 2
        limits.append(limit)
    return limits


def entry_kernel(x_hbm, mask_ref, out_ref, x_ref, in_sem, send, send_sem, recv_sem, own_sem):
    blocks, beams, bands, samples = send.shape
    groups = lax.axis_size("beam")
    beam_dev = beams // groups
    width = x_ref.shape[1]
    group = width // (bands * blocks)
    trial_dev = NDM // blocks
    row_total = float(beams * samples)
    fold = folds(trial_dev, samples)
    limits = channel_limits(trial_dev, blocks, samples)
    my_block = lax.axis_index("freq")
    my_group = lax.axis_index("beam")
    my_place = my_block * groups + my_group
    devices = blocks * groups

    barrier = pltpu.get_barrier_semaphore()
    for step in range(1, devices):
        peer = (my_place + step) % devices
        pl.semaphore_signal(
            barrier, inc=1, device_id={"freq": peer // groups, "beam": peer % groups},
            device_id_type=pl.DeviceIdType.MESH,
        )

    chunks = in_sem.shape[0]
    span = width // chunks
    loads = [
        pltpu.make_async_copy(
            x_hbm.at[:, pl.ds(c * span, span)], x_ref.at[:, pl.ds(c * span, span)], in_sem.at[c]
        )
        for c in range(chunks)
    ]
    for load in loads:
        load.start()
    means, scales = [], []
    for c in range(chunks):
        loads[c].wait()
        total = jnp.zeros((span, samples), jnp.float32)
        squares = jnp.zeros((span, samples), jnp.float32)
        for beam in range(beams):
            wide = x_ref[beam, c * span:(c + 1) * span].astype(jnp.float32)
            total = total + wide
            squares = squares + wide * wide
        mean = jnp.sum(total, axis=1, keepdims=True) / row_total
        var = jnp.sum(squares, axis=1, keepdims=True) / row_total - mean * mean
        means.append(mean)
        scales.append(lax.rsqrt(var + epsilon))
    channel_mean = jnp.concatenate(means, axis=0)
    channel_scale = jnp.concatenate(scales, axis=0)
    out_row = lax.broadcasted_iota(jnp.int32, (blocks * bands, width), 0)
    channel = lax.broadcasted_iota(jnp.int32, (blocks * bands, width), 1)
    band = out_row % bands
    if fold:
        half = bands // 2
        band = (band % half) * 2 + band // half
    wanted = band * blocks + out_row // bands
    clean = mask_ref[:, pl.ds(pl.multiple_of(my_group * width, width), width)].astype(jnp.float32)
    chosen = jnp.where(channel // group == wanted, clean, 0.0).astype(jnp.bfloat16)
    upper = my_block * 2 >= blocks

    def message(block, slot, beam, rows):
        return pltpu.make_async_remote_copy(
            src_ref=send.at[block, slot, pl.ds(0, rows)],
            dst_ref=out_ref.at[beam % beam_dev, my_place, pl.ds(0, rows)],
            send_sem=send_sem.at[block, slot],
            recv_sem=recv_sem.at[beam % beam_dev, my_place],
            device_id={"freq": block, "beam": beam // beam_dev},
            device_id_type=pl.DeviceIdType.MESH,
        )

    def own_copy(slot, part):
        return pltpu.make_async_copy(
            send.at[my_block, slot], out_ref.at[part, my_place], own_sem.at[part]
        )

    def every_message(action, slot):
        beam = (my_group * beam_dev + slot) % beams
        for block in range(blocks):
            goes = my_place * width < limits[block]
            if slot < beam_dev:
                goes = goes & (my_block != block)
            if fold:
                @pl.when(goes & upper)
                def _(block=block):
                    action(message(block, slot, beam, bands // 2))
                goes = goes & jnp.logical_not(upper)

            @pl.when(goes)
            def _(block=block):
                action(message(block, slot, beam, bands))

    for slot in range(beams):
        beam = (my_group * beam_dev + slot) % beams
        wide = x_ref[beam].astype(jnp.float32)
        normed = ((wide - channel_mean) * channel_scale).astype(jnp.bfloat16)
        sums = jnp.dot(chosen, normed, preferred_element_type=jnp.float32)
        tree = [[sums[i * bands:(i + 1) * bands]] for i in range(blocks)]
        while len(tree) > 1:
            merged = []
            for low, high in zip(tree[0::2], tree[1::2]):
                merged.append(
                    [low[m // 2] + earlier(high[m // 2], (m + 1) // 2) for m in range(2 * len(low))]
                )
            tree = merged
        for number, row in enumerate(tree[0]):
            if fold:
                both = row[:half] + row[half:]
                row = jnp.concatenate([jnp.where(upper, both, row[:half]), row[half:]], axis=0)
            send[number, slot] = row.astype(jnp.bfloat16)
        if slot == 0:
            pl.semaphore_wait(barrier, devices - 1)
        every_message(lambda copy: copy.start(), slot)
        if slot < beam_dev:
            own_copy(slot, slot).start()

    for slot in range(beam_dev):
        own_copy(slot, slot).wait()
    limit = sum(jnp.where(my_block == block, limits[block], 0) for block in range(blocks))
    for place in range(devices):
        for part in range(beam_dev):
            rows = bands // 2 if fold and 2 * place >= devices else bands
            target = out_ref.at[part, place, pl.ds(0, rows)]
            @pl.when((place * width < limit) & (place != my_place))
            def _(target=target, place=place, part=part):
                pltpu.make_async_remote_copy(
                    src_ref=target, dst_ref=target, send_sem=send_sem.at[0, 0],
                    recv_sem=recv_sem.at[part, place],
                    device_id={"freq": my_block, "beam": my_group},
                    device_id_type=pl.DeviceIdType.MESH,
                ).wait_recv()
    for slot in range(beams):
        every_message(lambda copy: copy.wait_send(), slot)


def entry_rows(intensity, channel_mask):
    beams, width, samples = intensity.shape
    blocks, groups = lax.axis_size("freq"), lax.axis_size("beam")
    bands = width * NDM // (CHANS * blocks)
    beam_dev, devices = beams // groups, blocks * groups
    return pl.pallas_call(
        entry_kernel,
        in_specs=[pl.BlockSpec(memory_space=pl.ANY), pl.BlockSpec(memory_space=pltpu.VMEM)],
        out_specs=pl.BlockSpec(memory_space=pl.ANY),
        scratch_shapes=[
            pltpu.VMEM((beams, width, samples), jnp.bfloat16),
            pltpu.SemaphoreType.DMA((4,)),
            pltpu.VMEM((blocks, beams, bands, samples), jnp.bfloat16),
            pltpu.SemaphoreType.DMA((blocks, beams)),
            pltpu.SemaphoreType.DMA((beam_dev, devices)),
            pltpu.SemaphoreType.DMA((beam_dev,)),
        ],
        out_shape=jax.ShapeDtypeStruct((beam_dev, devices, bands, samples), jnp.bfloat16),
        compiler_params=pltpu.CompilerParams(collective_id=0, has_side_effects=True),
    )(intensity, channel_mask.reshape(1, -1))


def advanced(pieces, amount):
    lanes = pieces[0].shape[-1]
    position = lane_index(pieces[0].shape)
    turn = (lanes - amount) & (lanes - 1)
    turned = [pltpu.roll(piece, turn, 1) for piece in pieces]
    return joined(turned, lambda limit: position < limit - amount)


def advanced_rows(pieces, amounts):
    lanes = pieces[0].shape[-1]
    position = lane_index(pieces[0].shape) + amounts
    picks = position & (lanes - 1)
    turned = [jnp.take_along_axis(piece, picks, axis=1, mode="promise_in_bounds") for piece in pieces]
    return joined(turned, lambda limit: position < limit)


def joined(turned, below):
    lanes = turned[0].shape[-1]
    near = [below((k + 1) * lanes) for k in range(len(turned))]
    result = []
    for number in range(len(turned)):
        value = jnp.zeros_like(turned[0])
        for ahead in reversed(range(len(turned) - number)):
            value = jnp.where(near[ahead], turned[number + ahead], value)
        result.append(value)
    return result


def trial_kernel(place_ref, widths_ref, x_ref, out_ref, first, even, odd, series, prefix):
    total, samples = out_ref.shape[2], x_ref.shape[3]
    tiles = total // LANE_ROWS
    tile_bits = tiles.bit_length() - 1
    lanes = prefix.shape[2]
    parts = samples // lanes
    pitch = first.shape[1] // LANE_ROWS
    block = place_ref[0]
    bands = x_ref.shape[2]
    fold = folds(total, samples)
    half_bands = bands // 2
    sources = x_ref.shape[1]
    for number in range(sources):
        high, start = divmod(number * bands, tiles)
        start += reverse_bits(high, LANE_ROWS.bit_length() - 1) * pitch
        for part in range(parts):
            cut = slice(part * lanes, (part + 1) * lanes)
            if fold and 2 * number >= sources:
                first[part, start:start + half_bands] = x_ref[0, number, :half_bands, cut].astype(jnp.float32)
                first[part, start + half_bands:start + bands] = jnp.zeros((half_bands, lanes), jnp.float32)
            else:
                first[part, start:start + bands] = x_ref[0, number, :, cut].astype(jnp.float32)
    for tile in range(tiles):
        spot = tile
        if fold:
            band = tile % bands
            spot = tile - band + (band % 2) * half_bands + band // 2
        for part in range(parts):
            even[reverse_bits(tile, tile_bits), :, part * lanes:(part + 1) * lanes] = first[
                part, pl.ds(spot, LANE_ROWS, stride=pitch)
            ]

    source, target = even, odd
    count = 1
    while count < tiles:
        half = tiles // count // 2

        def merge(j, source=source, target=target, count=count, half=half):
            flat = (half * LANE_ROWS, lanes)
            cut = [slice(part * lanes, (part + 1) * lanes) for part in range(parts)]
            low = [source[pl.ds(j * 2 * half, half), :, c].reshape(flat) for c in cut]
            high = [source[pl.ds(j * 2 * half + half, half), :, c].reshape(flat) for c in cut]
            for side in range(2):
                moved = advanced(high, block * count + j + side)
                for c, base, extra in zip(cut, low, moved):
                    target[pl.ds((2 * j + side) * half, half), :, c] = (base + extra).reshape(
                        half, LANE_ROWS, lanes
                    )

        if count <= 16:
            for j in range(count):
                merge(j)
        else:
            def step(i, carry, merge=merge):
                for k in range(32):
                    merge(i * 32 + k)
                return carry
            lax.fori_loop(0, count // 32, step, 0)
        source, target = target, source
        count = count * 2

    spot = lax.broadcasted_iota(jnp.int32, (LANE_ROWS, lanes), 0)
    bits = [spot >> 2 & 1, spot >> 1 & 1, spot & 1]
    clear = [bit == 0 for bit in bits]

    def final_rows(j):
        pieces = [source[j, :, part * lanes:(part + 1) * lanes] for part in range(parts)]
        row = spot * 0 + (block * tiles + j)
        for level, reach in enumerate((4, 2, 1)):
            low, high = [], []
            for piece in pieces:
                down = pltpu.roll(piece, reach, 0)
                up = down if 2 * reach == LANE_ROWS else pltpu.roll(piece, LANE_ROWS - reach, 0)
                low.append(jnp.where(clear[level], piece, down))
                high.append(jnp.where(clear[level], up, piece))
            moved = advanced_rows(high, row + bits[level])
            pieces = [base + extra for base, extra in zip(low, moved)]
            row = 2 * row + bits[level]
        return jnp.concatenate(pieces, axis=1)

    def finish(i, carry):
        for k in range(16):
            pair = i * 16 + k
            rows = jnp.concatenate([final_rows(2 * pair), final_rows(2 * pair + 1)], axis=0)
            coarse = rows.astype(jnp.bfloat16)
            place = pl.ds(pl.multiple_of(pair * 16, 16), 16)
            series[place, :samples] = coarse
            series[place, samples:] = (rows - coarse.astype(jnp.float32)).astype(jnp.bfloat16)
        return carry

    lax.fori_loop(0, tiles // 32, finish, 0)

    until = lax.broadcasted_iota(jnp.int32, (samples, 2 * samples), 0)
    time = lax.broadcasted_iota(jnp.int32, (samples, 2 * samples), 1) & (samples - 1)
    ladder = jnp.where(time <= until, 1.0, 0.0).astype(jnp.bfloat16)
    margin = prefix.shape[1] - samples - LANE_ROWS
    piece = 2 * lanes
    for part in range(total // piece):
        sums = lax.dot_general(
            ladder, series[part * piece:(part + 1) * piece], (((1,), (1,)), ((), ())),
            preferred_element_type=jnp.float32,
        )
        for side in range(2):
            column = 2 * part + side
            prefix[column, :LANE_ROWS] = jnp.zeros((LANE_ROWS, lanes), jnp.float32)
            prefix[column, LANE_ROWS:LANE_ROWS + samples] = sums[:, side * lanes:(side + 1) * lanes]
            prefix[column, LANE_ROWS + samples:] = jnp.full((margin, lanes), -jnp.inf, jnp.float32)
    for column in range(total // lanes):
        best = None
        for number in range(widths_ref.shape[0]):
            width = widths_ref[number]
            sums = (
                prefix[column, pl.ds(LANE_ROWS - 1 + width, samples)]
                - prefix[column, LANE_ROWS - 1:LANE_ROWS - 1 + samples]
            )
            norm = lax.rsqrt(jnp.full((1, lanes), width * CHANS, jnp.int32).astype(jnp.float32))
            peak = jnp.max(sums, axis=0, keepdims=True) * norm
            best = peak if best is None else jnp.maximum(best, peak)
        out_ref[0, :, column * lanes:(column + 1) * lanes] = best


def trial_peaks(rows, box_widths, place):
    beams, devices, bands, samples = rows.shape
    total = devices * bands
    tiles = total // LANE_ROWS
    return pl.pallas_call(
        trial_kernel,
        grid_spec=pltpu.PrefetchScalarGridSpec(
            num_scalar_prefetch=2,
            grid=(beams,),
            in_specs=[pl.BlockSpec((1, devices, bands, samples), lambda b, p, w: (b, 0, 0, 0))],
            out_specs=pl.BlockSpec((1, 1, total), lambda b, p, w: (b, 0, 0)),
            scratch_shapes=[
                pltpu.VMEM((samples // LANES, total + LANE_ROWS * LANE_ROWS, LANES), jnp.float32),
                pltpu.VMEM((tiles, LANE_ROWS, samples), jnp.float32),
                pltpu.VMEM((tiles, LANE_ROWS, samples), jnp.float32),
                pltpu.VMEM((total, 2 * samples), jnp.bfloat16),
                pltpu.VMEM((total // LANES, LANE_ROWS + samples + WIDEST, LANES), jnp.float32),
            ],
        ),
        out_shape=jax.ShapeDtypeStruct((beams, 1, total), jnp.float32),
    )(place, box_widths, rows)[:, 0]


def compact(samples, devices, blocks, groups, beams, width):
    return (
        samples == 2 * LANES and NDM == 16 * samples and blocks == 4 and beams == groups
        and devices * LANE_ROWS == samples and width * devices == CHANS
    )


def block_span(block):
    return ((0, 8), (2, 8), (3, 6), (3, 6))[block]


def late_span(place, whole):
    return (0, 8) if place < whole else (4, 8)


def band_mask(depth, width):
    rows = LANE_ROWS * (2 << depth)
    row = lax.broadcasted_iota(jnp.int32, (rows, width), 0)
    channel = lax.broadcasted_iota(jnp.int32, (rows, width), 1)
    inner, tile = row % LANE_ROWS, row // LANE_ROWS
    if depth == 0:
        wanted = inner * 2 + tile
    else:
        quarter = tile % 4
        band = inner * 4 + (quarter % 2) * 2 + quarter // 2
        wanted = band * (rows // (4 * LANE_ROWS)) + tile // 4
    return channel // (width // rows) == wanted


def stepped(pair, amount):
    if amount == 0:
        return list(pair)
    lane = lane_index(pair[0].shape)
    near = lane < LANES - amount
    turned = [pltpu.roll(piece, LANES - amount, 1) for piece in pair]
    return [jnp.where(near, turned[0], turned[1]), jnp.where(near, turned[1], 0.0)]


def plus(low, high):
    return [a + b for a, b in zip(low, high)]


def near_leaves(tiles):
    if len(tiles) == 4:
        wide = [plus(tiles[0], tiles[2]), plus(tiles[1], tiles[3])]
    else:
        wide = tiles
    zero = plus(wide[0], wide[1])
    first = plus(wide[0], stepped(wide[1], 1))
    message = [None, None, first[0], first[1], zero[0], zero[1], None, None]
    if len(tiles) == 4:
        second = [plus(tiles[a], stepped(tiles[2 + a], 1)) for a in range(2)]
        message[0], message[1] = second[0][0], second[1][0]
        message[6], message[7] = second[0][1], second[1][1]
    return message


def far_leaves(tiles):
    parts = [tiles[at:at + 4] for at in range(0, len(tiles), 4)]
    halves = parts if len(parts) == 2 else [[plus(a, b) for a, b in zip(*parts[at:at + 2])] for at in (0, 2)]
    out = {1: [plus(low, stepped(high, 1)) for low, high in zip(*halves)]}
    if len(parts) == 4:
        one, two = [[plus(a, stepped(b, 1)) for a, b in zip(*parts[at:at + 2])] for at in (0, 2)]
        for block in (2, 3):
            out[block] = [plus(low, stepped(high, block - 1)) for low, high in zip(one, two)]
    return {block: [pair[part] for part in range(2) for pair in pairs] for block, pairs in out.items()}


def search_kernel(
    x_hbm, mask_hbm, widths_hbm, out_ref, x_ref, mask_ref, widths_ref, in_sem, send, send_sem, recv, recv_sem,
    ready_sem, first, work, mid, series, prefix,
):
    beams, width, samples = x_ref.shape
    blocks, groups = lax.axis_size("freq"), lax.axis_size("beam")
    devices = blocks * groups
    row_total = float(beams * samples)
    my_block = lax.axis_index("freq")
    my_group = lax.axis_index("beam")
    my_place = my_block * groups + my_group
    quarter = groups // 2

    chunks = in_sem.shape[0] - 2
    span = width // chunks
    loads = [
        pltpu.make_async_copy(
            x_hbm.at[:, pl.ds(c * span, span)], x_ref.at[:, pl.ds(c * span, span)], in_sem.at[c]
        )
        for c in range(chunks)
    ]
    mask_load = pltpu.make_async_copy(mask_hbm, mask_ref, in_sem.at[chunks])
    widths_load = pltpu.make_async_copy(widths_hbm, widths_ref, in_sem.at[chunks + 1])
    loads[0].start()
    mask_load.start()
    for load in loads[1:]:
        load.start()
    widths_load.start()

    def signal(semaphore, place):
        pl.semaphore_signal(
            semaphore, inc=1, device_id={"freq": place // groups, "beam": place % groups},
            device_id_type=pl.DeviceIdType.MESH,
        )

    barrier = pltpu.get_barrier_semaphore()

    @pl.when(my_block == 0)
    def _():
        for step in range(1, devices):
            signal(barrier, (my_place + devices - step) % devices)

    @pl.when(my_block == 1)
    def _():
        for place in range(groups):
            signal(barrier, place)

    lane = lax.broadcasted_iota(jnp.int32, (LANE_ROWS, LANES), 1)
    inner = lax.broadcasted_iota(jnp.int32, (LANE_ROWS, LANES), 0)
    ones = jnp.ones((2 * LANE_ROWS, samples), jnp.bfloat16)
    dims = (((1,), (1,)), ((), ()))
    means, scales = [], []
    for c in range(chunks):
        loads[c].wait()
        if c == 0:
            mask_load.wait()
        rows = slice(c * span, (c + 1) * span)
        dotted = beams // 2
        flat = jnp.concatenate([x_ref[b, rows] for b in range(dotted)], axis=1)
        rest = jnp.concatenate([x_ref[b, rows] for b in range(dotted, beams)], axis=1)
        gram = lax.dot_general(flat, flat, dims, preferred_element_type=jnp.float32)
        total = lax.dot_general(
            jnp.concatenate([ones] * beams, axis=1), jnp.concatenate([flat, rest], axis=1), dims,
            preferred_element_type=jnp.float32,
        )[:1]
        squares = []
        for column in range(span // LANES):
            sums = jnp.zeros((LANE_ROWS, LANES), jnp.float32)
            for tile in range(LANES // LANE_ROWS):
                at = column * LANES + tile * LANE_ROWS
                own = jnp.zeros((LANE_ROWS, samples), jnp.float32)
                for b in range(dotted, beams):
                    wide = x_ref[b, c * span + at:c * span + at + LANE_ROWS].astype(jnp.float32)
                    own = own + wide * wide
                own = jnp.sum(own, axis=1, keepdims=True)
                both = gram[at:at + LANE_ROWS, column * LANES:(column + 1) * LANES] + own
                sums = sums + jnp.where(lane == inner + tile * LANE_ROWS, both, 0.0)
            squares.append(jnp.sum(sums, axis=0, keepdims=True))
        mean = total / row_total
        var = jnp.concatenate(squares, axis=1) / row_total - mean * mean
        place = pl.multiple_of(my_group * width + c * span, span)
        clean = mask_ref[:, pl.ds(place, span)].astype(jnp.float32)
        means.append(mean)
        scales.append(lax.rsqrt(var + epsilon) * clean)
    channel_mean = jnp.concatenate(means, axis=1)
    channel_scale = jnp.concatenate(scales, axis=1)
    coarse = channel_scale.astype(jnp.bfloat16).astype(jnp.float32)
    fine = (channel_scale - coarse).astype(jnp.bfloat16).astype(jnp.float32)
    offset = channel_mean * (coarse + fine)

    def summing(depth):
        chosen = band_mask(depth, width)
        matrix = jnp.concatenate(
            [jnp.where(chosen, coarse, 0.0), jnp.where(chosen, fine, 0.0)], axis=0
        ).astype(jnp.bfloat16)
        shift = jnp.sum(jnp.where(chosen, offset, 0.0), axis=1, keepdims=True)

        def tiles(beam):
            both = jnp.dot(matrix, x_ref[beam], preferred_element_type=jnp.float32)
            sums = both[:chosen.shape[0]] + both[chosen.shape[0]:] - shift
            return [
                [sums[t:t + LANE_ROWS, p * LANES:(p + 1) * LANES] for p in range(2)]
                for t in range(0, chosen.shape[0], LANE_ROWS)
            ]

        return tiles

    def message(block, slot, begin, end):
        return pltpu.make_async_remote_copy(
            src_ref=send.at[block, slot, pl.ds(begin, end - begin)],
            dst_ref=recv.at[my_place, pl.ds(begin, end - begin)],
            send_sem=send_sem.at[block, slot],
            recv_sem=recv_sem.at[my_place],
            device_id={"freq": block, "beam": (my_group + slot) % beams},
            device_id_type=pl.DeviceIdType.MESH,
        )

    def near_messages(action, slot, narrow):
        if narrow:
            action(message(0, slot, *block_span(2)))
            return

        @pl.when(my_block == 1)
        def _():
            action(message(0, slot, *block_span(1)))
        if slot > 0:
            @pl.when(my_block == 0)
            def _():
                action(message(0, slot, *block_span(0)))

    def near_phase(narrow):
        tiles = summing(0 if narrow else 1)
        for slot in range(beams):
            for number, leaf in enumerate(near_leaves(tiles((my_group + slot) % beams))):
                if leaf is not None:
                    send[0, slot, number] = leaf.astype(jnp.bfloat16)
                    if slot == 0 and not narrow:
                        @pl.when(my_block == 0)
                        def _(leaf=leaf, number=number):
                            recv[my_place, number] = leaf.astype(jnp.bfloat16)
            if slot == 0:
                if narrow:
                    pl.semaphore_wait(barrier, groups)
                    for place in range(quarter):
                        signal(ready_sem, place)
                else:
                    pl.semaphore_wait(barrier, jnp.where(my_block == 0, 2 * groups - 1, groups))
            near_messages(lambda copy: copy.start(), slot, narrow)

    def far_messages(action, slot, low):
        action(message(1, slot, 0 if low else 4, 8))
        if low:
            for half in range(2):
                @pl.when((my_group * 2 >= quarter) if half else (my_group * 2 < quarter))
                def _(half=half):
                    for block in (2, 3):
                        action(message(block, slot, 4 * half, 8))

    def far_phase(low):
        tiles = summing(3 if low else 2)
        if low:
            pl.semaphore_wait(ready_sem, 2 * groups)
        for slot in range(beams):
            for block, leaves in far_leaves(tiles((my_group + slot) % beams)).items():
                for number, leaf in enumerate(leaves):
                    send[block, slot, number] = leaf.astype(jnp.bfloat16)
            far_messages(lambda copy: copy.start(), slot, low)

    def arrival(place, begin, end):
        target = recv.at[place, pl.ds(begin, end - begin)]
        pltpu.make_async_remote_copy(
            src_ref=target, dst_ref=target, send_sem=send_sem.at[0, 0], recv_sem=recv_sem.at[place],
            device_id={"freq": my_block, "beam": my_group}, device_id_type=pl.DeviceIdType.MESH,
        ).wait_recv()

    args = (recv, first, work, mid, series)
    pitch = first.shape[1] // LANE_ROWS

    def wide_places(count, numbers_of):
        per = count // LANE_ROWS
        return [
            ((place // per) * pitch + (place % per) * (pitch - LANE_ROWS) // per + address, place, numbers)
            for place in range(count) for address, numbers in numbers_of(place)
        ]

    @pl.when(my_block < 2)
    def _():
        near_phase(False)

    @pl.when(my_block >= 2)
    def _():
        near_phase(True)

    for low in (True, False):
        @pl.when((my_block == 0) & ((my_group < quarter) == low))
        def _(low=low):
            far_phase(low)

    widths_load.wait()

    @pl.when(my_block == 0)
    def _():
        for place in range(groups):
            @pl.when(place != my_group)
            def _(place=place):
                arrival(place, *block_span(0))
        for place in range(groups, 2 * groups):
            arrival(place, *block_span(1))
        unit_rows(*args, 512, 1, 256, 1, wide_places(
            2 * groups,
            lambda place: [(8 * a, (a if place < groups else None, 6 + a)) for a in range(2)],
        ))
        for place in range(2 * groups, 4 * groups):
            arrival(place, *block_span(2))
        unit_rows(*args, 256, 1, 256, 0, wide_places(
            4 * groups, lambda place: [(0, (2 if place < 2 * groups else None, 3))],
        ))
        unit_rows(*args, 0, 0, 256, 0, wide_places(4 * groups, lambda place: [(0, (4, 5))]))
        result = boxcar_rows(widths_ref, series, prefix, 6)
        unpermuted(result[:4], out_ref, 0, 0)
        unpermuted(result[4:], out_ref, 512, 1)

    @pl.when(my_block == 1)
    def _():
        for place in range(groups):
            arrival(place, *late_span(place, quarter))
        unit_rows(*args, 0, 1, 256, 2, wide_places(
            groups,
            lambda place: [
                (8 * (2 * (q % 2) + q // 2), (q if place < quarter else None, 4 + q)) for q in range(4)
            ],
        ))
        unpermuted(boxcar_rows(widths_ref, series, prefix, 2), out_ref, 0, 2)

    for late in (2, 3):
        @pl.when(my_block == late)
        def _(late=late):
            found = []
            for place in range(quarter):
                arrival(place, *late_span(place, quarter // 2))
                for q in range(4):
                    found.append((
                        (2 * (q % 2) + q // 2) * pitch + place * LANE_ROWS, place,
                        (q if 2 * place < quarter else None, 4 + q),
                    ))
            unit_rows(*args, 0, late, 128, 2, found)
            unpermuted(boxcar_rows(widths_ref, series, prefix, 1), out_ref, 0, 3)

    for slot in range(beams):
        for narrow in (True, False):
            @pl.when((my_block >= 2) == narrow)
            def _(narrow=narrow, slot=slot):
                near_messages(lambda copy: copy.wait_send(), slot, narrow)
        for low in (True, False):
            @pl.when((my_block == 0) & ((my_group < quarter) == low))
            def _(low=low, slot=slot):
                far_messages(lambda copy: copy.wait_send(), slot, low)


def search(intensity, channel_mask, box_widths):
    beams, width, samples = intensity.shape
    blocks, groups = lax.axis_size("freq"), lax.axis_size("beam")
    devices = blocks * groups
    return pl.pallas_call(
        search_kernel,
        in_specs=[pl.BlockSpec(memory_space=pl.ANY)] * 3,
        out_specs=pl.BlockSpec(memory_space=pltpu.VMEM),
        scratch_shapes=[
            pltpu.VMEM((beams, width, samples), jnp.bfloat16),
            pltpu.VMEM((1, width * groups), jnp.int32),
            pltpu.SMEM(box_widths.shape, jnp.int32),
            pltpu.SemaphoreType.DMA((4,)),
            pltpu.VMEM((blocks, beams, 8, LANE_ROWS, LANES), jnp.bfloat16),
            pltpu.SemaphoreType.DMA((blocks, beams)),
            pltpu.VMEM((devices, 8, LANE_ROWS, LANES), jnp.bfloat16),
            pltpu.SemaphoreType.DMA((devices,)),
            pltpu.SemaphoreType.REGULAR,
            pltpu.VMEM((2, samples + LANE_ROWS * LANE_ROWS, LANES), jnp.float32),
            pltpu.VMEM((2, samples, LANES), jnp.float32),
            pltpu.VMEM((2, samples, LANES), jnp.float32),
            pltpu.VMEM((3 * samples, 2 * samples), jnp.bfloat16),
            pltpu.VMEM((6, LANE_ROWS + samples + WIDEST, LANES), jnp.float32),
        ],
        out_shape=jax.ShapeDtypeStruct((1, NDM // blocks), jnp.float32),
        compiler_params=pltpu.CompilerParams(collective_id=0, has_side_effects=True),
    )(intensity, channel_mask.reshape(1, -1), box_widths)


def ramped(pair, start, stride, far, only_late=False):
    shape = pair[1].shape
    place = lane_index(shape) + (lax.broadcasted_iota(jnp.int32, shape, 0) * stride + start)
    picks = place & (LANES - 1)
    late = jnp.take_along_axis(pair[1], picks, axis=1, mode="promise_in_bounds")
    if far:
        return [jnp.where(place < 2 * LANES, late, 0.0), None]
    near = place < LANES
    moved = [None, jnp.where(near, late, 0.0)]
    if not only_late:
        early = jnp.take_along_axis(pair[0], picks, axis=1, mode="promise_in_bounds")
        moved[0] = jnp.where(near, early, late)
    return moved


def joined_pair(low, high):
    return [a if b is None else (None if a is None else a + b) for a, b in zip(low, high)]


def unit_rows(recv, first, work, mid, series, base, root, leaves, kinds, found):
    tiles = leaves // LANE_ROWS
    pitch = first.shape[1] // LANE_ROWS
    for address, place, numbers in found:
        for part in range(2):
            if numbers[part] is not None:
                first[part, address:address + LANE_ROWS] = recv[place, numbers[part]].astype(jnp.float32)

    def leaf(tile, part):
        outer, kind = tile >> kinds, tile & ((1 << kinds) - 1)
        if leaves == LANE_ROWS * (pitch - LANE_ROWS):
            spot, step = ((outer >> 3 << kinds) + kind) * LANE_ROWS + (outer & 7), pitch
        else:
            spot, step = kind * pitch + outer, LANE_ROWS // 2
        return first[part, pl.ds(spot, LANE_ROWS, stride=step)]

    chunk = 8
    for c in range(tiles // chunk):
        tree = [[[leaf(c * chunk + k, part) for part in range(2)]] for k in range(chunk)]
        level_root = root
        while len(tree) > 1:
            tree = [
                [
                    plus(low[r // 2], stepped(high[r // 2], level_root + r // 2 + r % 2))
                    for r in range(2 * len(low))
                ]
                for low, high in zip(tree[0::2], tree[1::2])
            ]
            level_root = level_root * 2
        for j in range(chunk):
            for part in range(2):
                at = (j * (tiles // chunk) + c) * LANE_ROWS
                work[part, at:at + LANE_ROWS] = tree[0][j][part]
    chunks = tiles // chunk
    for j in range(chunk):
        tree = []
        for c in range(chunks):
            at = (j * chunks + c) * LANE_ROWS
            tree.append([[work[part, at:at + LANE_ROWS] for part in range(2)]])
        level_root = root * chunk + j
        while len(tree) > 1:
            tree = [
                [
                    plus(low[r // 2], stepped(high[r // 2], level_root + r // 2 + r % 2))
                    for r in range(2 * len(low))
                ]
                for low, high in zip(tree[0::2], tree[1::2])
            ]
            level_root = level_root * 2
        for k in range(chunks):
            for part in range(2):
                at = (j * chunks + k) * LANE_ROWS
                mid[part, at:at + LANE_ROWS] = tree[0][k][part]
    far = root > 0
    for g in range(tiles // LANE_ROWS):
        tree = []
        for s in range(LANE_ROWS):
            pair = [
                None if far and 2 * s >= LANE_ROWS and part == 0
                else mid[part, pl.ds(g * LANE_ROWS * LANE_ROWS + s, LANE_ROWS, stride=LANE_ROWS)]
                for part in range(2)
            ]
            tree.append([pair])
        start, stride = root * tiles + g * LANE_ROWS, 1
        while len(tree) > 1:
            last = len(tree) == 2
            merged = []
            for number in range(len(tree) // 2):
                low, high = tree[2 * number], tree[2 * number + 1]
                rows = []
                for r in range(2 * len(low)):
                    source = r // 2
                    begin = start + source + r % 2
                    missing = high[source][0] is None
                    moved = ramped(high[source], begin, stride, far and last, missing)
                    rows.append(joined_pair(low[source], moved))
                merged.append(rows)
            tree = merged
            start, stride = start * 2, stride * 2
        for k in range(0, LANE_ROWS, 2):
            rows = jnp.concatenate(
                [jnp.concatenate(tree[0][k + half], axis=1) for half in range(2)], axis=0
            )
            coarse = rows.astype(jnp.bfloat16)
            at = base + g * 64 + k * LANE_ROWS
            samples = rows.shape[1]
            series[at:at + 2 * LANE_ROWS, :samples] = coarse
            series[at:at + 2 * LANE_ROWS, samples:] = (rows - coarse.astype(jnp.float32)).astype(jnp.bfloat16)


def boxcar_rows(widths_ref, series, prefix, columns):
    lanes = prefix.shape[2]
    samples = series.shape[1] // 2
    until = lax.broadcasted_iota(jnp.int32, (samples, 2 * samples), 0)
    time = lax.broadcasted_iota(jnp.int32, (samples, 2 * samples), 1) & (samples - 1)
    ladder = jnp.where(time <= until, 1.0, 0.0).astype(jnp.bfloat16)
    margin = prefix.shape[1] - samples - LANE_ROWS
    piece = min(2, columns)
    for part in range(columns // piece):
        sums = lax.dot_general(
            ladder, series[part * piece * lanes:(part + 1) * piece * lanes], (((1,), (1,)), ((), ())),
            preferred_element_type=jnp.float32,
        )
        for side in range(piece):
            column = piece * part + side
            prefix[column, :LANE_ROWS] = jnp.zeros((LANE_ROWS, lanes), jnp.float32)
            prefix[column, LANE_ROWS:LANE_ROWS + samples] = sums[:, side * lanes:(side + 1) * lanes]
            prefix[column, LANE_ROWS + samples:] = jnp.full((margin, lanes), -jnp.inf, jnp.float32)
    result = []
    for column in range(columns):
        best = None
        for number in range(widths_ref.shape[0]):
            width = widths_ref[number]
            sums = (
                prefix[column, pl.ds(LANE_ROWS - 1 + width, samples)]
                - prefix[column, LANE_ROWS - 1:LANE_ROWS - 1 + samples]
            )
            norm = lax.rsqrt(jnp.full((1, lanes), width * CHANS, jnp.int32).astype(jnp.float32))
            peak = jnp.max(sums, axis=0, keepdims=True) * norm
            best = peak if best is None else jnp.maximum(best, peak)
        result.append(jnp.broadcast_to(best, (LANE_ROWS, lanes)))
    return result


def unpermuted(columns, out_ref, offset, repeat_bits):
    lane = lane_index((LANE_ROWS, LANES))
    for number in range(len(columns) << repeat_bits):
        row = (lane + number * LANES) >> repeat_bits
        row = row & (LANES - 1)
        picks = (row & 64) + (row & 7) * LANE_ROWS + ((row >> 3) & 7)
        column = columns[number >> repeat_bits]
        spread = jnp.take_along_axis(column, picks, axis=1, mode="promise_in_bounds")
        at = offset + number * LANES
        out_ref[:, at:at + LANES] = spread[:1]


def shards(intensity, channel_mask, box_widths):
    beams, width, samples = intensity.shape
    blocks, groups = lax.axis_size("freq"), lax.axis_size("beam")
    if compact(samples, blocks * groups, blocks, groups, beams, width):
        return search(intensity, channel_mask, box_widths)
    rows = entry_rows(intensity, channel_mask)
    return trial_peaks(rows, box_widths, lax.axis_index("freq").reshape(1))


def solution(mesh):
    in_specs = (P(None, ("freq", "beam"), None), P("freq"), P())
    out_specs = P("beam", "freq")
    return jax.shard_map(shards, mesh=mesh, in_specs=in_specs, out_specs=out_specs, check_vma=False)
```

```python
import jax
import jax.numpy as jnp
from jax import lax
from jax.experimental import pallas as pl
from jax.experimental.pallas import tpu as pltpu
from jax.sharding import PartitionSpec as P

CHANS = 16384
NDM = 4096
LANE_ROWS = 8
LANES = 128
WIDEST = 64

epsilon = 1e-05


def reverse_bits(number, count):
    result = 0
    for _ in range(count):
        result = result << 1 | number & 1
        number >>= 1
    return result


def lane_index(shape):
    return lax.broadcasted_iota(jnp.int32, shape, len(shape) - 1)


def earlier(block, amount):
    if amount == 0:
        return block
    samples = block.shape[-1]
    return jnp.where(lane_index(block.shape) < samples - amount, pltpu.roll(block, samples - amount, 1), 0.0)


def folds(trial_dev, samples):
    return trial_dev >= 4 * samples


def channel_limits(trial_dev, blocks, samples):
    limits = []
    for block in range(blocks):
        limit, rows = CHANS, NDM
        while (block * trial_dev * rows // NDM + 1) // 2 >= samples:
            limit, rows = limit // 2, rows // 2
        limits.append(limit)
    return limits


def entry_kernel(x_hbm, mask_ref, out_ref, x_ref, in_sem, send, send_sem, recv_sem, own_sem):
    blocks, beams, bands, samples = send.shape
    groups = lax.axis_size("beam")
    beam_dev = beams // groups
    width = x_ref.shape[1]
    group = width // (bands * blocks)
    trial_dev = NDM // blocks
    row_total = float(beams * samples)
    fold = folds(trial_dev, samples)
    limits = channel_limits(trial_dev, blocks, samples)
    my_block = lax.axis_index("freq")
    my_group = lax.axis_index("beam")
    my_place = my_block * groups + my_group
    devices = blocks * groups

    barrier = pltpu.get_barrier_semaphore()
    for step in range(1, devices):
        peer = (my_place + step) % devices
        pl.semaphore_signal(
            barrier, inc=1, device_id={"freq": peer // groups, "beam": peer % groups},
            device_id_type=pl.DeviceIdType.MESH,
        )

    chunks = in_sem.shape[0]
    span = width // chunks
    loads = [
        pltpu.make_async_copy(
            x_hbm.at[:, pl.ds(c * span, span)], x_ref.at[:, pl.ds(c * span, span)], in_sem.at[c]
        )
        for c in range(chunks)
    ]
    for load in loads:
        load.start()
    means, scales = [], []
    for c in range(chunks):
        loads[c].wait()
        total = jnp.zeros((span, samples), jnp.float32)
        squares = jnp.zeros((span, samples), jnp.float32)
        for beam in range(beams):
            wide = x_ref[beam, c * span:(c + 1) * span].astype(jnp.float32)
            total = total + wide
            squares = squares + wide * wide
        mean = jnp.sum(total, axis=1, keepdims=True) / row_total
        var = jnp.sum(squares, axis=1, keepdims=True) / row_total - mean * mean
        means.append(mean)
        scales.append(lax.rsqrt(var + epsilon))
    channel_mean = jnp.concatenate(means, axis=0)
    channel_scale = jnp.concatenate(scales, axis=0)
    out_row = lax.broadcasted_iota(jnp.int32, (blocks * bands, width), 0)
    channel = lax.broadcasted_iota(jnp.int32, (blocks * bands, width), 1)
    band = out_row % bands
    if fold:
        half = bands // 2
        band = (band % half) * 2 + band // half
    wanted = band * blocks + out_row // bands
    clean = mask_ref[:, pl.ds(pl.multiple_of(my_group * width, width), width)].astype(jnp.float32)
    chosen = jnp.where(channel // group == wanted, clean, 0.0).astype(jnp.bfloat16)
    upper = my_block * 2 >= blocks

    def message(block, slot, beam, rows):
        return pltpu.make_async_remote_copy(
            src_ref=send.at[block, slot, pl.ds(0, rows)],
            dst_ref=out_ref.at[beam % beam_dev, my_place, pl.ds(0, rows)],
            send_sem=send_sem.at[block, slot],
            recv_sem=recv_sem.at[beam % beam_dev, my_place],
            device_id={"freq": block, "beam": beam // beam_dev},
            device_id_type=pl.DeviceIdType.MESH,
        )

    def own_copy(slot, part):
        return pltpu.make_async_copy(
            send.at[my_block, slot], out_ref.at[part, my_place], own_sem.at[part]
        )

    def every_message(action, slot):
        beam = (my_group * beam_dev + slot) % beams
        for block in range(blocks):
            goes = my_place * width < limits[block]
            if slot < beam_dev:
                goes = goes & (my_block != block)
            if fold:
                @pl.when(goes & upper)
                def _(block=block):
                    action(message(block, slot, beam, bands // 2))
                goes = goes & jnp.logical_not(upper)

            @pl.when(goes)
            def _(block=block):
                action(message(block, slot, beam, bands))

    for slot in range(beams):
        beam = (my_group * beam_dev + slot) % beams
        wide = x_ref[beam].astype(jnp.float32)
        normed = ((wide - channel_mean) * channel_scale).astype(jnp.bfloat16)
        sums = jnp.dot(chosen, normed, preferred_element_type=jnp.float32)
        tree = [[sums[i * bands:(i + 1) * bands]] for i in range(blocks)]
        while len(tree) > 1:
            merged = []
            for low, high in zip(tree[0::2], tree[1::2]):
                merged.append(
                    [low[m // 2] + earlier(high[m // 2], (m + 1) // 2) for m in range(2 * len(low))]
                )
            tree = merged
        for number, row in enumerate(tree[0]):
            if fold:
                both = row[:half] + row[half:]
                row = jnp.concatenate([jnp.where(upper, both, row[:half]), row[half:]], axis=0)
            send[number, slot] = row.astype(jnp.bfloat16)
        if slot == 0:
            pl.semaphore_wait(barrier, devices - 1)
        every_message(lambda copy: copy.start(), slot)
        if slot < beam_dev:
            own_copy(slot, slot).start()

    for slot in range(beam_dev):
        own_copy(slot, slot).wait()
    limit = sum(jnp.where(my_block == block, limits[block], 0) for block in range(blocks))
    for place in range(devices):
        for part in range(beam_dev):
            rows = bands // 2 if fold and 2 * place >= devices else bands
            target = out_ref.at[part, place, pl.ds(0, rows)]
            @pl.when((place * width < limit) & (place != my_place))
            def _(target=target, place=place, part=part):
                pltpu.make_async_remote_copy(
                    src_ref=target, dst_ref=target, send_sem=send_sem.at[0, 0],
                    recv_sem=recv_sem.at[part, place],
                    device_id={"freq": my_block, "beam": my_group},
                    device_id_type=pl.DeviceIdType.MESH,
                ).wait_recv()
    for slot in range(beams):
        every_message(lambda copy: copy.wait_send(), slot)


def entry_rows(intensity, channel_mask):
    beams, width, samples = intensity.shape
    blocks, groups = lax.axis_size("freq"), lax.axis_size("beam")
    bands = width * NDM // (CHANS * blocks)
    beam_dev, devices = beams // groups, blocks * groups
    return pl.pallas_call(
        entry_kernel,
        in_specs=[pl.BlockSpec(memory_space=pl.ANY), pl.BlockSpec(memory_space=pltpu.VMEM)],
        out_specs=pl.BlockSpec(memory_space=pl.ANY),
        scratch_shapes=[
            pltpu.VMEM((beams, width, samples), jnp.bfloat16),
            pltpu.SemaphoreType.DMA((4,)),
            pltpu.VMEM((blocks, beams, bands, samples), jnp.bfloat16),
            pltpu.SemaphoreType.DMA((blocks, beams)),
            pltpu.SemaphoreType.DMA((beam_dev, devices)),
            pltpu.SemaphoreType.DMA((beam_dev,)),
        ],
        out_shape=jax.ShapeDtypeStruct((beam_dev, devices, bands, samples), jnp.bfloat16),
        compiler_params=pltpu.CompilerParams(collective_id=0, has_side_effects=True),
    )(intensity, channel_mask.reshape(1, -1))


def advanced(pieces, amount):
    lanes = pieces[0].shape[-1]
    position = lane_index(pieces[0].shape)
    turn = (lanes - amount) & (lanes - 1)
    turned = [pltpu.roll(piece, turn, 1) for piece in pieces]
    return joined(turned, lambda limit: position < limit - amount)


def advanced_rows(pieces, amounts):
    lanes = pieces[0].shape[-1]
    position = lane_index(pieces[0].shape) + amounts
    picks = position & (lanes - 1)
    turned = [jnp.take_along_axis(piece, picks, axis=1, mode="promise_in_bounds") for piece in pieces]
    return joined(turned, lambda limit: position < limit)


def joined(turned, below):
    lanes = turned[0].shape[-1]
    near = [below((k + 1) * lanes) for k in range(len(turned))]
    result = []
    for number in range(len(turned)):
        value = jnp.zeros_like(turned[0])
        for ahead in reversed(range(len(turned) - number)):
            value = jnp.where(near[ahead], turned[number + ahead], value)
        result.append(value)
    return result


def trial_kernel(place_ref, widths_ref, x_ref, out_ref, first, even, odd, series, prefix):
    total, samples = out_ref.shape[2], x_ref.shape[3]
    tiles = total // LANE_ROWS
    tile_bits = tiles.bit_length() - 1
    lanes = prefix.shape[2]
    parts = samples // lanes
    pitch = first.shape[1] // LANE_ROWS
    block = place_ref[0]
    bands = x_ref.shape[2]
    fold = folds(total, samples)
    half_bands = bands // 2
    sources = x_ref.shape[1]
    for number in range(sources):
        high, start = divmod(number * bands, tiles)
        start += reverse_bits(high, LANE_ROWS.bit_length() - 1) * pitch
        for part in range(parts):
            cut = slice(part * lanes, (part + 1) * lanes)
            if fold and 2 * number >= sources:
                first[part, start:start + half_bands] = x_ref[0, number, :half_bands, cut].astype(jnp.float32)
                first[part, start + half_bands:start + bands] = jnp.zeros((half_bands, lanes), jnp.float32)
            else:
                first[part, start:start + bands] = x_ref[0, number, :, cut].astype(jnp.float32)
    for tile in range(tiles):
        spot = tile
        if fold:
            band = tile % bands
            spot = tile - band + (band % 2) * half_bands + band // 2
        for part in range(parts):
            even[reverse_bits(tile, tile_bits), :, part * lanes:(part + 1) * lanes] = first[
                part, pl.ds(spot, LANE_ROWS, stride=pitch)
            ]

    source, target = even, odd
    count = 1
    while count < tiles:
        half = tiles // count // 2

        def merge(j, source=source, target=target, count=count, half=half):
            flat = (half * LANE_ROWS, lanes)
            cut = [slice(part * lanes, (part + 1) * lanes) for part in range(parts)]
            low = [source[pl.ds(j * 2 * half, half), :, c].reshape(flat) for c in cut]
            high = [source[pl.ds(j * 2 * half + half, half), :, c].reshape(flat) for c in cut]
            for side in range(2):
                moved = advanced(high, block * count + j + side)
                for c, base, extra in zip(cut, low, moved):
                    target[pl.ds((2 * j + side) * half, half), :, c] = (base + extra).reshape(
                        half, LANE_ROWS, lanes
                    )

        if count <= 16:
            for j in range(count):
                merge(j)
        else:
            def step(i, carry, merge=merge):
                for k in range(32):
                    merge(i * 32 + k)
                return carry
            lax.fori_loop(0, count // 32, step, 0)
        source, target = target, source
        count = count * 2

    spot = lax.broadcasted_iota(jnp.int32, (LANE_ROWS, lanes), 0)
    bits = [spot >> 2 & 1, spot >> 1 & 1, spot & 1]
    clear = [bit == 0 for bit in bits]

    def final_rows(j):
        pieces = [source[j, :, part * lanes:(part + 1) * lanes] for part in range(parts)]
        row = spot * 0 + (block * tiles + j)
        for level, reach in enumerate((4, 2, 1)):
            low, high = [], []
            for piece in pieces:
                down = pltpu.roll(piece, reach, 0)
                up = down if 2 * reach == LANE_ROWS else pltpu.roll(piece, LANE_ROWS - reach, 0)
                low.append(jnp.where(clear[level], piece, down))
                high.append(jnp.where(clear[level], up, piece))
            moved = advanced_rows(high, row + bits[level])
            pieces = [base + extra for base, extra in zip(low, moved)]
            row = 2 * row + bits[level]
        return jnp.concatenate(pieces, axis=1)

    def finish(i, carry):
        for k in range(16):
            pair = i * 16 + k
            rows = jnp.concatenate([final_rows(2 * pair), final_rows(2 * pair + 1)], axis=0)
            coarse = rows.astype(jnp.bfloat16)
            place = pl.ds(pl.multiple_of(pair * 16, 16), 16)
            series[place, :samples] = coarse
            series[place, samples:] = (rows - coarse.astype(jnp.float32)).astype(jnp.bfloat16)
        return carry

    lax.fori_loop(0, tiles // 32, finish, 0)

    until = lax.broadcasted_iota(jnp.int32, (samples, 2 * samples), 0)
    time = lax.broadcasted_iota(jnp.int32, (samples, 2 * samples), 1) & (samples - 1)
    ladder = jnp.where(time <= until, 1.0, 0.0).astype(jnp.bfloat16)
    margin = prefix.shape[1] - samples - LANE_ROWS
    piece = 2 * lanes
    for part in range(total // piece):
        sums = lax.dot_general(
            ladder, series[part * piece:(part + 1) * piece], (((1,), (1,)), ((), ())),
            preferred_element_type=jnp.float32,
        )
        for side in range(2):
            column = 2 * part + side
            prefix[column, :LANE_ROWS] = jnp.zeros((LANE_ROWS, lanes), jnp.float32)
            prefix[column, LANE_ROWS:LANE_ROWS + samples] = sums[:, side * lanes:(side + 1) * lanes]
            prefix[column, LANE_ROWS + samples:] = jnp.full((margin, lanes), -jnp.inf, jnp.float32)
    for column in range(total // lanes):
        best = None
        for number in range(widths_ref.shape[0]):
            width = widths_ref[number]
            sums = (
                prefix[column, pl.ds(LANE_ROWS - 1 + width, samples)]
                - prefix[column, LANE_ROWS - 1:LANE_ROWS - 1 + samples]
            )
            norm = lax.rsqrt(jnp.full((1, lanes), width * CHANS, jnp.int32).astype(jnp.float32))
            peak = jnp.max(sums, axis=0, keepdims=True) * norm
            best = peak if best is None else jnp.maximum(best, peak)
        out_ref[0, :, column * lanes:(column + 1) * lanes] = best


def trial_peaks(rows, box_widths, place):
    beams, devices, bands, samples = rows.shape
    total = devices * bands
    tiles = total // LANE_ROWS
    return pl.pallas_call(
        trial_kernel,
        grid_spec=pltpu.PrefetchScalarGridSpec(
            num_scalar_prefetch=2,
            grid=(beams,),
            in_specs=[pl.BlockSpec((1, devices, bands, samples), lambda b, p, w: (b, 0, 0, 0))],
            out_specs=pl.BlockSpec((1, 1, total), lambda b, p, w: (b, 0, 0)),
            scratch_shapes=[
                pltpu.VMEM((samples // LANES, total + LANE_ROWS * LANE_ROWS, LANES), jnp.float32),
                pltpu.VMEM((tiles, LANE_ROWS, samples), jnp.float32),
                pltpu.VMEM((tiles, LANE_ROWS, samples), jnp.float32),
                pltpu.VMEM((total, 2 * samples), jnp.bfloat16),
                pltpu.VMEM((total // LANES, LANE_ROWS + samples + WIDEST, LANES), jnp.float32),
            ],
        ),
        out_shape=jax.ShapeDtypeStruct((beams, 1, total), jnp.float32),
    )(place, box_widths, rows)[:, 0]


def compact(samples, devices, blocks, groups, beams, width):
    return (
        samples == 2 * LANES and NDM == 16 * samples and blocks == 4 and beams == groups
        and devices * LANE_ROWS == samples and width * devices == CHANS
    )


def block_span(block):
    return ((0, 8), (2, 8), (3, 6), (3, 6))[block]


def late_span(place, whole):
    return (0, 8) if place < whole else (4, 8)


def band_mask(depth, width):
    rows = LANE_ROWS * (2 << depth)
    row = lax.broadcasted_iota(jnp.int32, (rows, width), 0)
    channel = lax.broadcasted_iota(jnp.int32, (rows, width), 1)
    inner, tile = row % LANE_ROWS, row // LANE_ROWS
    if depth == 0:
        wanted = inner * 2 + tile
    else:
        quarter = tile % 4
        band = inner * 4 + (quarter % 2) * 2 + quarter // 2
        wanted = band * (rows // (4 * LANE_ROWS)) + tile // 4
    return channel // (width // rows) == wanted


def stepped(pair, amount):
    if amount == 0:
        return list(pair)
    lane = lane_index(pair[1].shape)
    near = lane < LANES - amount
    turned = [None if piece is None else pltpu.roll(piece, LANES - amount, 1) for piece in pair]
    early = None if turned[0] is None else jnp.where(near, turned[0], turned[1])
    return [early, jnp.where(near, turned[1], 0.0)]


def plus(low, high):
    return [a + b for a, b in zip(low, high)]


def near_leaves(tiles):
    if len(tiles) == 4:
        wide = [plus(tiles[0], tiles[2]), plus(tiles[1], tiles[3])]
    else:
        wide = tiles
    zero = plus(wide[0], wide[1])
    first = plus(wide[0], stepped(wide[1], 1))
    message = [None, None, first[0], first[1], zero[0], zero[1], None, None]
    if len(tiles) == 4:
        second = [plus(tiles[a], stepped(tiles[2 + a], 1)) for a in range(2)]
        message[0], message[1] = second[0][0], second[1][0]
        message[6], message[7] = second[0][1], second[1][1]
    return message


def far_leaves(tiles):
    parts = [tiles[at:at + 4] for at in range(0, len(tiles), 4)]
    halves = parts if len(parts) == 2 else [[plus(a, b) for a, b in zip(*parts[at:at + 2])] for at in (0, 2)]
    out = {1: [plus(low, stepped(high, 1)) for low, high in zip(*halves)]}
    if len(parts) == 4:
        one, two = [[plus(a, stepped(b, 1)) for a, b in zip(*parts[at:at + 2])] for at in (0, 2)]
        for block in (2, 3):
            out[block] = [plus(low, stepped(high, block - 1)) for low, high in zip(one, two)]
    return {block: [pair[part] for part in range(2) for pair in pairs] for block, pairs in out.items()}


def search_kernel(
    x_hbm, mask_hbm, widths_hbm, out_ref, x_ref, mask_ref, widths_ref, in_sem, send, send_sem, recv, recv_sem,
    ready_sem, first, work, mid, planes, lower, series, prefix,
):
    beams, width, samples = x_ref.shape
    blocks, groups = lax.axis_size("freq"), lax.axis_size("beam")
    devices = blocks * groups
    row_total = float(beams * samples)
    my_block = lax.axis_index("freq")
    my_group = lax.axis_index("beam")
    my_place = my_block * groups + my_group
    quarter = groups // 2

    chunks = in_sem.shape[0] - 2
    span = width // chunks
    loads = [
        pltpu.make_async_copy(
            x_hbm.at[:, pl.ds(c * span, span)], x_ref.at[:, pl.ds(c * span, span)], in_sem.at[c]
        )
        for c in range(chunks)
    ]
    mask_load = pltpu.make_async_copy(mask_hbm, mask_ref, in_sem.at[chunks])
    widths_load = pltpu.make_async_copy(widths_hbm, widths_ref, in_sem.at[chunks + 1])
    loads[0].start()
    mask_load.start()
    for load in loads[1:]:
        load.start()
    widths_load.start()

    def signal(semaphore, place):
        pl.semaphore_signal(
            semaphore, inc=1, device_id={"freq": place // groups, "beam": place % groups},
            device_id_type=pl.DeviceIdType.MESH,
        )

    barrier = pltpu.get_barrier_semaphore()

    @pl.when(my_block == 0)
    def _():
        for step in range(1, devices):
            signal(barrier, (my_place + devices - step) % devices)

    @pl.when(my_block == 1)
    def _():
        for place in range(groups):
            signal(barrier, place)

    @pl.when(my_block >= 2)
    def _():
        pl.semaphore_wait(barrier, groups)
        for place in range(quarter):
            signal(ready_sem, place)

    for column in range(prefix.shape[0]):
        prefix[column, :LANE_ROWS] = jnp.zeros((LANE_ROWS, LANES), jnp.float32)
        prefix[column, LANE_ROWS + samples:] = jnp.full((WIDEST, LANES), -jnp.inf, jnp.float32)

    lane = lax.broadcasted_iota(jnp.int32, (LANE_ROWS, LANES), 1)
    inner = lax.broadcasted_iota(jnp.int32, (LANE_ROWS, LANES), 0)
    ones = jnp.ones((2 * LANE_ROWS, samples), jnp.bfloat16)
    dims = (((1,), (1,)), ((), ()))
    means, scales = [], []
    for c in range(chunks):
        loads[c].wait()
        if c == 0:
            mask_load.wait()
        rows = slice(c * span, (c + 1) * span)
        dotted = beams // 2
        flat = jnp.concatenate([x_ref[b, rows] for b in range(dotted)], axis=1)
        rest = jnp.concatenate([x_ref[b, rows] for b in range(dotted, beams)], axis=1)
        gram = lax.dot_general(flat, flat, dims, preferred_element_type=jnp.float32)
        total = lax.dot_general(
            jnp.concatenate([ones] * beams, axis=1), jnp.concatenate([flat, rest], axis=1), dims,
            preferred_element_type=jnp.float32,
        )[:1]
        squares = []
        for column in range(span // LANES):
            sums = jnp.zeros((LANE_ROWS, LANES), jnp.float32)
            for tile in range(LANES // LANE_ROWS):
                at = column * LANES + tile * LANE_ROWS
                own = jnp.zeros((LANE_ROWS, samples), jnp.float32)
                for b in range(dotted, beams):
                    wide = x_ref[b, c * span + at:c * span + at + LANE_ROWS].astype(jnp.float32)
                    own = own + wide * wide
                own = jnp.sum(own, axis=1, keepdims=True)
                both = gram[at:at + LANE_ROWS, column * LANES:(column + 1) * LANES] + own
                sums = sums + jnp.where(lane == inner + tile * LANE_ROWS, both, 0.0)
            squares.append(jnp.sum(sums, axis=0, keepdims=True))
        mean = total / row_total
        var = jnp.concatenate(squares, axis=1) / row_total - mean * mean
        place = pl.multiple_of(my_group * width + c * span, span)
        clean = mask_ref[:, pl.ds(place, span)].astype(jnp.float32)
        means.append(mean)
        scales.append(lax.rsqrt(var + epsilon) * clean)
    channel_mean = jnp.concatenate(means, axis=1)
    channel_scale = jnp.concatenate(scales, axis=1)
    coarse = channel_scale.astype(jnp.bfloat16).astype(jnp.float32)
    fine = (channel_scale - coarse).astype(jnp.bfloat16).astype(jnp.float32)
    offset = channel_mean * (coarse + fine)

    def summing(depth):
        chosen = band_mask(depth, width)
        matrix = jnp.concatenate(
            [jnp.where(chosen, coarse, 0.0), jnp.where(chosen, fine, 0.0)], axis=1
        ).astype(jnp.bfloat16)
        shift = jnp.sum(jnp.where(chosen, offset, 0.0), axis=1, keepdims=True)

        def tiles(slot):
            rows = x_ref[(my_group + slot) % beams]
            sums = jnp.dot(
                matrix, jnp.concatenate([rows, rows], axis=0), preferred_element_type=jnp.float32
            ) - shift
            return [
                [sums[t:t + LANE_ROWS, p * LANES:(p + 1) * LANES] for p in range(2)]
                for t in range(0, chosen.shape[0], LANE_ROWS)
            ]

        return tiles

    def message(block, slot, begin, end):
        return pltpu.make_async_remote_copy(
            src_ref=send.at[block, slot, pl.ds(begin, end - begin)],
            dst_ref=recv.at[my_place, pl.ds(begin, end - begin)],
            send_sem=send_sem.at[block, slot],
            recv_sem=recv_sem.at[my_place],
            device_id={"freq": block, "beam": (my_group + slot) % beams},
            device_id_type=pl.DeviceIdType.MESH,
        )

    def near_messages(action, slot, narrow):
        if narrow:
            action(message(0, slot, *block_span(2)))
            return

        @pl.when(my_block == 1)
        def _():
            action(message(0, slot, *block_span(1)))
        if slot > 0:
            @pl.when(my_block == 0)
            def _():
                action(message(0, slot, *block_span(0)))

    def near_phase(narrow):
        tiles = summing(0 if narrow else 1)
        batch = 4
        for begin in range(0, beams, batch):
            slots = range(begin, begin + batch)
            for slot, summed in [(slot, tiles(slot)) for slot in slots]:
                for number, leaf in enumerate(near_leaves(summed)):
                    if leaf is not None:
                        send[0, slot, number] = leaf.astype(jnp.bfloat16)
                if slot == 0 and not narrow:
                    @pl.when(my_block == 0)
                    def _():
                        recv[my_place] = send[0, 0]
            if begin == 0 and not narrow:
                pl.semaphore_wait(barrier, jnp.where(my_block == 0, 2 * groups - 1, groups))
            for slot in slots:
                near_messages(lambda copy: copy.start(), slot, narrow)

    def far_messages(action, slot, low):
        action(message(1, slot, 0 if low else 4, 8))
        if low:
            for half in range(2):
                @pl.when((my_group * 2 >= quarter) if half else (my_group * 2 < quarter))
                def _(half=half):
                    for block in (2, 3):
                        action(message(block, slot, 4 * half, 8))

    def far_phase(low):
        tiles = summing(3 if low else 2)
        batch = 2
        for begin in range(0, beams, batch):
            slots = range(begin, begin + batch)
            for slot, summed in [(slot, tiles(slot)) for slot in slots]:
                for block, leaves in far_leaves(summed).items():
                    for number, leaf in enumerate(leaves):
                        send[block, slot, number] = leaf.astype(jnp.bfloat16)
            if low and begin < 2:
                continue
            if low and begin == 2:
                pl.semaphore_wait(ready_sem, 2 * groups)
                slots = range(begin + batch)
            for slot in slots:
                far_messages(lambda copy: copy.start(), slot, low)

    def arrival(place, begin, end):
        target = recv.at[place, pl.ds(begin, end - begin)]
        pltpu.make_async_remote_copy(
            src_ref=target, dst_ref=target, send_sem=send_sem.at[0, 0], recv_sem=recv_sem.at[place],
            device_id={"freq": my_block, "beam": my_group}, device_id_type=pl.DeviceIdType.MESH,
        ).wait_recv()

    args = (recv, first, work, mid, series)
    pitch = first.shape[1] // LANE_ROWS

    def wide_places(count, numbers_of):
        per = count // LANE_ROWS
        return [
            ((place // per) * pitch + (place % per) * (pitch - LANE_ROWS) // per + address, place, numbers)
            for place in range(count) for address, numbers in numbers_of(place)
        ]

    @pl.when(my_block < 2)
    def _():
        near_phase(False)

    @pl.when(my_block >= 2)
    def _():
        near_phase(True)

    for low in (True, False):
        @pl.when((my_block == 0) & ((my_group < quarter) == low))
        def _(low=low):
            far_phase(low)

    widths_load.wait()

    @pl.when(my_block == 0)
    def _():
        for place in range(groups):
            @pl.when(place != my_group)
            def _(place=place):
                arrival(place, *block_span(0))
        for place in range(groups, 2 * groups):
            arrival(place, *block_span(1))
        unit_rows(*args, 0, 1, 256, 1, wide_places(
            2 * groups,
            lambda place: [(8 * a, (a if place < groups else None, 6 + a)) for a in range(2)],
        ))
        for plane in range(2):
            for root in range(2):
                numbers = (4 - 2 * root, 5 - 2 * root)
                plane_rows(recv, first, mid, planes.at[root], plane, groups, root, numbers)
        for root in range(2):
            lower_rows(planes.at[root], lower.at[root], root)
        unpermuted(boxcar_rows(widths_ref, series, prefix, 0, 2), out_ref, 512, 1)
        for plane in range(2, blocks):
            for place in range(plane * groups, (plane + 1) * groups):
                arrival(place, *block_span(2))
            for root in range(2):
                numbers = (4, 5) if root == 0 else (None, 3)
                plane_rows(recv, first, mid, planes.at[root], plane, groups, root, numbers)
        for root in range(2):
            upper_rows(planes.at[root], lower.at[root], series, 256 * (1 + root), root)
        result = boxcar_rows(widths_ref, series, prefix, 2, 4)
        unfolded(result[:2], out_ref, 0)
        unfolded(result[2:], out_ref, 256)

    @pl.when(my_block == 1)
    def _():
        for place in range(groups):
            arrival(place, *late_span(place, quarter))
        unit_rows(*args, 0, 1, 256, 2, wide_places(
            groups,
            lambda place: [
                (8 * (2 * (q % 2) + q // 2), (q if place < quarter else None, 4 + q)) for q in range(4)
            ],
        ))
        unpermuted(boxcar_rows(widths_ref, series, prefix, 0, 2), out_ref, 0, 2)

    for late in (2, 3):
        @pl.when(my_block == late)
        def _(late=late):
            found = []
            for place in range(quarter):
                arrival(place, *late_span(place, quarter // 2))
                for q in range(4):
                    found.append((
                        (2 * (q % 2) + q // 2) * pitch + place * LANE_ROWS, place,
                        (q if 2 * place < quarter else None, 4 + q),
                    ))
            unit_rows(*args, 0, late, 128, 2, found)
            unpermuted(boxcar_rows(widths_ref, series, prefix, 0, 1), out_ref, 0, 3)

    for slot in range(beams):
        for narrow in (True, False):
            @pl.when((my_block >= 2) == narrow)
            def _(narrow=narrow, slot=slot):
                near_messages(lambda copy: copy.wait_send(), slot, narrow)
        for low in (True, False):
            @pl.when((my_block == 0) & ((my_group < quarter) == low))
            def _(low=low, slot=slot):
                far_messages(lambda copy: copy.wait_send(), slot, low)


def search(intensity, channel_mask, box_widths):
    beams, width, samples = intensity.shape
    blocks, groups = lax.axis_size("freq"), lax.axis_size("beam")
    devices = blocks * groups
    return pl.pallas_call(
        search_kernel,
        in_specs=[pl.BlockSpec(memory_space=pl.ANY)] * 3,
        out_specs=pl.BlockSpec(memory_space=pltpu.VMEM),
        scratch_shapes=[
            pltpu.VMEM((beams, width, samples), jnp.bfloat16),
            pltpu.VMEM((1, width * groups), jnp.int32),
            pltpu.SMEM(box_widths.shape, jnp.int32),
            pltpu.SemaphoreType.DMA((6,)),
            pltpu.VMEM((blocks, beams, 8, LANE_ROWS, LANES), jnp.bfloat16),
            pltpu.SemaphoreType.DMA((blocks, beams)),
            pltpu.VMEM((devices, 8, LANE_ROWS, LANES), jnp.bfloat16),
            pltpu.SemaphoreType.DMA((devices,)),
            pltpu.SemaphoreType.REGULAR,
            pltpu.VMEM((2, samples + LANE_ROWS * LANE_ROWS, LANES), jnp.float32),
            pltpu.VMEM((2, samples, LANES), jnp.float32),
            pltpu.VMEM((2, samples, LANES), jnp.float32),
            pltpu.VMEM((2, blocks, 2, LANE_ROWS * LANE_ROWS, LANES), jnp.float32),
            pltpu.VMEM((2, 2, LANES, LANES), jnp.float32),
            pltpu.VMEM((3 * samples, 2 * samples), jnp.bfloat16),
            pltpu.VMEM((6, LANE_ROWS + samples + WIDEST, LANES), jnp.float32),
        ],
        out_shape=jax.ShapeDtypeStruct((1, NDM // blocks), jnp.float32),
        compiler_params=pltpu.CompilerParams(collective_id=0, has_side_effects=True),
    )(intensity, channel_mask.reshape(1, -1), box_widths)


def ramped(pair, start, stride, far, only_late=False):
    shape = pair[1].shape
    place = lane_index(shape) + (lax.broadcasted_iota(jnp.int32, shape, 0) * stride + start)
    picks = place & (LANES - 1)
    late = jnp.take_along_axis(pair[1], picks, axis=1, mode="promise_in_bounds")
    if far:
        return [jnp.where(place < 2 * LANES, late, 0.0), None]
    near = place < LANES
    moved = [None, jnp.where(near, late, 0.0)]
    if not only_late:
        early = jnp.take_along_axis(pair[0], picks, axis=1, mode="promise_in_bounds")
        moved[0] = jnp.where(near, early, late)
    return moved


def joined_pair(low, high):
    return [a if b is None else (None if a is None else a + b) for a, b in zip(low, high)]


def unit_rows(recv, first, work, mid, series, base, root, leaves, kinds, found):
    tiles = leaves // LANE_ROWS
    pitch = first.shape[1] // LANE_ROWS
    for address, place, numbers in found:
        for part in range(2):
            if numbers[part] is not None:
                first[part, address:address + LANE_ROWS] = recv[place, numbers[part]].astype(jnp.float32)

    def leaf(tile, part):
        outer, kind = tile >> kinds, tile & ((1 << kinds) - 1)
        if leaves == LANE_ROWS * (pitch - LANE_ROWS):
            spot, step = ((outer >> 3 << kinds) + kind) * LANE_ROWS + (outer & 7), pitch
        else:
            spot, step = kind * pitch + outer, LANE_ROWS // 2
        return first[part, pl.ds(spot, LANE_ROWS, stride=step)]

    chunk = 8
    for c in range(tiles // chunk):
        tree = [[[leaf(c * chunk + k, part) for part in range(2)]] for k in range(chunk)]
        level_root = root
        while len(tree) > 1:
            tree = [
                [
                    plus(low[r // 2], stepped(high[r // 2], level_root + r // 2 + r % 2))
                    for r in range(2 * len(low))
                ]
                for low, high in zip(tree[0::2], tree[1::2])
            ]
            level_root = level_root * 2
        for j in range(chunk):
            for part in range(2):
                at = (j * (tiles // chunk) + c) * LANE_ROWS
                work[part, at:at + LANE_ROWS] = tree[0][j][part]
    chunks = tiles // chunk
    for j in range(chunk):
        tree = []
        for c in range(chunks):
            at = (j * chunks + c) * LANE_ROWS
            tree.append([[work[part, at:at + LANE_ROWS] for part in range(2)]])
        level_root = root * chunk + j
        while len(tree) > 1:
            tree = [
                [
                    plus(low[r // 2], stepped(high[r // 2], level_root + r // 2 + r % 2))
                    for r in range(2 * len(low))
                ]
                for low, high in zip(tree[0::2], tree[1::2])
            ]
            level_root = level_root * 2
        for k in range(chunks):
            for part in range(2):
                at = (j * chunks + k) * LANE_ROWS
                mid[part, at:at + LANE_ROWS] = tree[0][k][part]
    far = root > 0
    for g in range(tiles // LANE_ROWS):
        tree = []
        for s in range(LANE_ROWS):
            pair = [
                None if far and 2 * s >= LANE_ROWS and part == 0
                else mid[part, pl.ds(g * LANE_ROWS * LANE_ROWS + s, LANE_ROWS, stride=LANE_ROWS)]
                for part in range(2)
            ]
            tree.append([pair])
        rows = merged_rows(tree, root * tiles + g * LANE_ROWS, 1, far)
        for k in range(0, LANE_ROWS, 2):
            save_series(series, base + g * LANE_ROWS * LANE_ROWS + k * LANE_ROWS, rows[k:k + 2])


def merged_rows(tree, start, stride, far):
    while len(tree) > 1:
        tree = [
            [
                joined_pair(
                    low[r // 2],
                    ramped(
                        high[r // 2], start + r // 2 + r % 2, stride, far and len(tree) == 2,
                        high[r // 2][0] is None,
                    ),
                )
                for r in range(2 * len(low))
            ]
            for low, high in zip(tree[0::2], tree[1::2])
        ]
        start, stride = start * 2, stride * 2
    return tree[0]


def plane_rows(recv, first, mid, target, plane, groups, root, numbers):
    parts = [part for part in range(2) if numbers[part] is not None]
    for place in range(groups):
        for part in parts:
            at = place * LANE_ROWS
            first[part, at:at + LANE_ROWS] = recv[plane * groups + place, numbers[part]].astype(jnp.float32)
    tree = [
        [[first[part, pl.ds(j, LANE_ROWS, stride=LANE_ROWS)] if part in parts else None for part in range(2)]]
        for j in range(LANE_ROWS)
    ]
    level_root = root
    while len(tree) > 1:
        tree = [
            [
                joined_pair(low[r // 2], stepped(high[r // 2], level_root + r // 2 + r % 2))
                for r in range(2 * len(low))
            ]
            for low, high in zip(tree[0::2], tree[1::2])
        ]
        level_root = level_root * 2
    for j, pair in enumerate(tree[0]):
        for part in parts:
            mid[part, j * LANE_ROWS:(j + 1) * LANE_ROWS] = pair[part]
    tree = [
        [[mid[part, pl.ds(p, LANE_ROWS, stride=LANE_ROWS)] if part in parts else None for part in range(2)]]
        for p in range(LANE_ROWS)
    ]
    for k, pair in enumerate(merged_rows(tree, root * LANE_ROWS, 1, False)):
        for part in parts:
            target[plane, part, k * LANE_ROWS:(k + 1) * LANE_ROWS] = pair[part]


def plane_tile(target, plane, k, parts):
    return [
        target[plane, part, k * LANE_ROWS:(k + 1) * LANE_ROWS] if part in parts else None for part in range(2)
    ]


def lower_rows(target, lower, root):
    for k in range(LANE_ROWS):
        tree = [[plane_tile(target, plane, k, (0, 1))] for plane in range(2)]
        for q, pair in enumerate(merged_rows(tree, root * LANE_ROWS * LANE_ROWS + k, LANE_ROWS, False)):
            for part in range(2):
                at = (2 * k + q) * LANE_ROWS
                lower[part, at:at + LANE_ROWS] = pair[part]


def upper_rows(target, lower, series, base, root):
    parts = (0, 1) if root == 0 else (1,)
    for k in range(LANE_ROWS):
        begin = root * LANE_ROWS * LANE_ROWS + k
        high = merged_rows([[plane_tile(target, plane, k, parts)] for plane in (2, 3)], begin, LANE_ROWS, False)
        low = []
        for q in range(2):
            at = (2 * k + q) * LANE_ROWS
            low.append([lower[part, at:at + LANE_ROWS] for part in range(2)])
        rows = merged_rows([low, high], begin * 2, 2 * LANE_ROWS, root > 0)
        for number in range(0, 4, 2):
            save_series(series, base + (4 * k + number) * LANE_ROWS, rows[number:number + 2])


def save_series(series, at, pairs):
    rows = jnp.concatenate([jnp.concatenate(pair, axis=1) for pair in pairs], axis=0)
    coarse = rows.astype(jnp.bfloat16)
    samples = rows.shape[1]
    series[at:at + 2 * LANE_ROWS, :samples] = coarse
    series[at:at + 2 * LANE_ROWS, samples:] = (rows - coarse.astype(jnp.float32)).astype(jnp.bfloat16)


def unfolded(columns, out_ref, offset):
    lane = lane_index((LANE_ROWS, LANES))
    for number in range(2):
        picks = (lane & 15) * LANE_ROWS + (lane >> 5) + 4 * number
        spread = [jnp.take_along_axis(column, picks, axis=1, mode="promise_in_bounds") for column in columns]
        at = offset + number * LANES
        out_ref[:, at:at + LANES] = jnp.where(lane & 16 == 0, spread[0], spread[1])[:1]


def boxcar_rows(widths_ref, series, prefix, begin, count):
    lanes = prefix.shape[2]
    samples = series.shape[1] // 2
    until = lax.broadcasted_iota(jnp.int32, (samples, 2 * samples), 0)
    time = lax.broadcasted_iota(jnp.int32, (samples, 2 * samples), 1) & (samples - 1)
    ladder = jnp.where(time <= until, 1.0, 0.0).astype(jnp.bfloat16)
    piece = min(2, count)
    for start in range(begin, begin + count, piece):
        sums = lax.dot_general(
            ladder, series[start * lanes:(start + piece) * lanes], (((1,), (1,)), ((), ())),
            preferred_element_type=jnp.float32,
        )
        for side in range(piece):
            prefix[start + side, LANE_ROWS:LANE_ROWS + samples] = sums[:, side * lanes:(side + 1) * lanes]
    widths = [widths_ref[number] for number in range(widths_ref.shape[0])]
    norms = [
        lax.rsqrt(jnp.full((LANE_ROWS, lanes), width * CHANS, jnp.int32).astype(jnp.float32)) for width in widths
    ]
    result = []
    for column in range(begin, begin + count):
        ahead = [prefix[column, pl.ds(LANE_ROWS - 1 + width, samples)] for width in widths]
        base = prefix[column, LANE_ROWS - 1:LANE_ROWS - 1 + samples]
        best = [None] * len(widths)
        for at in range(0, samples, LANE_ROWS):
            before = base[at:at + LANE_ROWS]
            for number, after in enumerate(ahead):
                gain = after[at:at + LANE_ROWS] - before
                best[number] = gain if at == 0 else jnp.maximum(best[number], gain)
        peak = best[0] * norms[0]
        for value, norm in zip(best[1:], norms[1:]):
            peak = jnp.maximum(peak, value * norm)
        result.append(jnp.broadcast_to(jnp.max(peak, axis=0, keepdims=True), (LANE_ROWS, lanes)))
    return result


def unpermuted(columns, out_ref, offset, repeat_bits):
    lane = lane_index((LANE_ROWS, LANES))
    for number in range(len(columns) << repeat_bits):
        row = (lane + number * LANES) >> repeat_bits
        row = row & (LANES - 1)
        picks = (row & 64) + (row & 7) * LANE_ROWS + ((row >> 3) & 7)
        column = columns[number >> repeat_bits]
        spread = jnp.take_along_axis(column, picks, axis=1, mode="promise_in_bounds")
        at = offset + number * LANES
        out_ref[:, at:at + LANES] = spread[:1]


def shards(intensity, channel_mask, box_widths):
    beams, width, samples = intensity.shape
    blocks, groups = lax.axis_size("freq"), lax.axis_size("beam")
    if compact(samples, blocks * groups, blocks, groups, beams, width):
        return search(intensity, channel_mask, box_widths)
    rows = entry_rows(intensity, channel_mask)
    return trial_peaks(rows, box_widths, lax.axis_index("freq").reshape(1))


def solution(mesh):
    in_specs = (P(None, ("freq", "beam"), None), P("freq"), P())
    out_specs = P("beam", "freq")
    return jax.shard_map(shards, mesh=mesh, in_specs=in_specs, out_specs=out_specs, check_vma=False)
```

```python
import jax
import jax.numpy as jnp
from jax import lax
from jax.experimental import pallas as pl
from jax.experimental.pallas import tpu as pltpu
from jax.sharding import PartitionSpec as P

CHANS = 16384
NDM = 4096
LANE_ROWS = 8
LANES = 128
WIDEST = 64

epsilon = 1e-05


def reverse_bits(number, count):
    result = 0
    for _ in range(count):
        result = result << 1 | number & 1
        number >>= 1
    return result


def lane_index(shape):
    return lax.broadcasted_iota(jnp.int32, shape, len(shape) - 1)


def earlier(block, amount):
    if amount == 0:
        return block
    samples = block.shape[-1]
    return jnp.where(lane_index(block.shape) < samples - amount, pltpu.roll(block, samples - amount, 1), 0.0)


def folds(trial_dev, samples):
    return trial_dev >= 4 * samples


def channel_limits(trial_dev, blocks, samples):
    limits = []
    for block in range(blocks):
        limit, rows = CHANS, NDM
        while (block * trial_dev * rows // NDM + 1) // 2 >= samples:
            limit, rows = limit // 2, rows // 2
        limits.append(limit)
    return limits


def entry_kernel(x_hbm, mask_ref, out_ref, x_ref, in_sem, send, send_sem, recv_sem, own_sem):
    blocks, beams, bands, samples = send.shape
    groups = lax.axis_size("beam")
    beam_dev = beams // groups
    width = x_ref.shape[1]
    group = width // (bands * blocks)
    trial_dev = NDM // blocks
    row_total = float(beams * samples)
    fold = folds(trial_dev, samples)
    limits = channel_limits(trial_dev, blocks, samples)
    my_block = lax.axis_index("freq")
    my_group = lax.axis_index("beam")
    my_place = my_block * groups + my_group
    devices = blocks * groups

    barrier = pltpu.get_barrier_semaphore()
    for step in range(1, devices):
        peer = (my_place + step) % devices
        pl.semaphore_signal(
            barrier, inc=1, device_id={"freq": peer // groups, "beam": peer % groups},
            device_id_type=pl.DeviceIdType.MESH,
        )

    chunks = in_sem.shape[0]
    span = width // chunks
    loads = [
        pltpu.make_async_copy(
            x_hbm.at[:, pl.ds(c * span, span)], x_ref.at[:, pl.ds(c * span, span)], in_sem.at[c]
        )
        for c in range(chunks)
    ]
    for load in loads:
        load.start()
    means, scales = [], []
    for c in range(chunks):
        loads[c].wait()
        total = jnp.zeros((span, samples), jnp.float32)
        squares = jnp.zeros((span, samples), jnp.float32)
        for beam in range(beams):
            wide = x_ref[beam, c * span:(c + 1) * span].astype(jnp.float32)
            total = total + wide
            squares = squares + wide * wide
        mean = jnp.sum(total, axis=1, keepdims=True) / row_total
        var = jnp.sum(squares, axis=1, keepdims=True) / row_total - mean * mean
        means.append(mean)
        scales.append(lax.rsqrt(var + epsilon))
    channel_mean = jnp.concatenate(means, axis=0)
    channel_scale = jnp.concatenate(scales, axis=0)
    out_row = lax.broadcasted_iota(jnp.int32, (blocks * bands, width), 0)
    channel = lax.broadcasted_iota(jnp.int32, (blocks * bands, width), 1)
    band = out_row % bands
    if fold:
        half = bands // 2
        band = (band % half) * 2 + band // half
    wanted = band * blocks + out_row // bands
    clean = mask_ref[:, pl.ds(pl.multiple_of(my_group * width, width), width)].astype(jnp.float32)
    chosen = jnp.where(channel // group == wanted, clean, 0.0).astype(jnp.bfloat16)
    upper = my_block * 2 >= blocks

    def message(block, slot, beam, rows):
        return pltpu.make_async_remote_copy(
            src_ref=send.at[block, slot, pl.ds(0, rows)],
            dst_ref=out_ref.at[beam % beam_dev, my_place, pl.ds(0, rows)],
            send_sem=send_sem.at[block, slot],
            recv_sem=recv_sem.at[beam % beam_dev, my_place],
            device_id={"freq": block, "beam": beam // beam_dev},
            device_id_type=pl.DeviceIdType.MESH,
        )

    def own_copy(slot, part):
        return pltpu.make_async_copy(
            send.at[my_block, slot], out_ref.at[part, my_place], own_sem.at[part]
        )

    def every_message(action, slot):
        beam = (my_group * beam_dev + slot) % beams
        for block in range(blocks):
            goes = my_place * width < limits[block]
            if slot < beam_dev:
                goes = goes & (my_block != block)
            if fold:
                @pl.when(goes & upper)
                def _(block=block):
                    action(message(block, slot, beam, bands // 2))
                goes = goes & jnp.logical_not(upper)

            @pl.when(goes)
            def _(block=block):
                action(message(block, slot, beam, bands))

    for slot in range(beams):
        beam = (my_group * beam_dev + slot) % beams
        wide = x_ref[beam].astype(jnp.float32)
        normed = ((wide - channel_mean) * channel_scale).astype(jnp.bfloat16)
        sums = jnp.dot(chosen, normed, preferred_element_type=jnp.float32)
        tree = [[sums[i * bands:(i + 1) * bands]] for i in range(blocks)]
        while len(tree) > 1:
            merged = []
            for low, high in zip(tree[0::2], tree[1::2]):
                merged.append(
                    [low[m // 2] + earlier(high[m // 2], (m + 1) // 2) for m in range(2 * len(low))]
                )
            tree = merged
        for number, row in enumerate(tree[0]):
            if fold:
                both = row[:half] + row[half:]
                row = jnp.concatenate([jnp.where(upper, both, row[:half]), row[half:]], axis=0)
            send[number, slot] = row.astype(jnp.bfloat16)
        if slot == 0:
            pl.semaphore_wait(barrier, devices - 1)
        every_message(lambda copy: copy.start(), slot)
        if slot < beam_dev:
            own_copy(slot, slot).start()

    for slot in range(beam_dev):
        own_copy(slot, slot).wait()
    limit = sum(jnp.where(my_block == block, limits[block], 0) for block in range(blocks))
    for place in range(devices):
        for part in range(beam_dev):
            rows = bands // 2 if fold and 2 * place >= devices else bands
            target = out_ref.at[part, place, pl.ds(0, rows)]
            @pl.when((place * width < limit) & (place != my_place))
            def _(target=target, place=place, part=part):
                pltpu.make_async_remote_copy(
                    src_ref=target, dst_ref=target, send_sem=send_sem.at[0, 0],
                    recv_sem=recv_sem.at[part, place],
                    device_id={"freq": my_block, "beam": my_group},
                    device_id_type=pl.DeviceIdType.MESH,
                ).wait_recv()
    for slot in range(beams):
        every_message(lambda copy: copy.wait_send(), slot)


def entry_rows(intensity, channel_mask):
    beams, width, samples = intensity.shape
    blocks, groups = lax.axis_size("freq"), lax.axis_size("beam")
    bands = width * NDM // (CHANS * blocks)
    beam_dev, devices = beams // groups, blocks * groups
    return pl.pallas_call(
        entry_kernel,
        in_specs=[pl.BlockSpec(memory_space=pl.ANY), pl.BlockSpec(memory_space=pltpu.VMEM)],
        out_specs=pl.BlockSpec(memory_space=pl.ANY),
        scratch_shapes=[
            pltpu.VMEM((beams, width, samples), jnp.bfloat16),
            pltpu.SemaphoreType.DMA((4,)),
            pltpu.VMEM((blocks, beams, bands, samples), jnp.bfloat16),
            pltpu.SemaphoreType.DMA((blocks, beams)),
            pltpu.SemaphoreType.DMA((beam_dev, devices)),
            pltpu.SemaphoreType.DMA((beam_dev,)),
        ],
        out_shape=jax.ShapeDtypeStruct((beam_dev, devices, bands, samples), jnp.bfloat16),
        compiler_params=pltpu.CompilerParams(collective_id=0, has_side_effects=True),
    )(intensity, channel_mask.reshape(1, -1))


def advanced(pieces, amount):
    lanes = pieces[0].shape[-1]
    position = lane_index(pieces[0].shape)
    turn = (lanes - amount) & (lanes - 1)
    turned = [pltpu.roll(piece, turn, 1) for piece in pieces]
    return joined(turned, lambda limit: position < limit - amount)


def advanced_rows(pieces, amounts):
    lanes = pieces[0].shape[-1]
    position = lane_index(pieces[0].shape) + amounts
    picks = position & (lanes - 1)
    turned = [jnp.take_along_axis(piece, picks, axis=1, mode="promise_in_bounds") for piece in pieces]
    return joined(turned, lambda limit: position < limit)


def joined(turned, below):
    lanes = turned[0].shape[-1]
    near = [below((k + 1) * lanes) for k in range(len(turned))]
    result = []
    for number in range(len(turned)):
        value = jnp.zeros_like(turned[0])
        for ahead in reversed(range(len(turned) - number)):
            value = jnp.where(near[ahead], turned[number + ahead], value)
        result.append(value)
    return result


def trial_kernel(place_ref, widths_ref, x_ref, out_ref, first, even, odd, series, prefix):
    total, samples = out_ref.shape[2], x_ref.shape[3]
    tiles = total // LANE_ROWS
    tile_bits = tiles.bit_length() - 1
    lanes = prefix.shape[2]
    parts = samples // lanes
    pitch = first.shape[1] // LANE_ROWS
    block = place_ref[0]
    bands = x_ref.shape[2]
    fold = folds(total, samples)
    half_bands = bands // 2
    sources = x_ref.shape[1]
    for number in range(sources):
        high, start = divmod(number * bands, tiles)
        start += reverse_bits(high, LANE_ROWS.bit_length() - 1) * pitch
        for part in range(parts):
            cut = slice(part * lanes, (part + 1) * lanes)
            if fold and 2 * number >= sources:
                first[part, start:start + half_bands] = x_ref[0, number, :half_bands, cut].astype(jnp.float32)
                first[part, start + half_bands:start + bands] = jnp.zeros((half_bands, lanes), jnp.float32)
            else:
                first[part, start:start + bands] = x_ref[0, number, :, cut].astype(jnp.float32)
    for tile in range(tiles):
        spot = tile
        if fold:
            band = tile % bands
            spot = tile - band + (band % 2) * half_bands + band // 2
        for part in range(parts):
            even[reverse_bits(tile, tile_bits), :, part * lanes:(part + 1) * lanes] = first[
                part, pl.ds(spot, LANE_ROWS, stride=pitch)
            ]

    source, target = even, odd
    count = 1
    while count < tiles:
        half = tiles // count // 2

        def merge(j, source=source, target=target, count=count, half=half):
            flat = (half * LANE_ROWS, lanes)
            cut = [slice(part * lanes, (part + 1) * lanes) for part in range(parts)]
            low = [source[pl.ds(j * 2 * half, half), :, c].reshape(flat) for c in cut]
            high = [source[pl.ds(j * 2 * half + half, half), :, c].reshape(flat) for c in cut]
            for side in range(2):
                moved = advanced(high, block * count + j + side)
                for c, base, extra in zip(cut, low, moved):
                    target[pl.ds((2 * j + side) * half, half), :, c] = (base + extra).reshape(
                        half, LANE_ROWS, lanes
                    )

        if count <= 16:
            for j in range(count):
                merge(j)
        else:
            def step(i, carry, merge=merge):
                for k in range(32):
                    merge(i * 32 + k)
                return carry
            lax.fori_loop(0, count // 32, step, 0)
        source, target = target, source
        count = count * 2

    spot = lax.broadcasted_iota(jnp.int32, (LANE_ROWS, lanes), 0)
    bits = [spot >> 2 & 1, spot >> 1 & 1, spot & 1]
    clear = [bit == 0 for bit in bits]

    def final_rows(j):
        pieces = [source[j, :, part * lanes:(part + 1) * lanes] for part in range(parts)]
        row = spot * 0 + (block * tiles + j)
        for level, reach in enumerate((4, 2, 1)):
            low, high = [], []
            for piece in pieces:
                down = pltpu.roll(piece, reach, 0)
                up = down if 2 * reach == LANE_ROWS else pltpu.roll(piece, LANE_ROWS - reach, 0)
                low.append(jnp.where(clear[level], piece, down))
                high.append(jnp.where(clear[level], up, piece))
            moved = advanced_rows(high, row + bits[level])
            pieces = [base + extra for base, extra in zip(low, moved)]
            row = 2 * row + bits[level]
        return jnp.concatenate(pieces, axis=1)

    def finish(i, carry):
        for k in range(16):
            pair = i * 16 + k
            rows = jnp.concatenate([final_rows(2 * pair), final_rows(2 * pair + 1)], axis=0)
            coarse = rows.astype(jnp.bfloat16)
            place = pl.ds(pl.multiple_of(pair * 16, 16), 16)
            series[place, :samples] = coarse
            series[place, samples:] = (rows - coarse.astype(jnp.float32)).astype(jnp.bfloat16)
        return carry

    lax.fori_loop(0, tiles // 32, finish, 0)

    until = lax.broadcasted_iota(jnp.int32, (samples, 2 * samples), 0)
    time = lax.broadcasted_iota(jnp.int32, (samples, 2 * samples), 1) & (samples - 1)
    ladder = jnp.where(time <= until, 1.0, 0.0).astype(jnp.bfloat16)
    margin = prefix.shape[1] - samples - LANE_ROWS
    piece = 2 * lanes
    for part in range(total // piece):
        sums = lax.dot_general(
            ladder, series[part * piece:(part + 1) * piece], (((1,), (1,)), ((), ())),
            preferred_element_type=jnp.float32,
        )
        for side in range(2):
            column = 2 * part + side
            prefix[column, :LANE_ROWS] = jnp.zeros((LANE_ROWS, lanes), jnp.float32)
            prefix[column, LANE_ROWS:LANE_ROWS + samples] = sums[:, side * lanes:(side + 1) * lanes]
            prefix[column, LANE_ROWS + samples:] = jnp.full((margin, lanes), -jnp.inf, jnp.float32)
    for column in range(total // lanes):
        best = None
        for number in range(widths_ref.shape[0]):
            width = widths_ref[number]
            sums = (
                prefix[column, pl.ds(LANE_ROWS - 1 + width, samples)]
                - prefix[column, LANE_ROWS - 1:LANE_ROWS - 1 + samples]
            )
            norm = lax.rsqrt(jnp.full((1, lanes), width * CHANS, jnp.int32).astype(jnp.float32))
            peak = jnp.max(sums, axis=0, keepdims=True) * norm
            best = peak if best is None else jnp.maximum(best, peak)
        out_ref[0, :, column * lanes:(column + 1) * lanes] = best


def trial_peaks(rows, box_widths, place):
    beams, devices, bands, samples = rows.shape
    total = devices * bands
    tiles = total // LANE_ROWS
    return pl.pallas_call(
        trial_kernel,
        grid_spec=pltpu.PrefetchScalarGridSpec(
            num_scalar_prefetch=2,
            grid=(beams,),
            in_specs=[pl.BlockSpec((1, devices, bands, samples), lambda b, p, w: (b, 0, 0, 0))],
            out_specs=pl.BlockSpec((1, 1, total), lambda b, p, w: (b, 0, 0)),
            scratch_shapes=[
                pltpu.VMEM((samples // LANES, total + LANE_ROWS * LANE_ROWS, LANES), jnp.float32),
                pltpu.VMEM((tiles, LANE_ROWS, samples), jnp.float32),
                pltpu.VMEM((tiles, LANE_ROWS, samples), jnp.float32),
                pltpu.VMEM((total, 2 * samples), jnp.bfloat16),
                pltpu.VMEM((total // LANES, LANE_ROWS + samples + WIDEST, LANES), jnp.float32),
            ],
        ),
        out_shape=jax.ShapeDtypeStruct((beams, 1, total), jnp.float32),
    )(place, box_widths, rows)[:, 0]


def compact(samples, devices, blocks, groups, beams, width):
    return (
        samples == 2 * LANES and NDM == 16 * samples and blocks == 4 and beams == groups
        and devices * LANE_ROWS == samples and width * devices == CHANS
    )


def block_span(block):
    return ((0, 8), (2, 8), (3, 6), (3, 6))[block]


def late_span(place, whole):
    return (0, 8) if place < whole else (4, 8)


def band_mask(depth, width):
    rows = LANE_ROWS * (2 << depth)
    row = lax.broadcasted_iota(jnp.int32, (rows, width), 0)
    channel = lax.broadcasted_iota(jnp.int32, (rows, width), 1)
    inner, tile = row % LANE_ROWS, row // LANE_ROWS
    if depth == 0:
        wanted = inner * 2 + tile
    else:
        quarter = tile % 4
        band = inner * 4 + (quarter % 2) * 2 + quarter // 2
        wanted = band * (rows // (4 * LANE_ROWS)) + tile // 4
    return channel // (width // rows) == wanted


def stepped(pair, amount):
    if amount == 0:
        return list(pair)
    lane = lane_index(pair[1].shape)
    near = lane < LANES - amount
    turned = [None if piece is None else pltpu.roll(piece, LANES - amount, 1) for piece in pair]
    early = None if turned[0] is None else jnp.where(near, turned[0], turned[1])
    return [early, jnp.where(near, turned[1], 0.0)]


def plus(low, high):
    return [a + b for a, b in zip(low, high)]


def near_leaves(tiles):
    if len(tiles) == 4:
        wide = [plus(tiles[0], tiles[2]), plus(tiles[1], tiles[3])]
    else:
        wide = tiles
    zero = plus(wide[0], wide[1])
    first = plus(wide[0], stepped(wide[1], 1))
    message = [None, None, first[0], first[1], zero[0], zero[1], None, None]
    if len(tiles) == 4:
        second = [plus(tiles[a], stepped(tiles[2 + a], 1)) for a in range(2)]
        message[0], message[1] = second[0][0], second[1][0]
        message[6], message[7] = second[0][1], second[1][1]
    return message


def far_leaves(tiles):
    parts = [tiles[at:at + 4] for at in range(0, len(tiles), 4)]
    halves = parts if len(parts) == 2 else [[plus(a, b) for a, b in zip(*parts[at:at + 2])] for at in (0, 2)]
    out = {1: [plus(low, stepped(high, 1)) for low, high in zip(*halves)]}
    if len(parts) == 4:
        one, two = [[plus(a, stepped(b, 1)) for a, b in zip(*parts[at:at + 2])] for at in (0, 2)]
        for block in (2, 3):
            out[block] = [plus(low, stepped(high, block - 1)) for low, high in zip(one, two)]
    return {block: [pair[part] for part in range(2) for pair in pairs] for block, pairs in out.items()}


def search_kernel(
    x_hbm, mask_hbm, widths_hbm, out_ref, x_ref, unit_ref, mask_ref, widths_ref, in_sem, send, send_sem, recv, recv_sem,
    ready_sem, first, work, mid, planes, double, lower, series, prefix,
):
    beams, width, samples = x_ref.shape
    blocks, groups = lax.axis_size("freq"), lax.axis_size("beam")
    devices = blocks * groups
    row_total = float(beams * samples)
    my_block = lax.axis_index("freq")
    my_group = lax.axis_index("beam")
    my_place = my_block * groups + my_group
    quarter = groups // 2

    chunks = in_sem.shape[0] - 2
    span = width // chunks
    loads = [
        pltpu.make_async_copy(
            x_hbm.at[:, pl.ds(c * span, span)], x_ref.at[:, pl.ds(c * span, span)], in_sem.at[c]
        )
        for c in range(chunks)
    ]
    mask_load = pltpu.make_async_copy(mask_hbm, mask_ref, in_sem.at[chunks])
    widths_load = pltpu.make_async_copy(widths_hbm, widths_ref, in_sem.at[chunks + 1])
    loads[0].start()
    mask_load.start()
    for load in loads[1:]:
        load.start()
    widths_load.start()

    def signal(semaphore, place):
        pl.semaphore_signal(
            semaphore, inc=1, device_id={"freq": place // groups, "beam": place % groups},
            device_id_type=pl.DeviceIdType.MESH,
        )

    barrier = pltpu.get_barrier_semaphore()

    @pl.when(my_block == 0)
    def _():
        for step in range(1, devices):
            signal(barrier, (my_place + devices - step) % devices)

    @pl.when(my_block == 1)
    def _():
        for place in range(groups):
            signal(barrier, place)

    @pl.when(my_block >= 2)
    def _():
        pl.semaphore_wait(barrier, groups)
        for place in range(quarter):
            signal(ready_sem, place)

    for column in range(prefix.shape[0]):
        prefix[column, :LANE_ROWS] = jnp.zeros((LANE_ROWS, LANES), jnp.float32)
        prefix[column, LANE_ROWS + samples:] = jnp.full((WIDEST, LANES), -jnp.inf, jnp.float32)

    lane = lax.broadcasted_iota(jnp.int32, (LANE_ROWS, LANES), 1)
    inner = lax.broadcasted_iota(jnp.int32, (LANE_ROWS, LANES), 0)
    unit_ref[...] = jnp.ones(unit_ref.shape, jnp.bfloat16)
    means, scales = [], []
    for c in range(chunks):
        loads[c].wait()
        if c == 0:
            mask_load.wait()
        unit = unit_ref[...].astype(jnp.float32)
        totals = []
        for column in range(span // LANES):
            found = [jnp.zeros((LANE_ROWS, LANES), jnp.float32) for _ in range(2)]
            for pair in range(LANES // (2 * LANE_ROWS)):
                at = c * span + column * LANES + pair * 2 * LANE_ROWS
                sums = [jnp.zeros((2 * LANE_ROWS, samples), jnp.float32) for _ in range(2)]
                for b in range(beams):
                    wide = x_ref[b, at:at + 2 * LANE_ROWS].astype(jnp.float32)
                    sums = [sums[0] + wide * unit, sums[1] + wide * wide]
                sums = [jnp.sum(value, axis=1, keepdims=True) for value in sums]
                for half in range(2):
                    spot = lane == inner + (2 * pair + half) * LANE_ROWS
                    cut = slice(half * LANE_ROWS, (half + 1) * LANE_ROWS)
                    found = [have + jnp.where(spot, value[cut], 0.0) for have, value in zip(found, sums)]
            totals.append([jnp.sum(value, axis=0, keepdims=True) for value in found])
        mean = jnp.concatenate([total[0] for total in totals], axis=1) / row_total
        var = jnp.concatenate([total[1] for total in totals], axis=1) / row_total - mean * mean
        place = pl.multiple_of(my_group * width + c * span, span)
        clean = mask_ref[:, pl.ds(place, span)].astype(jnp.float32)
        means.append(mean)
        scales.append(lax.rsqrt(var + epsilon) * clean)
    channel_mean = jnp.concatenate(means, axis=1)
    channel_scale = jnp.concatenate(scales, axis=1)
    coarse = channel_scale.astype(jnp.bfloat16).astype(jnp.float32)
    fine = (channel_scale - coarse).astype(jnp.bfloat16).astype(jnp.float32)
    offset = channel_mean * (coarse + fine)

    def summing(depth):
        chosen = band_mask(depth, width)
        matrix = jnp.concatenate(
            [jnp.where(chosen, coarse, 0.0), jnp.where(chosen, fine, 0.0)], axis=1
        ).astype(jnp.bfloat16)
        shift = jnp.sum(jnp.where(chosen, offset, 0.0), axis=1, keepdims=True)

        def tiles(slot):
            rows = x_ref[(my_group + slot) % beams]
            sums = jnp.dot(
                matrix, jnp.concatenate([rows, rows], axis=0), preferred_element_type=jnp.float32
            ) - shift
            return [
                [sums[t:t + LANE_ROWS, p * LANES:(p + 1) * LANES] for p in range(2)]
                for t in range(0, chosen.shape[0], LANE_ROWS)
            ]

        return tiles

    def message(block, slot, begin, end):
        return pltpu.make_async_remote_copy(
            src_ref=send.at[block, slot, pl.ds(begin, end - begin)],
            dst_ref=recv.at[my_place, pl.ds(begin, end - begin)],
            send_sem=send_sem.at[block, slot],
            recv_sem=recv_sem.at[my_place],
            device_id={"freq": block, "beam": (my_group + slot) % beams},
            device_id_type=pl.DeviceIdType.MESH,
        )

    def near_messages(action, slot, narrow):
        if narrow:
            action(message(0, slot, *block_span(2)))
            return

        @pl.when(my_block == 1)
        def _():
            action(message(0, slot, *block_span(1)))
        if slot > 0:
            @pl.when(my_block == 0)
            def _():
                action(message(0, slot, *block_span(0)))

    def near_phase(narrow):
        tiles = summing(0 if narrow else 1)
        batch = 4
        for begin in range(0, beams, batch):
            slots = range(begin, begin + batch)
            for slot, summed in [(slot, tiles(slot)) for slot in slots]:
                for number, leaf in enumerate(near_leaves(summed)):
                    if leaf is not None:
                        send[0, slot, number] = leaf.astype(jnp.bfloat16)
                if slot == 0 and not narrow:
                    @pl.when(my_block == 0)
                    def _():
                        recv[my_place] = send[0, 0]
            if begin == 0 and not narrow:
                pl.semaphore_wait(barrier, jnp.where(my_block == 0, 2 * groups - 1, groups))
            for slot in slots:
                near_messages(lambda copy: copy.start(), slot, narrow)

    def next_messages(action, slot, low):
        action(message(1, slot, 0 if low else 4, 8))

    def last_messages(action, slot):
        for half in range(2):
            @pl.when((my_group * 2 >= quarter) if half else (my_group * 2 < quarter))
            def _(half=half):
                for block in (3, 2):
                    action(message(block, slot, 4 * half, 8))

    def far_phase(low):
        tiles = summing(3 if low else 2)
        batch = 2
        for begin in range(0, beams, batch):
            slots = range(begin, begin + batch)
            for slot, summed in [(slot, tiles(slot)) for slot in slots]:
                for block, leaves in far_leaves(summed).items():
                    for number, leaf in enumerate(leaves):
                        send[block, slot, number] = leaf.astype(jnp.bfloat16)
            for slot in slots:
                next_messages(lambda copy: copy.start(), slot, low)
        if low:
            pl.semaphore_wait(ready_sem, 2 * groups)
            for slot in range(beams):
                last_messages(lambda copy: copy.start(), slot)

    def arrival(place, begin, end):
        target = recv.at[place, pl.ds(begin, end - begin)]
        pltpu.make_async_remote_copy(
            src_ref=target, dst_ref=target, send_sem=send_sem.at[0, 0], recv_sem=recv_sem.at[place],
            device_id={"freq": my_block, "beam": my_group}, device_id_type=pl.DeviceIdType.MESH,
        ).wait_recv()

    args = (recv, first, work, mid, series)
    pitch = first.shape[1] // LANE_ROWS

    def wide_places(count, numbers_of):
        per = count // LANE_ROWS
        return [
            ((place // per) * pitch + (place % per) * (pitch - LANE_ROWS) // per + address, place, numbers)
            for place in range(count) for address, numbers in numbers_of(place)
        ]

    @pl.when(my_block < 2)
    def _():
        near_phase(False)

    @pl.when(my_block >= 2)
    def _():
        near_phase(True)

    for low in (True, False):
        @pl.when((my_block == 0) & ((my_group < quarter) == low))
        def _(low=low):
            far_phase(low)

    widths_load.wait()

    @pl.when(my_block == 0)
    def _():
        for place in range(groups):
            @pl.when(place != my_group)
            def _(place=place):
                arrival(place, *block_span(0))
        plane_rows(recv, first, mid, double, 0, groups, 1, ((0, 6), (1, 7)))
        for root in range(2):
            plane_rows(recv, first, mid, planes.at[root], 0, groups, root, ((4 - 2 * root, 5 - 2 * root),))
        for place in range(groups, 2 * groups):
            arrival(place, *block_span(1))
        plane_rows(recv, first, mid, double, 1, groups, 1, ((None, 6), (None, 7)))
        double_rows(double, series, 0)
        for root in range(2):
            plane_rows(recv, first, mid, planes.at[root], 1, groups, root, ((4 - 2 * root, 5 - 2 * root),))
        for root in range(2):
            lower_rows(planes.at[root], lower.at[root], root)
        unpermuted(boxcar_rows(widths_ref, series, prefix, 0, 2), out_ref, 512, 1, 4)
        for plane in range(2, blocks):
            for place in range(plane * groups, (plane + 1) * groups):
                arrival(place, *block_span(2))
            for root in range(2):
                numbers = ((4, 5) if root == 0 else (None, 3),)
                plane_rows(recv, first, mid, planes.at[root], plane, groups, root, numbers)
        for root in range(2):
            upper_rows(planes.at[root], lower.at[root], series, 256 * (1 + root), root)
        result = boxcar_rows(widths_ref, series, prefix, 2, 4)
        unfolded(result[:2], out_ref, 0)
        unfolded(result[2:], out_ref, 256)

    @pl.when(my_block == 1)
    def _():
        for place in range(groups):
            arrival(place, *late_span(place, quarter))
        unit_rows(*args, 0, 1, 256, 2, wide_places(
            groups,
            lambda place: [
                (8 * (2 * (q % 2) + q // 2), (q if place < quarter else None, 4 + q)) for q in range(4)
            ],
        ))
        unpermuted(boxcar_rows(widths_ref, series, prefix, 0, 2), out_ref, 0, 2, 3)

    for late in (2, 3):
        @pl.when(my_block == late)
        def _(late=late):
            found = []
            for place in range(quarter):
                arrival(place, *late_span(place, quarter // 2))
                for q in range(4):
                    found.append((
                        (2 * (q % 2) + q // 2) * pitch + place * LANE_ROWS, place,
                        (q if 2 * place < quarter else None, 4 + q),
                    ))
            unit_rows(*args, 0, late, 128, 2, found)
            unpermuted(boxcar_rows(widths_ref, series, prefix, 0, 1), out_ref, 0, 3, 3)

    for slot in range(beams):
        for narrow in (True, False):
            @pl.when((my_block >= 2) == narrow)
            def _(narrow=narrow, slot=slot):
                near_messages(lambda copy: copy.wait_send(), slot, narrow)
        for low in (True, False):
            @pl.when((my_block == 0) & ((my_group < quarter) == low))
            def _(low=low, slot=slot):
                next_messages(lambda copy: copy.wait_send(), slot, low)
                if low:
                    last_messages(lambda copy: copy.wait_send(), slot)


def search(intensity, channel_mask, box_widths):
    beams, width, samples = intensity.shape
    blocks, groups = lax.axis_size("freq"), lax.axis_size("beam")
    devices = blocks * groups
    operands = (intensity, channel_mask.reshape(1, -1), box_widths)
    return pl.pallas_call(
        search_kernel,
        in_specs=[pl.BlockSpec(memory_space=pl.ANY)] * 3,
        out_specs=pl.BlockSpec(memory_space=pltpu.VMEM),
        scratch_shapes=[
            pltpu.VMEM((beams, width, samples), jnp.bfloat16),
            pltpu.VMEM((2 * LANE_ROWS, samples), jnp.bfloat16),
            pltpu.VMEM((1, width * groups), jnp.int32),
            pltpu.SMEM(box_widths.shape, jnp.int32),
            pltpu.SemaphoreType.DMA((6,)),
            pltpu.VMEM((blocks, beams, 8, LANE_ROWS, LANES), jnp.bfloat16),
            pltpu.SemaphoreType.DMA((blocks, beams)),
            pltpu.VMEM((devices, 8, LANE_ROWS, LANES), jnp.bfloat16),
            pltpu.SemaphoreType.DMA((devices,)),
            pltpu.SemaphoreType.REGULAR,
            pltpu.VMEM((2, samples + LANE_ROWS * LANE_ROWS, LANES), jnp.float32),
            pltpu.VMEM((2, samples, LANES), jnp.float32),
            pltpu.VMEM((2, samples, LANES), jnp.float32),
            pltpu.VMEM((2, blocks, 2, LANE_ROWS * LANE_ROWS, LANES), jnp.float32),
            pltpu.VMEM((2, 2, LANES, LANES), jnp.float32),
            pltpu.VMEM((2, 2, LANES, LANES), jnp.float32),
            pltpu.VMEM((3 * samples, 2 * samples), jnp.bfloat16),
            pltpu.VMEM((6, LANE_ROWS + samples + WIDEST, LANES), jnp.float32),
        ],
        out_shape=jax.ShapeDtypeStruct((1, NDM // blocks), jnp.float32),
        compiler_params=pltpu.CompilerParams(collective_id=0, has_side_effects=True, vmem_limit_bytes=32 << 20),
    )(*[pltpu.with_memory_space_constraint(value, pltpu.HBM) for value in operands])


def ramped(pair, start, stride, far, only_late=False):
    shape = pair[1].shape
    place = lane_index(shape) + (lax.broadcasted_iota(jnp.int32, shape, 0) * stride + start)
    picks = place & (LANES - 1)
    late = jnp.take_along_axis(pair[1], picks, axis=1, mode="promise_in_bounds")
    if far:
        return [jnp.where(place < 2 * LANES, late, 0.0), None]
    near = place < LANES
    moved = [None, jnp.where(near, late, 0.0)]
    if not only_late:
        early = jnp.take_along_axis(pair[0], picks, axis=1, mode="promise_in_bounds")
        moved[0] = jnp.where(near, early, late)
    return moved


def joined_pair(low, high):
    return [a if b is None else (None if a is None else a + b) for a, b in zip(low, high)]


def unit_rows(recv, first, work, mid, series, base, root, leaves, kinds, found):
    tiles = leaves // LANE_ROWS
    pitch = first.shape[1] // LANE_ROWS
    for address, place, numbers in found:
        for part in range(2):
            if numbers[part] is not None:
                first[part, address:address + LANE_ROWS] = recv[place, numbers[part]].astype(jnp.float32)

    def leaf(tile, part):
        outer, kind = tile >> kinds, tile & ((1 << kinds) - 1)
        if leaves == LANE_ROWS * (pitch - LANE_ROWS):
            spot, step = ((outer >> 3 << kinds) + kind) * LANE_ROWS + (outer & 7), pitch
        else:
            spot, step = kind * pitch + outer, LANE_ROWS // 2
        return first[part, pl.ds(spot, LANE_ROWS, stride=step)]

    chunk = 8
    for c in range(tiles // chunk):
        tree = [[[leaf(c * chunk + k, part) for part in range(2)]] for k in range(chunk)]
        level_root = root
        while len(tree) > 1:
            tree = [
                [
                    plus(low[r // 2], stepped(high[r // 2], level_root + r // 2 + r % 2))
                    for r in range(2 * len(low))
                ]
                for low, high in zip(tree[0::2], tree[1::2])
            ]
            level_root = level_root * 2
        for j in range(chunk):
            for part in range(2):
                at = (j * (tiles // chunk) + c) * LANE_ROWS
                work[part, at:at + LANE_ROWS] = tree[0][j][part]
    chunks = tiles // chunk
    for j in range(chunk):
        tree = []
        for c in range(chunks):
            at = (j * chunks + c) * LANE_ROWS
            tree.append([[work[part, at:at + LANE_ROWS] for part in range(2)]])
        level_root = root * chunk + j
        while len(tree) > 1:
            tree = [
                [
                    plus(low[r // 2], stepped(high[r // 2], level_root + r // 2 + r % 2))
                    for r in range(2 * len(low))
                ]
                for low, high in zip(tree[0::2], tree[1::2])
            ]
            level_root = level_root * 2
        for k in range(chunks):
            for part in range(2):
                at = (j * chunks + k) * LANE_ROWS
                mid[part, at:at + LANE_ROWS] = tree[0][k][part]
    far = root > 0
    for g in range(tiles // LANE_ROWS):
        tree = []
        for s in range(LANE_ROWS):
            pair = [
                None if far and 2 * s >= LANE_ROWS and part == 0
                else mid[part, pl.ds(g * LANE_ROWS * LANE_ROWS + s, LANE_ROWS, stride=LANE_ROWS)]
                for part in range(2)
            ]
            tree.append([pair])
        rows = merged_rows(tree, root * tiles + g * LANE_ROWS, 1, far)
        for k in range(0, LANE_ROWS, 2):
            save_series(series, base + g * LANE_ROWS * LANE_ROWS + k * LANE_ROWS, rows[k:k + 2])


def merged_rows(tree, start, stride, far):
    while len(tree) > 1:
        tree = [
            [
                joined_pair(
                    low[r // 2],
                    ramped(
                        high[r // 2], start + r // 2 + r % 2, stride, far and len(tree) == 2,
                        high[r // 2][0] is None,
                    ),
                )
                for r in range(2 * len(low))
            ]
            for low, high in zip(tree[0::2], tree[1::2])
        ]
        start, stride = start * 2, stride * 2
    return tree[0]


def plane_rows(recv, first, mid, target, plane, groups, root, numbers):
    kinds = len(numbers)
    parts = [part for part in range(2) if numbers[0][part] is not None]
    flat = LANE_ROWS * LANE_ROWS
    for place in range(groups):
        for kind in range(kinds):
            for part in parts:
                at = kind * flat + place * LANE_ROWS
                first[part, at:at + LANE_ROWS] = recv[plane * groups + place, numbers[kind][part]].astype(jnp.float32)

    def pair_at(source, start):
        return [source[part, pl.ds(start, LANE_ROWS, stride=LANE_ROWS)] if part in parts else None for part in range(2)]

    tree = [[pair_at(first, (tile % kinds) * flat + tile // kinds)] for tile in range(kinds * LANE_ROWS)]
    level_root = root
    while len(tree) > 1:
        tree = [
            [
                joined_pair(low[r // 2], stepped(high[r // 2], level_root + r // 2 + r % 2))
                for r in range(2 * len(low))
            ]
            for low, high in zip(tree[0::2], tree[1::2])
        ]
        level_root = level_root * 2
    for j, pair in enumerate(tree[0]):
        for part in parts:
            mid[part, j * LANE_ROWS:(j + 1) * LANE_ROWS] = pair[part]
    for g in range(kinds):
        tree = [[pair_at(mid, g * flat + p)] for p in range(LANE_ROWS)]
        for k, pair in enumerate(merged_rows(tree, (root * kinds + g) * LANE_ROWS, 1, False)):
            at = g * flat + k * LANE_ROWS
            for part in parts:
                target[plane, part, at:at + LANE_ROWS] = pair[part]


def double_rows(target, series, base):
    for g in range(2):
        for k in range(LANE_ROWS):
            number = g * LANE_ROWS + k
            tree = [[plane_tile(target, 0, number, (0, 1))], [plane_tile(target, 1, number, (1,))]]
            rows = merged_rows(tree, LANES + g * LANE_ROWS * LANE_ROWS + k, LANE_ROWS, True)
            save_series(series, base + 2 * number * LANE_ROWS, rows)


def plane_tile(target, plane, k, parts):
    return [
        target[plane, part, k * LANE_ROWS:(k + 1) * LANE_ROWS] if part in parts else None for part in range(2)
    ]


def lower_rows(target, lower, root):
    for k in range(LANE_ROWS):
        tree = [[plane_tile(target, plane, k, (0, 1))] for plane in range(2)]
        for q, pair in enumerate(merged_rows(tree, root * LANE_ROWS * LANE_ROWS + k, LANE_ROWS, False)):
            for part in range(2):
                at = (2 * k + q) * LANE_ROWS
                lower[part, at:at + LANE_ROWS] = pair[part]


def upper_rows(target, lower, series, base, root):
    parts = (0, 1) if root == 0 else (1,)
    for k in range(LANE_ROWS):
        begin = root * LANE_ROWS * LANE_ROWS + k
        high = merged_rows([[plane_tile(target, plane, k, parts)] for plane in (2, 3)], begin, LANE_ROWS, False)
        low = []
        for q in range(2):
            at = (2 * k + q) * LANE_ROWS
            low.append([lower[part, at:at + LANE_ROWS] for part in range(2)])
        rows = merged_rows([low, high], begin * 2, 2 * LANE_ROWS, root > 0)
        for number in range(0, 4, 2):
            save_series(series, base + (4 * k + number) * LANE_ROWS, rows[number:number + 2])


def save_series(series, at, pairs):
    rows = jnp.concatenate([jnp.concatenate(pair, axis=1) for pair in pairs], axis=0)
    coarse = rows.astype(jnp.bfloat16)
    samples = rows.shape[1]
    series[at:at + 2 * LANE_ROWS, :samples] = coarse
    series[at:at + 2 * LANE_ROWS, samples:] = (rows - coarse.astype(jnp.float32)).astype(jnp.bfloat16)


def unfolded(columns, out_ref, offset):
    lane = lane_index((LANE_ROWS, LANES))
    for number in range(2):
        picks = (lane & 15) * LANE_ROWS + (lane >> 5) + 4 * number
        spread = [jnp.take_along_axis(column, picks, axis=1, mode="promise_in_bounds") for column in columns]
        at = offset + number * LANES
        out_ref[:, at:at + LANES] = jnp.where(lane & 16 == 0, spread[0], spread[1])[:1]


def boxcar_rows(widths_ref, series, prefix, begin, count):
    lanes = prefix.shape[2]
    samples = series.shape[1] // 2
    until = lax.broadcasted_iota(jnp.int32, (samples, 2 * samples), 0)
    time = lax.broadcasted_iota(jnp.int32, (samples, 2 * samples), 1) & (samples - 1)
    ladder = jnp.where(time <= until, 1.0, 0.0).astype(jnp.bfloat16)
    piece = min(2, count)
    for start in range(begin, begin + count, piece):
        sums = lax.dot_general(
            ladder, series[start * lanes:(start + piece) * lanes], (((1,), (1,)), ((), ())),
            preferred_element_type=jnp.float32,
        )
        for side in range(piece):
            prefix[start + side, LANE_ROWS:LANE_ROWS + samples] = sums[:, side * lanes:(side + 1) * lanes]
    widths = [widths_ref[number] for number in range(widths_ref.shape[0])]
    norms = [
        lax.rsqrt(jnp.full((LANE_ROWS, lanes), width * CHANS, jnp.int32).astype(jnp.float32)) for width in widths
    ]
    result = []
    for column in range(begin, begin + count):
        ahead = [prefix[column, pl.ds(LANE_ROWS - 1 + width, samples)] for width in widths]
        base = prefix[column, LANE_ROWS - 1:LANE_ROWS - 1 + samples]
        best = [None] * len(widths)
        for at in range(0, samples, LANE_ROWS):
            before = base[at:at + LANE_ROWS]
            for number, after in enumerate(ahead):
                gain = after[at:at + LANE_ROWS] - before
                best[number] = gain if at == 0 else jnp.maximum(best[number], gain)
        peak = best[0] * norms[0]
        for value, norm in zip(best[1:], norms[1:]):
            peak = jnp.maximum(peak, value * norm)
        result.append(jnp.broadcast_to(jnp.max(peak, axis=0, keepdims=True), (LANE_ROWS, lanes)))
    return result


def unpermuted(columns, out_ref, offset, repeat_bits, bits):
    lane = lane_index((LANE_ROWS, LANES))
    for number in range(len(columns) << repeat_bits):
        row = (lane + number * LANES) >> repeat_bits
        row = row & (LANES - 1)
        block = LANE_ROWS << bits
        picks = (row & (LANES - block)) + (row & ((1 << bits) - 1)) * LANE_ROWS + ((row & (block - 1)) >> bits)
        column = columns[number >> repeat_bits]
        spread = jnp.take_along_axis(column, picks, axis=1, mode="promise_in_bounds")
        at = offset + number * LANES
        out_ref[:, at:at + LANES] = spread[:1]


def shards(intensity, channel_mask, box_widths):
    beams, width, samples = intensity.shape
    blocks, groups = lax.axis_size("freq"), lax.axis_size("beam")
    if compact(samples, blocks * groups, blocks, groups, beams, width):
        return search(intensity, channel_mask, box_widths)
    rows = entry_rows(intensity, channel_mask)
    return trial_peaks(rows, box_widths, lax.axis_index("freq").reshape(1))


def solution(mesh):
    in_specs = (P(None, ("freq", "beam"), None), P("freq"), P())
    out_specs = P("beam", "freq")
    return jax.shard_map(shards, mesh=mesh, in_specs=in_specs, out_specs=out_specs, check_vma=False)
```

```python
import jax
import jax.numpy as jnp
from jax import lax
from jax.experimental import pallas as pl
from jax.experimental.pallas import tpu as pltpu
from jax.sharding import PartitionSpec as P

CHANS = 16384
NDM = 4096
LANE_ROWS = 8
LANES = 128
WIDEST = 64

epsilon = 1e-05


def reverse_bits(number, count):
    result = 0
    for _ in range(count):
        result = result << 1 | number & 1
        number >>= 1
    return result


def lane_index(shape):
    return lax.broadcasted_iota(jnp.int32, shape, len(shape) - 1)


def earlier(block, amount):
    if amount == 0:
        return block
    samples = block.shape[-1]
    return jnp.where(lane_index(block.shape) < samples - amount, pltpu.roll(block, samples - amount, 1), 0.0)


def folds(trial_dev, samples):
    return trial_dev >= 4 * samples


def channel_limits(trial_dev, blocks, samples):
    limits = []
    for block in range(blocks):
        limit, rows = CHANS, NDM
        while (block * trial_dev * rows // NDM + 1) // 2 >= samples:
            limit, rows = limit // 2, rows // 2
        limits.append(limit)
    return limits


def entry_kernel(x_hbm, mask_ref, out_ref, x_ref, in_sem, send, send_sem, recv_sem, own_sem):
    blocks, beams, bands, samples = send.shape
    groups = lax.axis_size("beam")
    beam_dev = beams // groups
    width = x_ref.shape[1]
    group = width // (bands * blocks)
    trial_dev = NDM // blocks
    row_total = float(beams * samples)
    fold = folds(trial_dev, samples)
    limits = channel_limits(trial_dev, blocks, samples)
    my_block = lax.axis_index("freq")
    my_group = lax.axis_index("beam")
    my_place = my_block * groups + my_group
    devices = blocks * groups

    barrier = pltpu.get_barrier_semaphore()
    for step in range(1, devices):
        peer = (my_place + step) % devices
        pl.semaphore_signal(
            barrier, inc=1, device_id={"freq": peer // groups, "beam": peer % groups},
            device_id_type=pl.DeviceIdType.MESH,
        )

    chunks = in_sem.shape[0]
    span = width // chunks
    loads = [
        pltpu.make_async_copy(
            x_hbm.at[:, pl.ds(c * span, span)], x_ref.at[:, pl.ds(c * span, span)], in_sem.at[c]
        )
        for c in range(chunks)
    ]
    for load in loads:
        load.start()
    means, scales = [], []
    for c in range(chunks):
        loads[c].wait()
        total = jnp.zeros((span, samples), jnp.float32)
        squares = jnp.zeros((span, samples), jnp.float32)
        for beam in range(beams):
            wide = x_ref[beam, c * span:(c + 1) * span].astype(jnp.float32)
            total = total + wide
            squares = squares + wide * wide
        mean = jnp.sum(total, axis=1, keepdims=True) / row_total
        var = jnp.sum(squares, axis=1, keepdims=True) / row_total - mean * mean
        means.append(mean)
        scales.append(lax.rsqrt(var + epsilon))
    channel_mean = jnp.concatenate(means, axis=0)
    channel_scale = jnp.concatenate(scales, axis=0)
    out_row = lax.broadcasted_iota(jnp.int32, (blocks * bands, width), 0)
    channel = lax.broadcasted_iota(jnp.int32, (blocks * bands, width), 1)
    band = out_row % bands
    if fold:
        half = bands // 2
        band = (band % half) * 2 + band // half
    wanted = band * blocks + out_row // bands
    clean = mask_ref[:, pl.ds(pl.multiple_of(my_group * width, width), width)].astype(jnp.float32)
    chosen = jnp.where(channel // group == wanted, clean, 0.0).astype(jnp.bfloat16)
    upper = my_block * 2 >= blocks

    def message(block, slot, beam, rows):
        return pltpu.make_async_remote_copy(
            src_ref=send.at[block, slot, pl.ds(0, rows)],
            dst_ref=out_ref.at[beam % beam_dev, my_place, pl.ds(0, rows)],
            send_sem=send_sem.at[block, slot],
            recv_sem=recv_sem.at[beam % beam_dev, my_place],
            device_id={"freq": block, "beam": beam // beam_dev},
            device_id_type=pl.DeviceIdType.MESH,
        )

    def own_copy(slot, part):
        return pltpu.make_async_copy(
            send.at[my_block, slot], out_ref.at[part, my_place], own_sem.at[part]
        )

    def every_message(action, slot):
        beam = (my_group * beam_dev + slot) % beams
        for block in range(blocks):
            goes = my_place * width < limits[block]
            if slot < beam_dev:
                goes = goes & (my_block != block)
            if fold:
                @pl.when(goes & upper)
                def _(block=block):
                    action(message(block, slot, beam, bands // 2))
                goes = goes & jnp.logical_not(upper)

            @pl.when(goes)
            def _(block=block):
                action(message(block, slot, beam, bands))

    for slot in range(beams):
        beam = (my_group * beam_dev + slot) % beams
        wide = x_ref[beam].astype(jnp.float32)
        normed = ((wide - channel_mean) * channel_scale).astype(jnp.bfloat16)
        sums = jnp.dot(chosen, normed, preferred_element_type=jnp.float32)
        tree = [[sums[i * bands:(i + 1) * bands]] for i in range(blocks)]
        while len(tree) > 1:
            merged = []
            for low, high in zip(tree[0::2], tree[1::2]):
                merged.append(
                    [low[m // 2] + earlier(high[m // 2], (m + 1) // 2) for m in range(2 * len(low))]
                )
            tree = merged
        for number, row in enumerate(tree[0]):
            if fold:
                both = row[:half] + row[half:]
                row = jnp.concatenate([jnp.where(upper, both, row[:half]), row[half:]], axis=0)
            send[number, slot] = row.astype(jnp.bfloat16)
        if slot == 0:
            pl.semaphore_wait(barrier, devices - 1)
        every_message(lambda copy: copy.start(), slot)
        if slot < beam_dev:
            own_copy(slot, slot).start()

    for slot in range(beam_dev):
        own_copy(slot, slot).wait()
    limit = sum(jnp.where(my_block == block, limits[block], 0) for block in range(blocks))
    for place in range(devices):
        for part in range(beam_dev):
            rows = bands // 2 if fold and 2 * place >= devices else bands
            target = out_ref.at[part, place, pl.ds(0, rows)]
            @pl.when((place * width < limit) & (place != my_place))
            def _(target=target, place=place, part=part):
                pltpu.make_async_remote_copy(
                    src_ref=target, dst_ref=target, send_sem=send_sem.at[0, 0],
                    recv_sem=recv_sem.at[part, place],
                    device_id={"freq": my_block, "beam": my_group},
                    device_id_type=pl.DeviceIdType.MESH,
                ).wait_recv()
    for slot in range(beams):
        every_message(lambda copy: copy.wait_send(), slot)


def entry_rows(intensity, channel_mask):
    beams, width, samples = intensity.shape
    blocks, groups = lax.axis_size("freq"), lax.axis_size("beam")
    bands = width * NDM // (CHANS * blocks)
    beam_dev, devices = beams // groups, blocks * groups
    return pl.pallas_call(
        entry_kernel,
        in_specs=[pl.BlockSpec(memory_space=pl.ANY), pl.BlockSpec(memory_space=pltpu.VMEM)],
        out_specs=pl.BlockSpec(memory_space=pl.ANY),
        scratch_shapes=[
            pltpu.VMEM((beams, width, samples), jnp.bfloat16),
            pltpu.SemaphoreType.DMA((4,)),
            pltpu.VMEM((blocks, beams, bands, samples), jnp.bfloat16),
            pltpu.SemaphoreType.DMA((blocks, beams)),
            pltpu.SemaphoreType.DMA((beam_dev, devices)),
            pltpu.SemaphoreType.DMA((beam_dev,)),
        ],
        out_shape=jax.ShapeDtypeStruct((beam_dev, devices, bands, samples), jnp.bfloat16),
        compiler_params=pltpu.CompilerParams(collective_id=0, has_side_effects=True),
    )(intensity, channel_mask.reshape(1, -1))


def advanced(pieces, amount):
    lanes = pieces[0].shape[-1]
    position = lane_index(pieces[0].shape)
    turn = (lanes - amount) & (lanes - 1)
    turned = [pltpu.roll(piece, turn, 1) for piece in pieces]
    return joined(turned, lambda limit: position < limit - amount)


def advanced_rows(pieces, amounts):
    lanes = pieces[0].shape[-1]
    position = lane_index(pieces[0].shape) + amounts
    picks = position & (lanes - 1)
    turned = [jnp.take_along_axis(piece, picks, axis=1, mode="promise_in_bounds") for piece in pieces]
    return joined(turned, lambda limit: position < limit)


def joined(turned, below):
    lanes = turned[0].shape[-1]
    near = [below((k + 1) * lanes) for k in range(len(turned))]
    result = []
    for number in range(len(turned)):
        value = jnp.zeros_like(turned[0])
        for ahead in reversed(range(len(turned) - number)):
            value = jnp.where(near[ahead], turned[number + ahead], value)
        result.append(value)
    return result


def trial_kernel(place_ref, widths_ref, x_ref, out_ref, first, even, odd, series, prefix):
    total, samples = out_ref.shape[2], x_ref.shape[3]
    tiles = total // LANE_ROWS
    tile_bits = tiles.bit_length() - 1
    lanes = prefix.shape[2]
    parts = samples // lanes
    pitch = first.shape[1] // LANE_ROWS
    block = place_ref[0]
    bands = x_ref.shape[2]
    fold = folds(total, samples)
    half_bands = bands // 2
    sources = x_ref.shape[1]
    for number in range(sources):
        high, start = divmod(number * bands, tiles)
        start += reverse_bits(high, LANE_ROWS.bit_length() - 1) * pitch
        for part in range(parts):
            cut = slice(part * lanes, (part + 1) * lanes)
            if fold and 2 * number >= sources:
                first[part, start:start + half_bands] = x_ref[0, number, :half_bands, cut].astype(jnp.float32)
                first[part, start + half_bands:start + bands] = jnp.zeros((half_bands, lanes), jnp.float32)
            else:
                first[part, start:start + bands] = x_ref[0, number, :, cut].astype(jnp.float32)
    for tile in range(tiles):
        spot = tile
        if fold:
            band = tile % bands
            spot = tile - band + (band % 2) * half_bands + band // 2
        for part in range(parts):
            even[reverse_bits(tile, tile_bits), :, part * lanes:(part + 1) * lanes] = first[
                part, pl.ds(spot, LANE_ROWS, stride=pitch)
            ]

    source, target = even, odd
    count = 1
    while count < tiles:
        half = tiles // count // 2

        def merge(j, source=source, target=target, count=count, half=half):
            flat = (half * LANE_ROWS, lanes)
            cut = [slice(part * lanes, (part + 1) * lanes) for part in range(parts)]
            low = [source[pl.ds(j * 2 * half, half), :, c].reshape(flat) for c in cut]
            high = [source[pl.ds(j * 2 * half + half, half), :, c].reshape(flat) for c in cut]
            for side in range(2):
                moved = advanced(high, block * count + j + side)
                for c, base, extra in zip(cut, low, moved):
                    target[pl.ds((2 * j + side) * half, half), :, c] = (base + extra).reshape(
                        half, LANE_ROWS, lanes
                    )

        if count <= 16:
            for j in range(count):
                merge(j)
        else:
            def step(i, carry, merge=merge):
                for k in range(32):
                    merge(i * 32 + k)
                return carry
            lax.fori_loop(0, count // 32, step, 0)
        source, target = target, source
        count = count * 2

    spot = lax.broadcasted_iota(jnp.int32, (LANE_ROWS, lanes), 0)
    bits = [spot >> 2 & 1, spot >> 1 & 1, spot & 1]
    clear = [bit == 0 for bit in bits]

    def final_rows(j):
        pieces = [source[j, :, part * lanes:(part + 1) * lanes] for part in range(parts)]
        row = spot * 0 + (block * tiles + j)
        for level, reach in enumerate((4, 2, 1)):
            low, high = [], []
            for piece in pieces:
                down = pltpu.roll(piece, reach, 0)
                up = down if 2 * reach == LANE_ROWS else pltpu.roll(piece, LANE_ROWS - reach, 0)
                low.append(jnp.where(clear[level], piece, down))
                high.append(jnp.where(clear[level], up, piece))
            moved = advanced_rows(high, row + bits[level])
            pieces = [base + extra for base, extra in zip(low, moved)]
            row = 2 * row + bits[level]
        return jnp.concatenate(pieces, axis=1)

    def finish(i, carry):
        for k in range(16):
            pair = i * 16 + k
            rows = jnp.concatenate([final_rows(2 * pair), final_rows(2 * pair + 1)], axis=0)
            coarse = rows.astype(jnp.bfloat16)
            place = pl.ds(pl.multiple_of(pair * 16, 16), 16)
            series[place, :samples] = coarse
            series[place, samples:] = (rows - coarse.astype(jnp.float32)).astype(jnp.bfloat16)
        return carry

    lax.fori_loop(0, tiles // 32, finish, 0)

    until = lax.broadcasted_iota(jnp.int32, (samples, 2 * samples), 0)
    time = lax.broadcasted_iota(jnp.int32, (samples, 2 * samples), 1) & (samples - 1)
    ladder = jnp.where(time <= until, 1.0, 0.0).astype(jnp.bfloat16)
    margin = prefix.shape[1] - samples - LANE_ROWS
    piece = 2 * lanes
    for part in range(total // piece):
        sums = lax.dot_general(
            ladder, series[part * piece:(part + 1) * piece], (((1,), (1,)), ((), ())),
            preferred_element_type=jnp.float32,
        )
        for side in range(2):
            column = 2 * part + side
            prefix[column, :LANE_ROWS] = jnp.zeros((LANE_ROWS, lanes), jnp.float32)
            prefix[column, LANE_ROWS:LANE_ROWS + samples] = sums[:, side * lanes:(side + 1) * lanes]
            prefix[column, LANE_ROWS + samples:] = jnp.full((margin, lanes), -jnp.inf, jnp.float32)
    for column in range(total // lanes):
        best = None
        for number in range(widths_ref.shape[0]):
            width = widths_ref[number]
            sums = (
                prefix[column, pl.ds(LANE_ROWS - 1 + width, samples)]
                - prefix[column, LANE_ROWS - 1:LANE_ROWS - 1 + samples]
            )
            norm = lax.rsqrt(jnp.full((1, lanes), width * CHANS, jnp.int32).astype(jnp.float32))
            peak = jnp.max(sums, axis=0, keepdims=True) * norm
            best = peak if best is None else jnp.maximum(best, peak)
        out_ref[0, :, column * lanes:(column + 1) * lanes] = best


def trial_peaks(rows, box_widths, place):
    beams, devices, bands, samples = rows.shape
    total = devices * bands
    tiles = total // LANE_ROWS
    return pl.pallas_call(
        trial_kernel,
        grid_spec=pltpu.PrefetchScalarGridSpec(
            num_scalar_prefetch=2,
            grid=(beams,),
            in_specs=[pl.BlockSpec((1, devices, bands, samples), lambda b, p, w: (b, 0, 0, 0))],
            out_specs=pl.BlockSpec((1, 1, total), lambda b, p, w: (b, 0, 0)),
            scratch_shapes=[
                pltpu.VMEM((samples // LANES, total + LANE_ROWS * LANE_ROWS, LANES), jnp.float32),
                pltpu.VMEM((tiles, LANE_ROWS, samples), jnp.float32),
                pltpu.VMEM((tiles, LANE_ROWS, samples), jnp.float32),
                pltpu.VMEM((total, 2 * samples), jnp.bfloat16),
                pltpu.VMEM((total // LANES, LANE_ROWS + samples + WIDEST, LANES), jnp.float32),
            ],
        ),
        out_shape=jax.ShapeDtypeStruct((beams, 1, total), jnp.float32),
    )(place, box_widths, rows)[:, 0]


def compact(samples, devices, blocks, groups, beams, width):
    return (
        samples == 2 * LANES and NDM == 16 * samples and blocks == 4 and beams == groups
        and devices * LANE_ROWS == samples and width * devices == CHANS
    )


def block_span(block):
    return ((0, 4), (0, 4), (1, 4), (1, 4))[block]


def late_span(place, whole):
    return (0, 8) if place < whole else (4, 8)


def band_mask(depth, width):
    rows = LANE_ROWS * (2 << depth)
    row = lax.broadcasted_iota(jnp.int32, (rows, width), 0)
    channel = lax.broadcasted_iota(jnp.int32, (rows, width), 1)
    inner, tile = row % LANE_ROWS, row // LANE_ROWS
    if depth == 0:
        wanted = inner * 2 + tile
    else:
        quarter = tile % 4
        band = inner * 4 + (quarter % 2) * 2 + quarter // 2
        wanted = band * (rows // (4 * LANE_ROWS)) + tile // 4
    return channel // (width // rows) == wanted


def stepped(pair, amount):
    if amount == 0:
        return list(pair)
    lane = lane_index(pair[1].shape)
    near = lane < LANES - amount
    turned = [None if piece is None else pltpu.roll(piece, LANES - amount, 1) for piece in pair]
    early = None if turned[0] is None else jnp.where(near, turned[0], turned[1])
    return [early, jnp.where(near, turned[1], 0.0)]


def plus(low, high):
    return [a + b for a, b in zip(low, high)]


def near_leaves(tiles):
    wide = [plus(tiles[0], tiles[2]), plus(tiles[1], tiles[3])] if len(tiles) == 4 else tiles
    return plus_late(wide) + plus(wide[0], wide[1])


def plus_late(pair):
    return plus(pair[0], stepped(pair[1], 1))


def double_leaves(tiles):
    pairs = [plus_late([tiles[a], tiles[2 + a]]) for a in range(2)]
    return [pair[part] for part in range(2) for pair in pairs]


def far_leaves(tiles):
    parts = [tiles[at:at + 4] for at in range(0, len(tiles), 4)]
    halves = parts if len(parts) == 2 else [[plus(a, b) for a, b in zip(*parts[at:at + 2])] for at in (0, 2)]
    out = {1: [plus(low, stepped(high, 1)) for low, high in zip(*halves)]}
    if len(parts) == 4:
        one, two = [[plus(a, stepped(b, 1)) for a, b in zip(*parts[at:at + 2])] for at in (0, 2)]
        for block in (2, 3):
            out[block] = [plus(low, stepped(high, block - 1)) for low, high in zip(one, two)]
    return {block: [pair[part] for part in range(2) for pair in pairs] for block, pairs in out.items()}


def search_kernel(
    x_hbm, mask_hbm, widths_hbm, out_ref, x_ref, unit_ref, mask_ref, widths_ref, in_sem, send, send_sem, recv, recv_sem,
    twice, twice_sem, taken, taken_sem, peaks, answered, answer_sem, ready_sem, far, far_sem, relay, relay_sem, onward_sem, first, work, mid, planes, double, lower, series, prefix,
):
    beams, width, samples = x_ref.shape
    blocks, groups = lax.axis_size("freq"), lax.axis_size("beam")
    devices = blocks * groups
    row_total = float(beams * samples)
    my_block = lax.axis_index("freq")
    my_group = lax.axis_index("beam")
    my_place = my_block * groups + my_group
    quarter = groups // 2

    chunks = in_sem.shape[0] - 2
    span = width // chunks
    loads = [
        pltpu.make_async_copy(
            x_hbm.at[:, pl.ds(c * span, span)], x_ref.at[:, pl.ds(c * span, span)], in_sem.at[c]
        )
        for c in range(chunks)
    ]
    mask_load = pltpu.make_async_copy(mask_hbm, mask_ref, in_sem.at[chunks])
    widths_load = pltpu.make_async_copy(widths_hbm, widths_ref, in_sem.at[chunks + 1])
    loads[0].start()
    mask_load.start()
    for load in loads[1:]:
        load.start()
    widths_load.start()

    def signal(semaphore, block, group):
        pl.semaphore_signal(
            semaphore, inc=1, device_id={"freq": block, "beam": group}, device_id_type=pl.DeviceIdType.MESH,
        )

    barrier = pltpu.get_barrier_semaphore()

    @pl.when(my_block == 0)
    def _():
        for block in (3, 1, 2):
            for group in range(groups):
                signal(barrier, block, group)
        for step in range(1, groups):
            signal(barrier, 0, (my_group + step) % groups)

    @pl.when(my_block == 1)
    def _():
        for group in range(groups):
            signal(barrier, 0, group)
        for step in range(1, groups):
            signal(barrier, 1, (my_group + step) % groups)

    @pl.when(my_block >= 2)
    def _():
        pl.semaphore_wait(barrier, groups)
        for group in range(groups):
            signal(ready_sem, 0, group)

    for column in range(prefix.shape[0]):
        prefix[column, :LANE_ROWS] = jnp.zeros((LANE_ROWS, LANES), jnp.float32)
        prefix[column, LANE_ROWS + samples:] = jnp.full((WIDEST, LANES), -jnp.inf, jnp.float32)

    lane = lax.broadcasted_iota(jnp.int32, (LANE_ROWS, LANES), 1)
    inner = lax.broadcasted_iota(jnp.int32, (LANE_ROWS, LANES), 0)
    unit_ref[...] = jnp.ones(unit_ref.shape, jnp.bfloat16)
    means, scales = [], []
    for c in range(chunks):
        loads[c].wait()
        if c == 0:
            mask_load.wait()
        unit = unit_ref[...].astype(jnp.float32)
        totals = []
        for column in range(span // LANES):
            found = [jnp.zeros((LANE_ROWS, LANES), jnp.float32) for _ in range(2)]
            for pair in range(LANES // (2 * LANE_ROWS)):
                at = c * span + column * LANES + pair * 2 * LANE_ROWS
                sums = [jnp.zeros((2 * LANE_ROWS, samples), jnp.float32) for _ in range(2)]
                for b in range(beams):
                    wide = x_ref[b, at:at + 2 * LANE_ROWS].astype(jnp.float32)
                    sums = [sums[0] + wide * unit, sums[1] + wide * wide]
                sums = [jnp.sum(value, axis=1, keepdims=True) for value in sums]
                for half in range(2):
                    spot = lane == inner + (2 * pair + half) * LANE_ROWS
                    cut = slice(half * LANE_ROWS, (half + 1) * LANE_ROWS)
                    found = [have + jnp.where(spot, value[cut], 0.0) for have, value in zip(found, sums)]
            totals.append([jnp.sum(value, axis=0, keepdims=True) for value in found])
        mean = jnp.concatenate([total[0] for total in totals], axis=1) / row_total
        var = jnp.concatenate([total[1] for total in totals], axis=1) / row_total - mean * mean
        place = pl.multiple_of(my_group * width + c * span, span)
        clean = mask_ref[:, pl.ds(place, span)].astype(jnp.float32)
        means.append(mean)
        scales.append(lax.rsqrt(var + epsilon) * clean)
    channel_mean = jnp.concatenate(means, axis=1)
    channel_scale = jnp.concatenate(scales, axis=1)
    coarse = channel_scale.astype(jnp.bfloat16).astype(jnp.float32)
    fine = (channel_scale - coarse).astype(jnp.bfloat16).astype(jnp.float32)
    offset = channel_mean * (coarse + fine)

    def summing(depth):
        chosen = band_mask(depth, width)
        count = chosen.shape[0]
        matrix = jnp.concatenate(
            [jnp.where(chosen, coarse, 0.0), jnp.where(chosen, fine, 0.0)], axis=0
        ).astype(jnp.bfloat16)
        shift = jnp.sum(jnp.where(chosen, offset, 0.0), axis=1, keepdims=True)

        def tiles(slot):
            both = jnp.dot(matrix, x_ref[(my_group + slot) % beams], preferred_element_type=jnp.float32)
            sums = both[:count] + both[count:] - shift
            return [
                [sums[t:t + LANE_ROWS, p * LANES:(p + 1) * LANES] for p in range(2)]
                for t in range(0, count, LANE_ROWS)
            ]

        return tiles

    def message(block, slot, begin, end):
        return pltpu.make_async_remote_copy(
            src_ref=send.at[block, slot, pl.ds(begin, end - begin)],
            dst_ref=recv.at[my_place, pl.ds(begin, end - begin)],
            send_sem=send_sem.at[block, slot],
            recv_sem=recv_sem.at[my_place],
            device_id={"freq": block, "beam": (my_group + slot) % beams},
            device_id_type=pl.DeviceIdType.MESH,
        )

    def near_messages(action, slot, narrow):
        if narrow:
            action(message(0, slot, *block_span(2)))
            return

        @pl.when((my_block == 1) | (slot > 0))
        def _():
            action(message(0, slot, *block_span(0)))

    def double_messages(action, slot):
        def message(begin):
            return pltpu.make_async_remote_copy(
                src_ref=twice.at[slot, pl.ds(begin, 4 - begin)],
                dst_ref=taken.at[my_place, pl.ds(begin, 4 - begin)],
                send_sem=twice_sem.at[slot],
                recv_sem=taken_sem.at[my_place],
                device_id={"freq": 1, "beam": (my_group + slot) % beams},
                device_id_type=pl.DeviceIdType.MESH,
            )

        @pl.when(my_block == 0)
        def _():
            action(message(0))
        if slot > 0:
            @pl.when(my_block == 1)
            def _():
                action(message(2))

    def answer():
        return pltpu.make_async_remote_copy(
            src_ref=peaks, dst_ref=answered, send_sem=answer_sem.at[0], recv_sem=answer_sem.at[1],
            device_id={"freq": 0, "beam": my_group}, device_id_type=pl.DeviceIdType.MESH,
        )

    def near_phase(narrow, begin, end):
        tiles = summing(0 if narrow else 1)
        batch = 4
        for start in range(begin, end, batch):
            slots = range(start, start + batch)
            for slot, summed in [(slot, tiles(slot)) for slot in slots]:
                for number, leaf in enumerate(near_leaves(summed)):
                    if not narrow or number > 0:
                        send[0, slot, number] = leaf.astype(jnp.bfloat16)
                if not narrow:
                    for number, leaf in enumerate(double_leaves(summed)):
                        twice[slot, number] = leaf.astype(jnp.bfloat16)
                if slot == 0 and not narrow:
                    @pl.when(my_block == 0)
                    def _():
                        recv[my_place, :4] = send[0, 0, :4]

                    @pl.when(my_block == 1)
                    def _():
                        taken[my_place] = twice[0]
            if narrow:
                for slot in slots:
                    near_messages(lambda copy: copy.start(), slot, narrow)

    def next_messages(action, slot, low):
        action(message(1, slot, 0 if low else 4, 8))

    def by_half(source, action):
        for half in range(2):
            @pl.when((source * 2 >= quarter) if half else (source * 2 < quarter))
            def _(half=half):
                action(4 * half)

    def passed(row, begin):
        return pltpu.make_async_remote_copy(
            src_ref=far.at[quarter + row, :, pl.ds(begin, 8 - begin)],
            dst_ref=relay.at[row, :, pl.ds(begin, 8 - begin)],
            send_sem=far_sem.at[quarter + row, 0],
            recv_sem=relay_sem.at[row],
            device_id={"freq": 0, "beam": (my_group + quarter) % groups},
            device_id_type=pl.DeviceIdType.MESH,
        )

    def direct(beam, block, begin):
        return pltpu.make_async_remote_copy(
            src_ref=far.at[beam, block - 2, pl.ds(begin, 8 - begin)],
            dst_ref=recv.at[my_place, pl.ds(begin, 8 - begin)],
            send_sem=far_sem.at[beam, block - 2],
            recv_sem=recv_sem.at[my_place],
            device_id={"freq": block, "beam": beam},
            device_id_type=pl.DeviceIdType.MESH,
        )

    def onward(row, block, begin):
        return pltpu.make_async_remote_copy(
            src_ref=relay.at[row, block - 2, pl.ds(begin, 8 - begin)],
            dst_ref=recv.at[my_place - quarter, pl.ds(begin, 8 - begin)],
            send_sem=onward_sem.at[row, block - 2],
            recv_sem=recv_sem.at[my_place - quarter],
            device_id={"freq": block, "beam": quarter + row},
            device_id_type=pl.DeviceIdType.MESH,
        )

    def far_phase(low):
        tiles = summing(3 if low else 2)
        batch = 2
        for begin in range(0, beams, batch):
            slots = range(begin, begin + batch)
            for slot, summed in [(slot, tiles(slot)) for slot in slots]:
                for block, leaves in far_leaves(summed).items():
                    for number, leaf in enumerate(leaves):
                        if block == 1:
                            send[block, slot, number] = leaf.astype(jnp.bfloat16)
                        else:
                            far[(my_group + slot) % beams, block - 2, number] = leaf.astype(jnp.bfloat16)
            if not low:
                for slot in slots:
                    next_messages(lambda copy: copy.start(), slot, low)

    def landed(target, semaphore):
        pltpu.make_async_remote_copy(
            src_ref=target, dst_ref=target, send_sem=send_sem.at[0, 0], recv_sem=semaphore,
            device_id={"freq": my_block, "beam": my_group}, device_id_type=pl.DeviceIdType.MESH,
        ).wait_recv()

    def arrival(place, begin, end):
        landed(recv.at[place, pl.ds(begin, end - begin)], recv_sem.at[place])

    args = (recv, first, work, mid, series)
    pitch = first.shape[1] // LANE_ROWS

    def wide_places(count, numbers_of):
        per = count // LANE_ROWS
        return [
            ((place // per) * pitch + (place % per) * (pitch - LANE_ROWS) // per + address, place, numbers)
            for place in range(count) for address, numbers in numbers_of(place)
        ]

    @pl.when(my_block < 2)
    def _():
        near_phase(False, 0, beams)

        @pl.when((my_block == 0) & (my_group < quarter))
        def _():
            far_phase(True)

        pl.semaphore_wait(barrier, 2 * groups - 1)
        for slot in range(beams):
            near_messages(lambda copy: copy.start(), slot, False)
        for slot in range(beams):
            double_messages(lambda copy: copy.start(), slot)

        @pl.when((my_block == 0) & (my_group < quarter))
        def _():
            by_half(my_group, lambda begin: [passed(row, begin).start() for row in range(quarter)])
            for slot in range(beams):
                next_messages(lambda copy: copy.start(), slot, True)

        @pl.when((my_block == 0) & (my_group >= quarter))
        def _():
            far_phase(False)

    @pl.when(my_block >= 2)
    def _():
        near_phase(True, 0, beams)

    widths_load.wait()

    @pl.when(my_block == 0)
    def _():
        for place in range(groups):
            @pl.when(place != my_group)
            def _(place=place):
                arrival(place, *block_span(0))
        for root in range(2):
            plane_rows(recv, first, mid, planes.at[root], 0, groups, root, ((2 - 2 * root, 3 - 2 * root),))

        pl.semaphore_wait(ready_sem, 2 * groups)

        @pl.when(my_group < quarter)
        def _():
            by_half(my_group, lambda begin: [
                direct(beam, block, begin).start() for beam in range(quarter) for block in (3, 2)
            ])

        @pl.when(my_group >= quarter)
        def _():
            def pass_on(begin):
                for row in range(quarter):
                    landed(relay.at[row, :, pl.ds(begin, 8 - begin)], relay_sem.at[row])
                    for block in (3, 2):
                        onward(row, block, begin).start()

            by_half(my_group - quarter, pass_on)

        for place in range(groups, 2 * groups):
            arrival(place, *block_span(1))
        for root in range(2):
            plane_rows(recv, first, mid, planes.at[root], 1, groups, root, ((2 - 2 * root, 3 - 2 * root),))
        for root in range(2):
            lower_rows(planes.at[root], lower.at[root], root)
        for plane in range(2, blocks):
            for place in range(plane * groups, (plane + 1) * groups):
                arrival(place, *block_span(2))
            for root in range(2):
                numbers = ((2, 3) if root == 0 else (None, 1),)
                plane_rows(recv, first, mid, planes.at[root], plane, groups, root, numbers)
        for root in range(2):
            upper_rows(planes.at[root], lower.at[root], series, 256 * (1 + root), root)
        result = boxcar_rows(widths_ref, series, prefix, 2, 4)
        unfolded(result[:2], out_ref, 0)
        unfolded(result[2:], out_ref, 256)
        landed(answered, answer_sem.at[1])
        unpermuted([answered[column] for column in range(2)], out_ref, 512, 1, 4)

    @pl.when(my_block == 1)
    def _():
        for place in range(groups):
            landed(taken.at[place], taken_sem.at[place])
        plane_rows(taken, first, mid, double, 0, groups, 1, ((0, 2), (1, 3)))
        for place in range(groups, 2 * groups):
            @pl.when(place != my_place)
            def _(place=place):
                landed(taken.at[place, pl.ds(2, 2)], taken_sem.at[place])
        plane_rows(taken, first, mid, double, 1, groups, 1, ((None, 2), (None, 3)))
        double_rows(double, series, 256)
        for number, column in enumerate(boxcar_rows(widths_ref, series, prefix, 2, 2)):
            peaks[number] = column
        answer().start()
        for place in range(groups):
            arrival(place, *late_span(place, quarter))
        unit_rows(*args, 0, 1, 256, 2, wide_places(
            groups,
            lambda place: [
                (8 * (2 * (q % 2) + q // 2), (q if place < quarter else None, 4 + q)) for q in range(4)
            ],
        ))
        unpermuted(boxcar_rows(widths_ref, series, prefix, 0, 2), out_ref, 0, 2, 3)
        answer().wait_send()

    for late in (2, 3):
        @pl.when(my_block == late)
        def _(late=late):
            found = []
            for place in range(quarter):
                arrival(place, *late_span(place, quarter // 2))
                for q in range(4):
                    found.append((
                        (2 * (q % 2) + q // 2) * pitch + place * LANE_ROWS, place,
                        (q if 2 * place < quarter else None, 4 + q),
                    ))
            unit_rows(*args, 0, late, 128, 2, found)
            unpermuted(boxcar_rows(widths_ref, series, prefix, 0, 1), out_ref, 0, 3, 3)

    for slot in range(beams):
        for narrow in (True, False):
            @pl.when((my_block >= 2) == narrow)
            def _(narrow=narrow, slot=slot):
                near_messages(lambda copy: copy.wait_send(), slot, narrow)
                if not narrow:
                    double_messages(lambda copy: copy.wait_send(), slot)
        for low in (True, False):
            @pl.when((my_block == 0) & ((my_group < quarter) == low))
            def _(low=low, slot=slot):
                next_messages(lambda copy: copy.wait_send(), slot, low)

    @pl.when((my_block == 0) & (my_group < quarter))
    def _():
        by_half(my_group, lambda begin: [passed(row, begin).wait_send() for row in range(quarter)])
        by_half(my_group, lambda begin: [
            direct(beam, block, begin).wait_send() for beam in range(quarter) for block in (3, 2)
        ])

    @pl.when((my_block == 0) & (my_group >= quarter))
    def _():
        by_half(my_group - quarter, lambda begin: [
            onward(row, block, begin).wait_send() for row in range(quarter) for block in (3, 2)
        ])


def search(intensity, channel_mask, box_widths):
    beams, width, samples = intensity.shape
    blocks, groups = lax.axis_size("freq"), lax.axis_size("beam")
    devices = blocks * groups
    operands = (intensity, channel_mask.reshape(1, -1), box_widths)
    return pl.pallas_call(
        search_kernel,
        in_specs=[pl.BlockSpec(memory_space=pl.ANY)] * 3,
        out_specs=pl.BlockSpec(memory_space=pltpu.VMEM),
        scratch_shapes=[
            pltpu.VMEM((beams, width, samples), jnp.bfloat16),
            pltpu.VMEM((2 * LANE_ROWS, samples), jnp.bfloat16),
            pltpu.VMEM((1, width * groups), jnp.int32),
            pltpu.SMEM(box_widths.shape, jnp.int32),
            pltpu.SemaphoreType.DMA((6,)),
            pltpu.VMEM((2, beams, 8, LANE_ROWS, LANES), jnp.bfloat16),
            pltpu.SemaphoreType.DMA((2, beams)),
            pltpu.VMEM((devices, 8, LANE_ROWS, LANES), jnp.bfloat16),
            pltpu.SemaphoreType.DMA((devices,)),
            pltpu.VMEM((beams, 4, LANE_ROWS, LANES), jnp.bfloat16),
            pltpu.SemaphoreType.DMA((beams,)),
            pltpu.VMEM((2 * groups, 4, LANE_ROWS, LANES), jnp.bfloat16),
            pltpu.SemaphoreType.DMA((2 * groups,)),
            pltpu.VMEM((2, LANE_ROWS, LANES), jnp.float32),
            pltpu.VMEM((2, LANE_ROWS, LANES), jnp.float32),
            pltpu.SemaphoreType.DMA((2,)),
            pltpu.SemaphoreType.REGULAR,
            pltpu.VMEM((beams, 2, 8, LANE_ROWS, LANES), jnp.bfloat16),
            pltpu.SemaphoreType.DMA((beams, 2)),
            pltpu.VMEM((groups // 2, 2, 8, LANE_ROWS, LANES), jnp.bfloat16),
            pltpu.SemaphoreType.DMA((groups // 2,)),
            pltpu.SemaphoreType.DMA((groups // 2, 2)),
            pltpu.VMEM((2, samples + LANE_ROWS * LANE_ROWS, LANES), jnp.float32),
            pltpu.VMEM((2, samples, LANES), jnp.float32),
            pltpu.VMEM((2, samples, LANES), jnp.float32),
            pltpu.VMEM((2, blocks, 2, LANE_ROWS * LANE_ROWS, LANES), jnp.float32),
            pltpu.VMEM((2, 2, LANES, LANES), jnp.float32),
            pltpu.VMEM((2, 2, LANES, LANES), jnp.float32),
            pltpu.VMEM((3 * samples, 2 * samples), jnp.bfloat16),
            pltpu.VMEM((6, LANE_ROWS + samples + WIDEST, LANES), jnp.float32),
        ],
        out_shape=jax.ShapeDtypeStruct((1, NDM // blocks), jnp.float32),
        compiler_params=pltpu.CompilerParams(collective_id=0, has_side_effects=True, vmem_limit_bytes=32 << 20),
    )(*[pltpu.with_memory_space_constraint(value, pltpu.HBM) for value in operands])


def ramped(pair, start, stride, far, only_late=False):
    shape = pair[1].shape
    place = lane_index(shape) + (lax.broadcasted_iota(jnp.int32, shape, 0) * stride + start)
    picks = place & (LANES - 1)
    late = jnp.take_along_axis(pair[1], picks, axis=1, mode="promise_in_bounds")
    if far:
        return [jnp.where(place < 2 * LANES, late, 0.0), None]
    near = place < LANES
    moved = [None, jnp.where(near, late, 0.0)]
    if not only_late:
        early = jnp.take_along_axis(pair[0], picks, axis=1, mode="promise_in_bounds")
        moved[0] = jnp.where(near, early, late)
    return moved


def joined_pair(low, high):
    return [a if b is None else (None if a is None else a + b) for a, b in zip(low, high)]


def unit_rows(recv, first, work, mid, series, base, root, leaves, kinds, found):
    tiles = leaves // LANE_ROWS
    pitch = first.shape[1] // LANE_ROWS
    for address, place, numbers in found:
        for part in range(2):
            if numbers[part] is not None:
                first[part, address:address + LANE_ROWS] = recv[place, numbers[part]].astype(jnp.float32)

    def leaf(tile, part):
        outer, kind = tile >> kinds, tile & ((1 << kinds) - 1)
        if leaves == LANE_ROWS * (pitch - LANE_ROWS):
            spot, step = ((outer >> 3 << kinds) + kind) * LANE_ROWS + (outer & 7), pitch
        else:
            spot, step = kind * pitch + outer, LANE_ROWS // 2
        return first[part, pl.ds(spot, LANE_ROWS, stride=step)]

    chunk = 8
    for c in range(tiles // chunk):
        tree = [[[leaf(c * chunk + k, part) for part in range(2)]] for k in range(chunk)]
        level_root = root
        while len(tree) > 1:
            tree = [
                [
                    plus(low[r // 2], stepped(high[r // 2], level_root + r // 2 + r % 2))
                    for r in range(2 * len(low))
                ]
                for low, high in zip(tree[0::2], tree[1::2])
            ]
            level_root = level_root * 2
        for j in range(chunk):
            for part in range(2):
                at = (j * (tiles // chunk) + c) * LANE_ROWS
                work[part, at:at + LANE_ROWS] = tree[0][j][part]
    chunks = tiles // chunk
    for j in range(chunk):
        tree = []
        for c in range(chunks):
            at = (j * chunks + c) * LANE_ROWS
            tree.append([[work[part, at:at + LANE_ROWS] for part in range(2)]])
        level_root = root * chunk + j
        while len(tree) > 1:
            tree = [
                [
                    plus(low[r // 2], stepped(high[r // 2], level_root + r // 2 + r % 2))
                    for r in range(2 * len(low))
                ]
                for low, high in zip(tree[0::2], tree[1::2])
            ]
            level_root = level_root * 2
        for k in range(chunks):
            for part in range(2):
                at = (j * chunks + k) * LANE_ROWS
                mid[part, at:at + LANE_ROWS] = tree[0][k][part]
    far = root > 0
    for g in range(tiles // LANE_ROWS):
        tree = []
        for s in range(LANE_ROWS):
            pair = [
                None if far and 2 * s >= LANE_ROWS and part == 0
                else mid[part, pl.ds(g * LANE_ROWS * LANE_ROWS + s, LANE_ROWS, stride=LANE_ROWS)]
                for part in range(2)
            ]
            tree.append([pair])
        rows = merged_rows(tree, root * tiles + g * LANE_ROWS, 1, far)
        for k in range(0, LANE_ROWS, 2):
            save_series(series, base + g * LANE_ROWS * LANE_ROWS + k * LANE_ROWS, rows[k:k + 2])


def merged_rows(tree, start, stride, far):
    while len(tree) > 1:
        tree = [
            [
                joined_pair(
                    low[r // 2],
                    ramped(
                        high[r // 2], start + r // 2 + r % 2, stride, far and len(tree) == 2,
                        high[r // 2][0] is None,
                    ),
                )
                for r in range(2 * len(low))
            ]
            for low, high in zip(tree[0::2], tree[1::2])
        ]
        start, stride = start * 2, stride * 2
    return tree[0]


def plane_rows(recv, first, mid, target, plane, groups, root, numbers):
    kinds = len(numbers)
    origin = (2 * (kinds - 1) + root * (2 - kinds)) * LANE_ROWS * LANE_ROWS
    parts = [part for part in range(2) if numbers[0][part] is not None]
    flat = LANE_ROWS * LANE_ROWS
    for place in range(groups):
        for kind in range(kinds):
            for part in parts:
                at = origin + kind * flat + place * LANE_ROWS
                first[part, at:at + LANE_ROWS] = recv[plane * groups + place, numbers[kind][part]].astype(jnp.float32)

    def pair_at(source, start):
        return [source[part, pl.ds(start, LANE_ROWS, stride=LANE_ROWS)] if part in parts else None for part in range(2)]

    tree = [[pair_at(first, origin + (tile % kinds) * flat + tile // kinds)] for tile in range(kinds * LANE_ROWS)]
    level_root = root
    while len(tree) > 1:
        tree = [
            [
                joined_pair(low[r // 2], stepped(high[r // 2], level_root + r // 2 + r % 2))
                for r in range(2 * len(low))
            ]
            for low, high in zip(tree[0::2], tree[1::2])
        ]
        level_root = level_root * 2
    for j, pair in enumerate(tree[0]):
        for part in parts:
            at = origin + j * LANE_ROWS
            mid[part, at:at + LANE_ROWS] = pair[part]
    for g in range(kinds):
        tree = [[pair_at(mid, origin + g * flat + p)] for p in range(LANE_ROWS)]
        for k, pair in enumerate(merged_rows(tree, (root * kinds + g) * LANE_ROWS, 1, False)):
            at = g * flat + k * LANE_ROWS
            for part in parts:
                target[plane, part, at:at + LANE_ROWS] = pair[part]


def double_rows(target, series, base):
    for g in range(2):
        for k in range(LANE_ROWS):
            number = g * LANE_ROWS + k
            tree = [[plane_tile(target, 0, number, (0, 1))], [plane_tile(target, 1, number, (1,))]]
            rows = merged_rows(tree, LANES + g * LANE_ROWS * LANE_ROWS + k, LANE_ROWS, True)
            save_series(series, base + 2 * number * LANE_ROWS, rows)


def plane_tile(target, plane, k, parts):
    return [
        target[plane, part, k * LANE_ROWS:(k + 1) * LANE_ROWS] if part in parts else None for part in range(2)
    ]


def lower_rows(target, lower, root):
    for k in range(LANE_ROWS):
        tree = [[plane_tile(target, plane, k, (0, 1))] for plane in range(2)]
        for q, pair in enumerate(merged_rows(tree, root * LANE_ROWS * LANE_ROWS + k, LANE_ROWS, False)):
            for part in range(2):
                at = (2 * k + q) * LANE_ROWS
                lower[part, at:at + LANE_ROWS] = pair[part]


def upper_rows(target, lower, series, base, root):
    parts = (0, 1) if root == 0 else (1,)
    for k in range(LANE_ROWS):
        begin = root * LANE_ROWS * LANE_ROWS + k
        high = merged_rows([[plane_tile(target, plane, k, parts)] for plane in (2, 3)], begin, LANE_ROWS, False)
        low = []
        for q in range(2):
            at = (2 * k + q) * LANE_ROWS
            low.append([lower[part, at:at + LANE_ROWS] for part in range(2)])
        rows = merged_rows([low, high], begin * 2, 2 * LANE_ROWS, root > 0)
        for number in range(0, 4, 2):
            save_series(series, base + (4 * k + number) * LANE_ROWS, rows[number:number + 2])


def save_series(series, at, pairs):
    rows = jnp.concatenate([jnp.concatenate(pair, axis=1) for pair in pairs], axis=0)
    coarse = rows.astype(jnp.bfloat16)
    samples = rows.shape[1]
    series[at:at + 2 * LANE_ROWS, :samples] = coarse
    series[at:at + 2 * LANE_ROWS, samples:] = (rows - coarse.astype(jnp.float32)).astype(jnp.bfloat16)


def unfolded(columns, out_ref, offset):
    lane = lane_index((LANE_ROWS, LANES))
    for number in range(2):
        picks = (lane & 15) * LANE_ROWS + (lane >> 5) + 4 * number
        spread = [jnp.take_along_axis(column, picks, axis=1, mode="promise_in_bounds") for column in columns]
        at = offset + number * LANES
        out_ref[:, at:at + LANES] = jnp.where(lane & 16 == 0, spread[0], spread[1])[:1]


def boxcar_rows(widths_ref, series, prefix, begin, count):
    lanes = prefix.shape[2]
    samples = series.shape[1] // 2
    until = lax.broadcasted_iota(jnp.int32, (samples, 2 * samples), 0)
    time = lax.broadcasted_iota(jnp.int32, (samples, 2 * samples), 1) & (samples - 1)
    ladder = jnp.where(time <= until, 1.0, 0.0).astype(jnp.bfloat16)
    piece = min(2, count)
    for start in range(begin, begin + count, piece):
        sums = lax.dot_general(
            ladder, series[start * lanes:(start + piece) * lanes], (((1,), (1,)), ((), ())),
            preferred_element_type=jnp.float32,
        )
        for side in range(piece):
            prefix[start + side, LANE_ROWS:LANE_ROWS + samples] = sums[:, side * lanes:(side + 1) * lanes]
    widths = [widths_ref[number] for number in range(widths_ref.shape[0])]
    norms = [
        lax.rsqrt(jnp.full((LANE_ROWS, lanes), width * CHANS, jnp.int32).astype(jnp.float32)) for width in widths
    ]
    result = []
    for column in range(begin, begin + count):
        ahead = [prefix[column, pl.ds(LANE_ROWS - 1 + width, samples)] for width in widths]
        base = prefix[column, LANE_ROWS - 1:LANE_ROWS - 1 + samples]
        best = [None] * len(widths)
        for at in range(0, samples, LANE_ROWS):
            before = base[at:at + LANE_ROWS]
            for number, after in enumerate(ahead):
                gain = after[at:at + LANE_ROWS] - before
                best[number] = gain if at == 0 else jnp.maximum(best[number], gain)
        peak = best[0] * norms[0]
        for value, norm in zip(best[1:], norms[1:]):
            peak = jnp.maximum(peak, value * norm)
        result.append(jnp.broadcast_to(jnp.max(peak, axis=0, keepdims=True), (LANE_ROWS, lanes)))
    return result


def unpermuted(columns, out_ref, offset, repeat_bits, bits):
    lane = lane_index((LANE_ROWS, LANES))
    for number in range(len(columns) << repeat_bits):
        row = (lane + number * LANES) >> repeat_bits
        row = row & (LANES - 1)
        block = LANE_ROWS << bits
        picks = (row & (LANES - block)) + (row & ((1 << bits) - 1)) * LANE_ROWS + ((row & (block - 1)) >> bits)
        column = columns[number >> repeat_bits]
        spread = jnp.take_along_axis(column, picks, axis=1, mode="promise_in_bounds")
        at = offset + number * LANES
        out_ref[:, at:at + LANES] = spread[:1]


def shards(intensity, channel_mask, box_widths):
    beams, width, samples = intensity.shape
    blocks, groups = lax.axis_size("freq"), lax.axis_size("beam")
    if compact(samples, blocks * groups, blocks, groups, beams, width):
        return search(intensity, channel_mask, box_widths)
    rows = entry_rows(intensity, channel_mask)
    return trial_peaks(rows, box_widths, lax.axis_index("freq").reshape(1))


def solution(mesh):
    in_specs = (P(None, ("freq", "beam"), None), P("freq"), P())
    out_specs = P("beam", "freq")
    return jax.shard_map(shards, mesh=mesh, in_specs=in_specs, out_specs=out_specs, check_vma=False)
```

```python
import jax
import jax.numpy as jnp
from jax import lax
from jax.experimental import pallas as pl
from jax.experimental.pallas import tpu as pltpu
from jax.sharding import PartitionSpec as P

CHANS = 16384
NDM = 4096
LANE_ROWS = 8
LANES = 128
WIDEST = 64

epsilon = 1e-05


def reverse_bits(number, count):
    result = 0
    for _ in range(count):
        result = result << 1 | number & 1
        number >>= 1
    return result


def lane_index(shape):
    return lax.broadcasted_iota(jnp.int32, shape, len(shape) - 1)


def earlier(block, amount):
    if amount == 0:
        return block
    samples = block.shape[-1]
    return jnp.where(lane_index(block.shape) < samples - amount, pltpu.roll(block, samples - amount, 1), 0.0)


def folds(trial_dev, samples):
    return trial_dev >= 4 * samples


def channel_limits(trial_dev, blocks, samples):
    limits = []
    for block in range(blocks):
        limit, rows = CHANS, NDM
        while (block * trial_dev * rows // NDM + 1) // 2 >= samples:
            limit, rows = limit // 2, rows // 2
        limits.append(limit)
    return limits


def entry_kernel(x_hbm, mask_ref, out_ref, x_ref, in_sem, send, send_sem, recv_sem, own_sem):
    blocks, beams, bands, samples = send.shape
    groups = lax.axis_size("beam")
    beam_dev = beams // groups
    width = x_ref.shape[1]
    group = width // (bands * blocks)
    trial_dev = NDM // blocks
    row_total = float(beams * samples)
    fold = folds(trial_dev, samples)
    limits = channel_limits(trial_dev, blocks, samples)
    my_block = lax.axis_index("freq")
    my_group = lax.axis_index("beam")
    my_place = my_block * groups + my_group
    devices = blocks * groups

    barrier = pltpu.get_barrier_semaphore()
    for step in range(1, devices):
        peer = (my_place + step) % devices
        pl.semaphore_signal(
            barrier, inc=1, device_id={"freq": peer // groups, "beam": peer % groups},
            device_id_type=pl.DeviceIdType.MESH,
        )

    chunks = in_sem.shape[0]
    span = width // chunks
    loads = [
        pltpu.make_async_copy(
            x_hbm.at[:, pl.ds(c * span, span)], x_ref.at[:, pl.ds(c * span, span)], in_sem.at[c]
        )
        for c in range(chunks)
    ]
    for load in loads:
        load.start()
    means, scales = [], []
    for c in range(chunks):
        loads[c].wait()
        total = jnp.zeros((span, samples), jnp.float32)
        squares = jnp.zeros((span, samples), jnp.float32)
        for beam in range(beams):
            wide = x_ref[beam, c * span:(c + 1) * span].astype(jnp.float32)
            total = total + wide
            squares = squares + wide * wide
        mean = jnp.sum(total, axis=1, keepdims=True) / row_total
        var = jnp.sum(squares, axis=1, keepdims=True) / row_total - mean * mean
        means.append(mean)
        scales.append(lax.rsqrt(var + epsilon))
    channel_mean = jnp.concatenate(means, axis=0)
    channel_scale = jnp.concatenate(scales, axis=0)
    out_row = lax.broadcasted_iota(jnp.int32, (blocks * bands, width), 0)
    channel = lax.broadcasted_iota(jnp.int32, (blocks * bands, width), 1)
    band = out_row % bands
    if fold:
        half = bands // 2
        band = (band % half) * 2 + band // half
    wanted = band * blocks + out_row // bands
    clean = mask_ref[:, pl.ds(pl.multiple_of(my_group * width, width), width)].astype(jnp.float32)
    chosen = jnp.where(channel // group == wanted, clean, 0.0).astype(jnp.bfloat16)
    upper = my_block * 2 >= blocks

    def message(block, slot, beam, rows):
        return pltpu.make_async_remote_copy(
            src_ref=send.at[block, slot, pl.ds(0, rows)],
            dst_ref=out_ref.at[beam % beam_dev, my_place, pl.ds(0, rows)],
            send_sem=send_sem.at[block, slot],
            recv_sem=recv_sem.at[beam % beam_dev, my_place],
            device_id={"freq": block, "beam": beam // beam_dev},
            device_id_type=pl.DeviceIdType.MESH,
        )

    def own_copy(slot, part):
        return pltpu.make_async_copy(
            send.at[my_block, slot], out_ref.at[part, my_place], own_sem.at[part]
        )

    def every_message(action, slot):
        beam = (my_group * beam_dev + slot) % beams
        for block in range(blocks):
            goes = my_place * width < limits[block]
            if slot < beam_dev:
                goes = goes & (my_block != block)
            if fold:
                @pl.when(goes & upper)
                def _(block=block):
                    action(message(block, slot, beam, bands // 2))
                goes = goes & jnp.logical_not(upper)

            @pl.when(goes)
            def _(block=block):
                action(message(block, slot, beam, bands))

    for slot in range(beams):
        beam = (my_group * beam_dev + slot) % beams
        wide = x_ref[beam].astype(jnp.float32)
        normed = ((wide - channel_mean) * channel_scale).astype(jnp.bfloat16)
        sums = jnp.dot(chosen, normed, preferred_element_type=jnp.float32)
        tree = [[sums[i * bands:(i + 1) * bands]] for i in range(blocks)]
        while len(tree) > 1:
            merged = []
            for low, high in zip(tree[0::2], tree[1::2]):
                merged.append(
                    [low[m // 2] + earlier(high[m // 2], (m + 1) // 2) for m in range(2 * len(low))]
                )
            tree = merged
        for number, row in enumerate(tree[0]):
            if fold:
                both = row[:half] + row[half:]
                row = jnp.concatenate([jnp.where(upper, both, row[:half]), row[half:]], axis=0)
            send[number, slot] = row.astype(jnp.bfloat16)
        if slot == 0:
            pl.semaphore_wait(barrier, devices - 1)
        every_message(lambda copy: copy.start(), slot)
        if slot < beam_dev:
            own_copy(slot, slot).start()

    for slot in range(beam_dev):
        own_copy(slot, slot).wait()
    limit = sum(jnp.where(my_block == block, limits[block], 0) for block in range(blocks))
    for place in range(devices):
        for part in range(beam_dev):
            rows = bands // 2 if fold and 2 * place >= devices else bands
            target = out_ref.at[part, place, pl.ds(0, rows)]
            @pl.when((place * width < limit) & (place != my_place))
            def _(target=target, place=place, part=part):
                pltpu.make_async_remote_copy(
                    src_ref=target, dst_ref=target, send_sem=send_sem.at[0, 0],
                    recv_sem=recv_sem.at[part, place],
                    device_id={"freq": my_block, "beam": my_group},
                    device_id_type=pl.DeviceIdType.MESH,
                ).wait_recv()
    for slot in range(beams):
        every_message(lambda copy: copy.wait_send(), slot)


def entry_rows(intensity, channel_mask):
    beams, width, samples = intensity.shape
    blocks, groups = lax.axis_size("freq"), lax.axis_size("beam")
    bands = width * NDM // (CHANS * blocks)
    beam_dev, devices = beams // groups, blocks * groups
    return pl.pallas_call(
        entry_kernel,
        in_specs=[pl.BlockSpec(memory_space=pl.ANY), pl.BlockSpec(memory_space=pltpu.VMEM)],
        out_specs=pl.BlockSpec(memory_space=pl.ANY),
        scratch_shapes=[
            pltpu.VMEM((beams, width, samples), jnp.bfloat16),
            pltpu.SemaphoreType.DMA((4,)),
            pltpu.VMEM((blocks, beams, bands, samples), jnp.bfloat16),
            pltpu.SemaphoreType.DMA((blocks, beams)),
            pltpu.SemaphoreType.DMA((beam_dev, devices)),
            pltpu.SemaphoreType.DMA((beam_dev,)),
        ],
        out_shape=jax.ShapeDtypeStruct((beam_dev, devices, bands, samples), jnp.bfloat16),
        compiler_params=pltpu.CompilerParams(collective_id=0, has_side_effects=True),
    )(intensity, channel_mask.reshape(1, -1))


def advanced(pieces, amount):
    lanes = pieces[0].shape[-1]
    position = lane_index(pieces[0].shape)
    turn = (lanes - amount) & (lanes - 1)
    turned = [pltpu.roll(piece, turn, 1) for piece in pieces]
    return joined(turned, lambda limit: position < limit - amount)


def advanced_rows(pieces, amounts):
    lanes = pieces[0].shape[-1]
    position = lane_index(pieces[0].shape) + amounts
    picks = position & (lanes - 1)
    turned = [jnp.take_along_axis(piece, picks, axis=1, mode="promise_in_bounds") for piece in pieces]
    return joined(turned, lambda limit: position < limit)


def joined(turned, below):
    lanes = turned[0].shape[-1]
    near = [below((k + 1) * lanes) for k in range(len(turned))]
    result = []
    for number in range(len(turned)):
        value = jnp.zeros_like(turned[0])
        for ahead in reversed(range(len(turned) - number)):
            value = jnp.where(near[ahead], turned[number + ahead], value)
        result.append(value)
    return result


def trial_kernel(place_ref, widths_ref, x_ref, out_ref, first, even, odd, series, prefix):
    total, samples = out_ref.shape[2], x_ref.shape[3]
    tiles = total // LANE_ROWS
    tile_bits = tiles.bit_length() - 1
    lanes = prefix.shape[2]
    parts = samples // lanes
    pitch = first.shape[1] // LANE_ROWS
    block = place_ref[0]
    bands = x_ref.shape[2]
    fold = folds(total, samples)
    half_bands = bands // 2
    sources = x_ref.shape[1]
    for number in range(sources):
        high, start = divmod(number * bands, tiles)
        start += reverse_bits(high, LANE_ROWS.bit_length() - 1) * pitch
        for part in range(parts):
            cut = slice(part * lanes, (part + 1) * lanes)
            if fold and 2 * number >= sources:
                first[part, start:start + half_bands] = x_ref[0, number, :half_bands, cut].astype(jnp.float32)
                first[part, start + half_bands:start + bands] = jnp.zeros((half_bands, lanes), jnp.float32)
            else:
                first[part, start:start + bands] = x_ref[0, number, :, cut].astype(jnp.float32)
    for tile in range(tiles):
        spot = tile
        if fold:
            band = tile % bands
            spot = tile - band + (band % 2) * half_bands + band // 2
        for part in range(parts):
            even[reverse_bits(tile, tile_bits), :, part * lanes:(part + 1) * lanes] = first[
                part, pl.ds(spot, LANE_ROWS, stride=pitch)
            ]

    source, target = even, odd
    count = 1
    while count < tiles:
        half = tiles // count // 2

        def merge(j, source=source, target=target, count=count, half=half):
            flat = (half * LANE_ROWS, lanes)
            cut = [slice(part * lanes, (part + 1) * lanes) for part in range(parts)]
            low = [source[pl.ds(j * 2 * half, half), :, c].reshape(flat) for c in cut]
            high = [source[pl.ds(j * 2 * half + half, half), :, c].reshape(flat) for c in cut]
            for side in range(2):
                moved = advanced(high, block * count + j + side)
                for c, base, extra in zip(cut, low, moved):
                    target[pl.ds((2 * j + side) * half, half), :, c] = (base + extra).reshape(
                        half, LANE_ROWS, lanes
                    )

        if count <= 16:
            for j in range(count):
                merge(j)
        else:
            def step(i, carry, merge=merge):
                for k in range(32):
                    merge(i * 32 + k)
                return carry
            lax.fori_loop(0, count // 32, step, 0)
        source, target = target, source
        count = count * 2

    spot = lax.broadcasted_iota(jnp.int32, (LANE_ROWS, lanes), 0)
    bits = [spot >> 2 & 1, spot >> 1 & 1, spot & 1]
    clear = [bit == 0 for bit in bits]

    def final_rows(j):
        pieces = [source[j, :, part * lanes:(part + 1) * lanes] for part in range(parts)]
        row = spot * 0 + (block * tiles + j)
        for level, reach in enumerate((4, 2, 1)):
            low, high = [], []
            for piece in pieces:
                down = pltpu.roll(piece, reach, 0)
                up = down if 2 * reach == LANE_ROWS else pltpu.roll(piece, LANE_ROWS - reach, 0)
                low.append(jnp.where(clear[level], piece, down))
                high.append(jnp.where(clear[level], up, piece))
            moved = advanced_rows(high, row + bits[level])
            pieces = [base + extra for base, extra in zip(low, moved)]
            row = 2 * row + bits[level]
        return jnp.concatenate(pieces, axis=1)

    def finish(i, carry):
        for k in range(16):
            pair = i * 16 + k
            rows = jnp.concatenate([final_rows(2 * pair), final_rows(2 * pair + 1)], axis=0)
            coarse = rows.astype(jnp.bfloat16)
            place = pl.ds(pl.multiple_of(pair * 16, 16), 16)
            series[place, :samples] = coarse
            series[place, samples:] = (rows - coarse.astype(jnp.float32)).astype(jnp.bfloat16)
        return carry

    lax.fori_loop(0, tiles // 32, finish, 0)

    until = lax.broadcasted_iota(jnp.int32, (samples, 2 * samples), 0)
    time = lax.broadcasted_iota(jnp.int32, (samples, 2 * samples), 1) & (samples - 1)
    ladder = jnp.where(time <= until, 1.0, 0.0).astype(jnp.bfloat16)
    margin = prefix.shape[1] - samples - LANE_ROWS
    piece = 2 * lanes
    for part in range(total // piece):
        sums = lax.dot_general(
            ladder, series[part * piece:(part + 1) * piece], (((1,), (1,)), ((), ())),
            preferred_element_type=jnp.float32,
        )
        for side in range(2):
            column = 2 * part + side
            prefix[column, :LANE_ROWS] = jnp.zeros((LANE_ROWS, lanes), jnp.float32)
            prefix[column, LANE_ROWS:LANE_ROWS + samples] = sums[:, side * lanes:(side + 1) * lanes]
            prefix[column, LANE_ROWS + samples:] = jnp.full((margin, lanes), -jnp.inf, jnp.float32)
    for column in range(total // lanes):
        best = None
        for number in range(widths_ref.shape[0]):
            width = widths_ref[number]
            sums = (
                prefix[column, pl.ds(LANE_ROWS - 1 + width, samples)]
                - prefix[column, LANE_ROWS - 1:LANE_ROWS - 1 + samples]
            )
            norm = lax.rsqrt(jnp.full((1, lanes), width * CHANS, jnp.int32).astype(jnp.float32))
            peak = jnp.max(sums, axis=0, keepdims=True) * norm
            best = peak if best is None else jnp.maximum(best, peak)
        out_ref[0, :, column * lanes:(column + 1) * lanes] = best


def trial_peaks(rows, box_widths, place):
    beams, devices, bands, samples = rows.shape
    total = devices * bands
    tiles = total // LANE_ROWS
    return pl.pallas_call(
        trial_kernel,
        grid_spec=pltpu.PrefetchScalarGridSpec(
            num_scalar_prefetch=2,
            grid=(beams,),
            in_specs=[pl.BlockSpec((1, devices, bands, samples), lambda b, p, w: (b, 0, 0, 0))],
            out_specs=pl.BlockSpec((1, 1, total), lambda b, p, w: (b, 0, 0)),
            scratch_shapes=[
                pltpu.VMEM((samples // LANES, total + LANE_ROWS * LANE_ROWS, LANES), jnp.float32),
                pltpu.VMEM((tiles, LANE_ROWS, samples), jnp.float32),
                pltpu.VMEM((tiles, LANE_ROWS, samples), jnp.float32),
                pltpu.VMEM((total, 2 * samples), jnp.bfloat16),
                pltpu.VMEM((total // LANES, LANE_ROWS + samples + WIDEST, LANES), jnp.float32),
            ],
        ),
        out_shape=jax.ShapeDtypeStruct((beams, 1, total), jnp.float32),
    )(place, box_widths, rows)[:, 0]


def compact(samples, devices, blocks, groups, beams, width):
    return (
        samples == 2 * LANES and NDM == 16 * samples and blocks == 4 and beams == groups
        and devices * LANE_ROWS == samples and width * devices == CHANS
    )


def block_span(block):
    return ((0, 4), (0, 4), (1, 4), (1, 4))[block]


def late_span(place, whole):
    return (0, 8) if place < whole else (4, 8)


def band_mask(depth, width):
    rows = LANE_ROWS * (2 << depth)
    row = lax.broadcasted_iota(jnp.int32, (rows, width), 0)
    channel = lax.broadcasted_iota(jnp.int32, (rows, width), 1)
    inner, tile = row % LANE_ROWS, row // LANE_ROWS
    if depth == 0:
        wanted = inner * 2 + tile
    else:
        quarter = tile % 4
        band = inner * 4 + (quarter % 2) * 2 + quarter // 2
        wanted = band * (rows // (4 * LANE_ROWS)) + tile // 4
    return channel // (width // rows) == wanted


def stepped(pair, amount):
    if amount == 0:
        return list(pair)
    lane = lane_index(pair[1].shape)
    near = lane < LANES - amount
    turned = [None if piece is None else pltpu.roll(piece, LANES - amount, 1) for piece in pair]
    early = None if turned[0] is None else jnp.where(near, turned[0], turned[1])
    return [early, jnp.where(near, turned[1], 0.0)]


def plus(low, high):
    return [a + b for a, b in zip(low, high)]


def near_leaves(tiles):
    wide = [plus(tiles[0], tiles[2]), plus(tiles[1], tiles[3])] if len(tiles) == 4 else tiles
    return plus_late(wide) + plus(wide[0], wide[1])


def plus_late(pair):
    return plus(pair[0], stepped(pair[1], 1))


def double_leaves(tiles):
    pairs = [plus_late([tiles[a], tiles[2 + a]]) for a in range(2)]
    return [pair[part] for part in range(2) for pair in pairs]


def far_leaves(tiles):
    parts = [tiles[at:at + 4] for at in range(0, len(tiles), 4)]
    halves = parts if len(parts) == 2 else [[plus(a, b) for a, b in zip(*parts[at:at + 2])] for at in (0, 2)]
    out = {1: [plus(low, stepped(high, 1)) for low, high in zip(*halves)]}
    if len(parts) == 4:
        one, two = [[plus(a, stepped(b, 1)) for a, b in zip(*parts[at:at + 2])] for at in (0, 2)]
        for block in (2, 3):
            out[block] = [plus(low, stepped(high, block - 1)) for low, high in zip(one, two)]
    return {block: [pair[part] for part in range(2) for pair in pairs] for block, pairs in out.items()}


def search_kernel(
    x_hbm, mask_hbm, widths_hbm, out_ref, x_ref, unit_ref, mask_ref, widths_ref, in_sem, send, send_sem, recv, recv_sem,
    twice, twice_sem, taken, taken_sem, peaks, answered, answer_sem, ready_sem, far, far_sem, relay, relay_sem, onward_sem, first, work, mid, planes, double, lower, series, prefix,
):
    beams, width, samples = x_ref.shape
    blocks, groups = lax.axis_size("freq"), lax.axis_size("beam")
    devices = blocks * groups
    row_total = float(beams * samples)
    my_block = lax.axis_index("freq")
    my_group = lax.axis_index("beam")
    my_place = my_block * groups + my_group
    quarter = groups // 2

    chunks = in_sem.shape[0] - 2
    span = width // chunks
    loads = [
        pltpu.make_async_copy(
            x_hbm.at[:, pl.ds(c * span, span)], x_ref.at[:, pl.ds(c * span, span)], in_sem.at[c]
        )
        for c in range(chunks)
    ]
    mask_load = pltpu.make_async_copy(mask_hbm, mask_ref, in_sem.at[chunks])
    widths_load = pltpu.make_async_copy(widths_hbm, widths_ref, in_sem.at[chunks + 1])
    loads[0].start()
    mask_load.start()
    for load in loads[1:]:
        load.start()
    widths_load.start()

    def signal(semaphore, block, group):
        pl.semaphore_signal(
            semaphore, inc=1, device_id={"freq": block, "beam": group}, device_id_type=pl.DeviceIdType.MESH,
        )

    barrier = pltpu.get_barrier_semaphore()

    @pl.when(my_block == 0)
    def _():
        for block in (3, 1, 2):
            for group in range(groups):
                signal(barrier, block, group)
        for step in range(1, groups):
            signal(barrier, 0, (my_group + step) % groups)

    @pl.when(my_block == 1)
    def _():
        for group in range(groups):
            signal(barrier, 0, group)
        for step in range(1, groups):
            signal(barrier, 1, (my_group + step) % groups)

    @pl.when(my_block >= 2)
    def _():
        pl.semaphore_wait(barrier, groups)
        for group in range(groups):
            signal(ready_sem, 0, group)

    for column in range(prefix.shape[0]):
        prefix[column, :LANE_ROWS] = jnp.zeros((LANE_ROWS, LANES), jnp.float32)
        prefix[column, LANE_ROWS + samples:] = jnp.full((WIDEST, LANES), -jnp.inf, jnp.float32)

    lane = lax.broadcasted_iota(jnp.int32, (LANE_ROWS, LANES), 1)
    inner = lax.broadcasted_iota(jnp.int32, (LANE_ROWS, LANES), 0)
    unit_ref[...] = jnp.ones(unit_ref.shape, jnp.bfloat16)
    means, scales = [], []
    for c in range(chunks):
        loads[c].wait()
        if c == 0:
            mask_load.wait()
        unit = unit_ref[...].astype(jnp.float32)
        totals = []
        for column in range(span // LANES):
            found = [jnp.zeros((LANE_ROWS, LANES), jnp.float32) for _ in range(2)]
            for pair in range(LANES // (2 * LANE_ROWS)):
                at = c * span + column * LANES + pair * 2 * LANE_ROWS
                sums = [jnp.zeros((2 * LANE_ROWS, samples), jnp.float32) for _ in range(2)]
                for b in range(beams):
                    wide = x_ref[b, at:at + 2 * LANE_ROWS].astype(jnp.float32)
                    sums = [sums[0] + wide * unit, sums[1] + wide * wide]
                sums = [jnp.sum(value, axis=1, keepdims=True) for value in sums]
                for half in range(2):
                    spot = lane == inner + (2 * pair + half) * LANE_ROWS
                    cut = slice(half * LANE_ROWS, (half + 1) * LANE_ROWS)
                    found = [have + jnp.where(spot, value[cut], 0.0) for have, value in zip(found, sums)]
            totals.append([jnp.sum(value, axis=0, keepdims=True) for value in found])
        mean = jnp.concatenate([total[0] for total in totals], axis=1) / row_total
        var = jnp.concatenate([total[1] for total in totals], axis=1) / row_total - mean * mean
        place = pl.multiple_of(my_group * width + c * span, span)
        clean = mask_ref[:, pl.ds(place, span)].astype(jnp.float32)
        means.append(mean)
        scales.append(lax.rsqrt(var + epsilon) * clean)
    channel_mean = jnp.concatenate(means, axis=1)
    channel_scale = jnp.concatenate(scales, axis=1)
    coarse = channel_scale.astype(jnp.bfloat16).astype(jnp.float32)
    fine = (channel_scale - coarse).astype(jnp.bfloat16).astype(jnp.float32)
    offset = channel_mean * (coarse + fine)

    def summing(depth):
        chosen = band_mask(depth, width)
        count = chosen.shape[0]
        matrix = jnp.concatenate(
            [jnp.where(chosen, coarse, 0.0), jnp.where(chosen, fine, 0.0)], axis=0
        ).astype(jnp.bfloat16)
        shift = jnp.sum(jnp.where(chosen, offset, 0.0), axis=1, keepdims=True)

        def tiles(slot):
            both = jnp.dot(matrix, x_ref[(my_group + slot) % beams], preferred_element_type=jnp.float32)
            sums = both[:count] + both[count:] - shift
            return [
                [sums[t:t + LANE_ROWS, p * LANES:(p + 1) * LANES] for p in range(2)]
                for t in range(0, count, LANE_ROWS)
            ]

        return tiles

    def message(block, slot, begin, end):
        return pltpu.make_async_remote_copy(
            src_ref=send.at[block, slot, pl.ds(begin, end - begin)],
            dst_ref=recv.at[my_place, pl.ds(begin, end - begin)],
            send_sem=send_sem.at[block, slot],
            recv_sem=recv_sem.at[my_place],
            device_id={"freq": block, "beam": (my_group + slot) % beams},
            device_id_type=pl.DeviceIdType.MESH,
        )

    def near_messages(action, slot, narrow):
        if narrow:
            action(message(0, slot, *block_span(2)))
            return

        @pl.when((my_block == 1) | (slot > 0))
        def _():
            action(message(0, slot, *block_span(0)))

    def double_messages(action, slot):
        def message(begin):
            return pltpu.make_async_remote_copy(
                src_ref=twice.at[slot, pl.ds(begin, 4 - begin)],
                dst_ref=taken.at[my_place, pl.ds(begin, 4 - begin)],
                send_sem=twice_sem.at[slot],
                recv_sem=taken_sem.at[my_place],
                device_id={"freq": 1, "beam": (my_group + slot) % beams},
                device_id_type=pl.DeviceIdType.MESH,
            )

        @pl.when(my_block == 0)
        def _():
            action(message(0))
        if slot > 0:
            @pl.when(my_block == 1)
            def _():
                action(message(2))

    def answer():
        return pltpu.make_async_remote_copy(
            src_ref=peaks, dst_ref=answered, send_sem=answer_sem.at[0], recv_sem=answer_sem.at[1],
            device_id={"freq": 0, "beam": my_group}, device_id_type=pl.DeviceIdType.MESH,
        )

    def near_phase(narrow, begin, end):
        tiles = summing(0 if narrow else 1)
        batch = 4
        for start in range(begin, end, batch):
            slots = range(start, start + batch)
            for slot, summed in [(slot, tiles(slot)) for slot in slots]:
                for number, leaf in enumerate(near_leaves(summed)):
                    if not narrow or number > 0:
                        send[0, slot, number] = leaf.astype(jnp.bfloat16)
                if not narrow:
                    for number, leaf in enumerate(double_leaves(summed)):
                        twice[slot, number] = leaf.astype(jnp.bfloat16)
                if slot == 0 and not narrow:
                    @pl.when(my_block == 0)
                    def _():
                        recv[my_place, :4] = send[0, 0, :4]

                    @pl.when(my_block == 1)
                    def _():
                        taken[my_place] = twice[0]
            if narrow:
                for slot in slots:
                    near_messages(lambda copy: copy.start(), slot, narrow)

    def next_messages(action, slot, low):
        action(message(1, slot, 0 if low else 4, 8))

    def by_half(source, action):
        for half in range(2):
            @pl.when((source * 2 >= quarter) if half else (source * 2 < quarter))
            def _(half=half):
                action(4 * half)

    def passed(row, begin):
        return pltpu.make_async_remote_copy(
            src_ref=far.at[quarter + row, :, pl.ds(begin, 8 - begin)],
            dst_ref=relay.at[row, :, pl.ds(begin, 8 - begin)],
            send_sem=far_sem.at[quarter + row, 0],
            recv_sem=relay_sem.at[row],
            device_id={"freq": 0, "beam": (my_group + quarter) % groups},
            device_id_type=pl.DeviceIdType.MESH,
        )

    def direct(beam, block, begin):
        return pltpu.make_async_remote_copy(
            src_ref=far.at[beam, block - 2, pl.ds(begin, 8 - begin)],
            dst_ref=recv.at[my_place, pl.ds(begin, 8 - begin)],
            send_sem=far_sem.at[beam, block - 2],
            recv_sem=recv_sem.at[my_place],
            device_id={"freq": block, "beam": beam},
            device_id_type=pl.DeviceIdType.MESH,
        )

    def onward(row, block, begin):
        return pltpu.make_async_remote_copy(
            src_ref=relay.at[row, block - 2, pl.ds(begin, 8 - begin)],
            dst_ref=recv.at[my_place - quarter, pl.ds(begin, 8 - begin)],
            send_sem=onward_sem.at[row, block - 2],
            recv_sem=recv_sem.at[my_place - quarter],
            device_id={"freq": block, "beam": quarter + row},
            device_id_type=pl.DeviceIdType.MESH,
        )

    def far_phase(low):
        tiles = summing(3 if low else 2)
        batch = 2
        for begin in range(0, beams, batch):
            slots = range(begin, begin + batch)
            for slot, summed in [(slot, tiles(slot)) for slot in slots]:
                for block, leaves in far_leaves(summed).items():
                    for number, leaf in enumerate(leaves):
                        if block == 1:
                            send[block, slot, number] = leaf.astype(jnp.bfloat16)
                        else:
                            far[(my_group + slot) % beams, block - 2, number] = leaf.astype(jnp.bfloat16)
            if not low:
                for slot in slots:
                    next_messages(lambda copy: copy.start(), slot, low)

    def landed(target, semaphore):
        pltpu.make_async_remote_copy(
            src_ref=target, dst_ref=target, send_sem=send_sem.at[0, 0], recv_sem=semaphore,
            device_id={"freq": my_block, "beam": my_group}, device_id_type=pl.DeviceIdType.MESH,
        ).wait_recv()

    def arrival(place, begin, end):
        landed(recv.at[place, pl.ds(begin, end - begin)], recv_sem.at[place])

    args = (recv, first, work, mid, series)
    pitch = first.shape[1] // LANE_ROWS

    def wide_places(count, numbers_of):
        per = count // LANE_ROWS
        return [
            ((place // per) * pitch + (place % per) * (pitch - LANE_ROWS) // per + address, place, numbers)
            for place in range(count) for address, numbers in numbers_of(place)
        ]

    @pl.when(my_block < 2)
    def _():
        near_phase(False, 0, beams)

        @pl.when((my_block == 0) & (my_group < quarter))
        def _():
            far_phase(True)

        pl.semaphore_wait(barrier, 2 * groups - 1)
        for slot in range(beams):
            near_messages(lambda copy: copy.start(), slot, False)
        for slot in range(beams):
            double_messages(lambda copy: copy.start(), slot)

        @pl.when((my_block == 0) & (my_group < quarter))
        def _():
            by_half(my_group, lambda begin: [passed(row, begin).start() for row in range(quarter)])
            for slot in range(beams):
                next_messages(lambda copy: copy.start(), slot, True)

        @pl.when((my_block == 0) & (my_group >= quarter))
        def _():
            far_phase(False)

    @pl.when(my_block >= 2)
    def _():
        near_phase(True, 0, beams)

    widths_load.wait()

    @pl.when(my_block == 0)
    def _():
        for place in range(groups):
            @pl.when(place != my_group)
            def _(place=place):
                arrival(place, *block_span(0))
        both = ((2, 3), (0, 1))
        plane_rows(recv, first, mid, groups, [(planes.at[root], 0, root, (both[root],)) for root in range(2)])

        pl.semaphore_wait(ready_sem, 2 * groups)

        @pl.when(my_group < quarter)
        def _():
            by_half(my_group, lambda begin: [
                direct(beam, block, begin).start() for beam in range(quarter) for block in (3, 2)
            ])

        @pl.when(my_group >= quarter)
        def _():
            def pass_on(begin):
                for row in range(quarter):
                    landed(relay.at[row, :, pl.ds(begin, 8 - begin)], relay_sem.at[row])
                    for block in (3, 2):
                        onward(row, block, begin).start()

            by_half(my_group - quarter, pass_on)

        for place in range(groups, 2 * groups):
            arrival(place, *block_span(1))
        plane_rows(recv, first, mid, groups, [(planes.at[root], 1, root, (both[root],)) for root in range(2)])
        lower_rows(planes, lower)
        late = ((2, 3), (None, 1))
        for plane in range(2, blocks):
            for place in range(plane * groups, (plane + 1) * groups):
                arrival(place, *block_span(2))
        plane_rows(recv, first, mid, groups, [
            (planes.at[root], plane, root, (late[root],)) for plane in range(2, blocks) for root in range(2)
        ])
        upper_rows(planes, lower, series)
        result = boxcar_rows(widths_ref, series, prefix, 2, 4)
        unfolded(result[:2], out_ref, 0)
        unfolded(result[2:], out_ref, 256)
        landed(answered, answer_sem.at[1])
        unpermuted([answered[column] for column in range(2)], out_ref, 512, 1, 4)

    @pl.when(my_block == 1)
    def _():
        for place in range(groups):
            landed(taken.at[place], taken_sem.at[place])
        plane_rows(taken, first, mid, groups, [(double, 0, 1, ((0, 2), (1, 3)))])
        for place in range(groups, 2 * groups):
            @pl.when(place != my_place)
            def _(place=place):
                landed(taken.at[place, pl.ds(2, 2)], taken_sem.at[place])
        plane_rows(taken, first, mid, groups, [(double, 1, 1, ((None, 2), (None, 3)))])
        double_rows(double, series, 256)
        for number, column in enumerate(boxcar_rows(widths_ref, series, prefix, 2, 2)):
            peaks[number] = column
        answer().start()
        for place in range(groups):
            arrival(place, *late_span(place, quarter))
        unit_rows(*args, 0, 1, 256, 2, wide_places(
            groups,
            lambda place: [
                (8 * (2 * (q % 2) + q // 2), (q if place < quarter else None, 4 + q)) for q in range(4)
            ],
        ))
        unpermuted(boxcar_rows(widths_ref, series, prefix, 0, 2), out_ref, 0, 2, 3)
        answer().wait_send()

    for late in (2, 3):
        @pl.when(my_block == late)
        def _(late=late):
            found = []
            for place in range(quarter):
                arrival(place, *late_span(place, quarter // 2))
                for q in range(4):
                    found.append((
                        (2 * (q % 2) + q // 2) * pitch + place * LANE_ROWS, place,
                        (q if 2 * place < quarter else None, 4 + q),
                    ))
            unit_rows(*args, 0, late, 128, 2, found)
            unpermuted(boxcar_rows(widths_ref, series, prefix, 0, 1), out_ref, 0, 3, 3)

    for slot in range(beams):
        for narrow in (True, False):
            @pl.when((my_block >= 2) == narrow)
            def _(narrow=narrow, slot=slot):
                near_messages(lambda copy: copy.wait_send(), slot, narrow)
                if not narrow:
                    double_messages(lambda copy: copy.wait_send(), slot)
        for low in (True, False):
            @pl.when((my_block == 0) & ((my_group < quarter) == low))
            def _(low=low, slot=slot):
                next_messages(lambda copy: copy.wait_send(), slot, low)

    @pl.when((my_block == 0) & (my_group < quarter))
    def _():
        by_half(my_group, lambda begin: [passed(row, begin).wait_send() for row in range(quarter)])
        by_half(my_group, lambda begin: [
            direct(beam, block, begin).wait_send() for beam in range(quarter) for block in (3, 2)
        ])

    @pl.when((my_block == 0) & (my_group >= quarter))
    def _():
        by_half(my_group - quarter, lambda begin: [
            onward(row, block, begin).wait_send() for row in range(quarter) for block in (3, 2)
        ])


def search(intensity, channel_mask, box_widths):
    beams, width, samples = intensity.shape
    blocks, groups = lax.axis_size("freq"), lax.axis_size("beam")
    devices = blocks * groups
    operands = (intensity, channel_mask.reshape(1, -1), box_widths)
    return pl.pallas_call(
        search_kernel,
        in_specs=[pl.BlockSpec(memory_space=pl.ANY)] * 3,
        out_specs=pl.BlockSpec(memory_space=pltpu.VMEM),
        scratch_shapes=[
            pltpu.VMEM((beams, width, samples), jnp.bfloat16),
            pltpu.VMEM((2 * LANE_ROWS, samples), jnp.bfloat16),
            pltpu.VMEM((1, width * groups), jnp.int32),
            pltpu.SMEM(box_widths.shape, jnp.int32),
            pltpu.SemaphoreType.DMA((6,)),
            pltpu.VMEM((2, beams, 8, LANE_ROWS, LANES), jnp.bfloat16),
            pltpu.SemaphoreType.DMA((2, beams)),
            pltpu.VMEM((devices, 8, LANE_ROWS, LANES), jnp.bfloat16),
            pltpu.SemaphoreType.DMA((devices,)),
            pltpu.VMEM((beams, 4, LANE_ROWS, LANES), jnp.bfloat16),
            pltpu.SemaphoreType.DMA((beams,)),
            pltpu.VMEM((2 * groups, 4, LANE_ROWS, LANES), jnp.bfloat16),
            pltpu.SemaphoreType.DMA((2 * groups,)),
            pltpu.VMEM((2, LANE_ROWS, LANES), jnp.float32),
            pltpu.VMEM((2, LANE_ROWS, LANES), jnp.float32),
            pltpu.SemaphoreType.DMA((2,)),
            pltpu.SemaphoreType.REGULAR,
            pltpu.VMEM((beams, 2, 8, LANE_ROWS, LANES), jnp.bfloat16),
            pltpu.SemaphoreType.DMA((beams, 2)),
            pltpu.VMEM((groups // 2, 2, 8, LANE_ROWS, LANES), jnp.bfloat16),
            pltpu.SemaphoreType.DMA((groups // 2,)),
            pltpu.SemaphoreType.DMA((groups // 2, 2)),
            pltpu.VMEM((2, samples + LANE_ROWS * LANE_ROWS, LANES), jnp.float32),
            pltpu.VMEM((2, samples, LANES), jnp.float32),
            pltpu.VMEM((2, samples, LANES), jnp.float32),
            pltpu.VMEM((2, blocks, 2, LANE_ROWS * LANE_ROWS, LANES), jnp.float32),
            pltpu.VMEM((2, 2, LANES, LANES), jnp.float32),
            pltpu.VMEM((2, 2, LANES, LANES), jnp.float32),
            pltpu.VMEM((3 * samples, 2 * samples), jnp.bfloat16),
            pltpu.VMEM((6, LANE_ROWS + samples + WIDEST, LANES), jnp.float32),
        ],
        out_shape=jax.ShapeDtypeStruct((1, NDM // blocks), jnp.float32),
        compiler_params=pltpu.CompilerParams(collective_id=0, has_side_effects=True, vmem_limit_bytes=32 << 20),
    )(*[pltpu.with_memory_space_constraint(value, pltpu.HBM) for value in operands])


def ramped(pair, start, stride, far, only_late=False):
    shape = pair[1].shape
    reach = (LANE_ROWS - 1) * stride
    place = lane_index(shape) + (start + reach - lax.broadcasted_iota(jnp.int32, shape, 0) * stride)
    turn = (-start - reach) % LANES

    def turned(piece):
        if turn + reach < LANES:
            return pltpu.roll(piece, turn, 1, stride=stride, stride_axis=0)
        return jnp.take_along_axis(piece, place & (LANES - 1), axis=1, mode="promise_in_bounds")

    late = turned(pair[1])
    if far:
        return [jnp.where(place < 2 * LANES, late, 0.0), None]
    near = place < LANES
    early = None if only_late else jnp.where(near, turned(pair[0]), late)
    return [early, jnp.where(near, late, 0.0)]


def joined_pair(low, high):
    return [a if b is None else (None if a is None else a + b) for a, b in zip(low, high)]


def unit_rows(recv, first, work, mid, series, base, root, leaves, kinds, found):
    tiles = leaves // LANE_ROWS
    pitch = first.shape[1] // LANE_ROWS
    for address, place, numbers in found:
        for part in range(2):
            if numbers[part] is not None:
                first[part, address:address + LANE_ROWS] = recv[place, numbers[part]].astype(jnp.float32)

    def leaf(tile, part):
        outer, kind = tile >> kinds, tile & ((1 << kinds) - 1)
        if leaves == LANE_ROWS * (pitch - LANE_ROWS):
            spot, step = ((outer >> 3 << kinds) + kind) * LANE_ROWS + (outer & 7), pitch
        else:
            spot, step = kind * pitch + outer, LANE_ROWS // 2
        return first[part, pl.ds(spot, LANE_ROWS, stride=step)]

    chunk = 8
    for c in range(tiles // chunk):
        tree = [[[leaf(c * chunk + k, part) for part in range(2)]] for k in range(chunk)]
        level_root = root
        while len(tree) > 1:
            tree = [
                [
                    plus(low[r // 2], stepped(high[r // 2], level_root + r // 2 + r % 2))
                    for r in range(2 * len(low))
                ]
                for low, high in zip(tree[0::2], tree[1::2])
            ]
            level_root = level_root * 2
        for j in range(chunk):
            for part in range(2):
                at = (j * (tiles // chunk) + c) * LANE_ROWS
                work[part, at:at + LANE_ROWS] = tree[0][j][part]
    chunks = tiles // chunk
    for j in range(chunk):
        tree = []
        for c in range(chunks):
            at = (j * chunks + c) * LANE_ROWS
            tree.append([[work[part, at:at + LANE_ROWS] for part in range(2)]])
        level_root = root * chunk + j
        while len(tree) > 1:
            tree = [
                [
                    plus(low[r // 2], stepped(high[r // 2], level_root + r // 2 + r % 2))
                    for r in range(2 * len(low))
                ]
                for low, high in zip(tree[0::2], tree[1::2])
            ]
            level_root = level_root * 2
        for k in range(chunks):
            for part in range(2):
                at = (j * chunks + k ^ LANE_ROWS - 1) * LANE_ROWS
                mid[part, at:at + LANE_ROWS] = tree[0][k][part]
    far = root > 0
    for g in range(tiles // LANE_ROWS):
        tree = []
        for s in range(LANE_ROWS):
            pair = [
                None if far and 2 * s >= LANE_ROWS and part == 0
                else mid[part, pl.ds(g * LANE_ROWS * LANE_ROWS + s, LANE_ROWS, stride=LANE_ROWS)]
                for part in range(2)
            ]
            tree.append([pair])
        rows = merged_rows(tree, root * tiles + g * LANE_ROWS, 1, far)
        for k in range(0, LANE_ROWS, 2):
            save_series(series, base + g * LANE_ROWS * LANE_ROWS + k * LANE_ROWS, rows[k:k + 2])


def merged_rows(tree, start, stride, far):
    while len(tree) > 1:
        tree = [
            [
                joined_pair(
                    low[r // 2],
                    ramped(
                        high[r // 2], start + r // 2 + r % 2, stride, far and len(tree) == 2,
                        high[r // 2][0] is None,
                    ),
                )
                for r in range(2 * len(low))
            ]
            for low, high in zip(tree[0::2], tree[1::2])
        ]
        start, stride = start * 2, stride * 2
    return tree[0]


def plane_rows(recv, first, mid, groups, jobs):
    flat = LANE_ROWS * LANE_ROWS
    origins, origin = [], 0
    for target, plane, root, numbers in jobs:
        origins.append(origin)
        origin += len(numbers) * flat
    used = [[part for part in range(2) if numbers[0][part] is not None] for _, _, _, numbers in jobs]
    for (target, plane, root, numbers), origin, parts in zip(jobs, origins, used):
        for place in range(groups):
            for kind in range(len(numbers)):
                for part in parts:
                    at = origin + kind * flat + place * LANE_ROWS
                    rows = recv[plane * groups + place, numbers[kind][part]]
                    first[part, at:at + LANE_ROWS] = rows.astype(jnp.float32)

    def pair_at(source, parts, start):
        return [source[part, pl.ds(start, LANE_ROWS, stride=LANE_ROWS)] if part in parts else None for part in range(2)]

    for (target, plane, root, numbers), origin, parts in zip(jobs, origins, used):
        kinds = len(numbers)
        tree = [
            [pair_at(first, parts, origin + (tile % kinds) * flat + tile // kinds)]
            for tile in range(kinds * LANE_ROWS)
        ]
        level_root = root
        while len(tree) > 1:
            tree = [
                [
                    joined_pair(low[r // 2], stepped(high[r // 2], level_root + r // 2 + r % 2))
                    for r in range(2 * len(low))
                ]
                for low, high in zip(tree[0::2], tree[1::2])
            ]
            level_root = level_root * 2
        for j, pair in enumerate(tree[0]):
            for part in parts:
                at = origin + (j ^ LANE_ROWS - 1) * LANE_ROWS
                mid[part, at:at + LANE_ROWS] = pair[part]
    for (target, plane, root, numbers), origin, parts in zip(jobs, origins, used):
        for g in range(len(numbers)):
            tree = [[pair_at(mid, parts, origin + g * flat + p)] for p in range(LANE_ROWS)]
            for k, pair in enumerate(merged_rows(tree, (root * len(numbers) + g) * LANE_ROWS, 1, False)):
                at = g * flat + k * LANE_ROWS
                for part in parts:
                    target[plane, part, at:at + LANE_ROWS] = pair[part]


def double_rows(target, series, base):
    for g in range(2):
        for k in range(LANE_ROWS):
            number = g * LANE_ROWS + k
            tree = [[plane_tile(target, 0, number, (0, 1))], [plane_tile(target, 1, number, (1,))]]
            rows = merged_rows(tree, LANES + g * LANE_ROWS * LANE_ROWS + k, LANE_ROWS, True)
            save_series(series, base + 2 * number * LANE_ROWS, rows)


def plane_tile(target, plane, k, parts):
    return [
        target[plane, part, k * LANE_ROWS:(k + 1) * LANE_ROWS] if part in parts else None for part in range(2)
    ]


def lower_rows(planes, lower):
    for k in range(LANE_ROWS):
        for root in range(2):
            tree = [[plane_tile(planes.at[root], plane, k, (0, 1))] for plane in range(2)]
            for q, pair in enumerate(merged_rows(tree, root * LANE_ROWS * LANE_ROWS + k, LANE_ROWS, False)):
                for part in range(2):
                    at = (2 * k + q) * LANE_ROWS
                    lower[root, part, at:at + LANE_ROWS] = pair[part]


def upper_rows(planes, lower, series):
    for root in range(2):
        parts = (0, 1) if root == 0 else (1,)
        for k in range(LANE_ROWS):
            begin = root * LANE_ROWS * LANE_ROWS + k
            tree = [[plane_tile(planes.at[root], plane, k, parts)] for plane in (2, 3)]
            high = merged_rows(tree, begin, LANE_ROWS, False)
            low = []
            for q in range(2):
                at = (2 * k + q) * LANE_ROWS
                low.append([lower[root, part, at:at + LANE_ROWS] for part in range(2)])
            rows = merged_rows([low, high], begin * 2, 2 * LANE_ROWS, root > 0)
            for number in range(0, 4, 2):
                at = (32 * (1 + root) + 4 * k + number) * LANE_ROWS
                save_series(series, at, rows[number:number + 2])


def save_series(series, at, pairs):
    rows = jnp.concatenate([jnp.concatenate(pair, axis=1) for pair in pairs], axis=0)
    coarse = rows.astype(jnp.bfloat16)
    samples = rows.shape[1]
    series[at:at + 2 * LANE_ROWS, :samples] = coarse
    series[at:at + 2 * LANE_ROWS, samples:] = (rows - coarse.astype(jnp.float32)).astype(jnp.bfloat16)


def unfolded(columns, out_ref, offset):
    lane = lane_index((LANE_ROWS, LANES))
    for number in range(2):
        picks = (lane & 15) * LANE_ROWS + (LANE_ROWS - 1) - (lane >> 5) - 4 * number
        spread = [jnp.take_along_axis(column, picks, axis=1, mode="promise_in_bounds") for column in columns]
        at = offset + number * LANES
        out_ref[:, at:at + LANES] = jnp.where(lane & 16 == 0, spread[0], spread[1])[:1]


def boxcar_rows(widths_ref, series, prefix, begin, count):
    lanes = prefix.shape[2]
    samples = series.shape[1] // 2
    until = lax.broadcasted_iota(jnp.int32, (samples, 2 * samples), 0)
    time = lax.broadcasted_iota(jnp.int32, (samples, 2 * samples), 1) & (samples - 1)
    ladder = jnp.where(time <= until, 1.0, 0.0).astype(jnp.bfloat16)
    piece = min(2, count)
    for start in range(begin, begin + count, piece):
        sums = lax.dot_general(
            ladder, series[start * lanes:(start + piece) * lanes], (((1,), (1,)), ((), ())),
            preferred_element_type=jnp.float32,
        )
        for side in range(piece):
            prefix[start + side, LANE_ROWS:LANE_ROWS + samples] = sums[:, side * lanes:(side + 1) * lanes]
    widths = [widths_ref[number] for number in range(widths_ref.shape[0])]
    norms = [
        lax.rsqrt(jnp.full((LANE_ROWS, lanes), width * CHANS, jnp.int32).astype(jnp.float32)) for width in widths
    ]
    result = []
    for column in range(begin, begin + count):
        ahead = [prefix[column, pl.ds(LANE_ROWS - 1 + width, samples)] for width in widths]
        base = prefix[column, LANE_ROWS - 1:LANE_ROWS - 1 + samples]
        best = [None] * len(widths)
        for at in range(0, samples, LANE_ROWS):
            before = base[at:at + LANE_ROWS]
            for number, after in enumerate(ahead):
                gain = after[at:at + LANE_ROWS] - before
                best[number] = gain if at == 0 else jnp.maximum(best[number], gain)
        peak = best[0] * norms[0]
        for value, norm in zip(best[1:], norms[1:]):
            peak = jnp.maximum(peak, value * norm)
        result.append(jnp.broadcast_to(jnp.max(peak, axis=0, keepdims=True), (LANE_ROWS, lanes)))
    return result


def unpermuted(columns, out_ref, offset, repeat_bits, bits):
    lane = lane_index((LANE_ROWS, LANES))
    for number in range(len(columns) << repeat_bits):
        row = (lane + number * LANES) >> repeat_bits
        row = row & (LANES - 1)
        block = LANE_ROWS << bits
        picks = (row & (LANES - block)) + (row & ((1 << bits) - 1)) * LANE_ROWS + (LANE_ROWS - 1) - ((row & (block - 1)) >> bits)
        column = columns[number >> repeat_bits]
        spread = jnp.take_along_axis(column, picks, axis=1, mode="promise_in_bounds")
        at = offset + number * LANES
        out_ref[:, at:at + LANES] = spread[:1]


def shards(intensity, channel_mask, box_widths):
    beams, width, samples = intensity.shape
    blocks, groups = lax.axis_size("freq"), lax.axis_size("beam")
    if compact(samples, blocks * groups, blocks, groups, beams, width):
        return search(intensity, channel_mask, box_widths)
    rows = entry_rows(intensity, channel_mask)
    return trial_peaks(rows, box_widths, lax.axis_index("freq").reshape(1))


def solution(mesh):
    in_specs = (P(None, ("freq", "beam"), None), P("freq"), P())
    out_specs = P("beam", "freq")
    return jax.shard_map(shards, mesh=mesh, in_specs=in_specs, out_specs=out_specs, check_vma=False)
```

```python
import jax
import jax.numpy as jnp
from jax import lax
from jax.experimental import pallas as pl
from jax.experimental.pallas import tpu as pltpu
from jax.sharding import PartitionSpec as P

CHANS = 16384
NDM = 4096
LANE_ROWS = 8
LANES = 128
WIDEST = 64

epsilon = 1e-05


def reverse_bits(number, count):
    result = 0
    for _ in range(count):
        result = result << 1 | number & 1
        number >>= 1
    return result


def lane_index(shape):
    return lax.broadcasted_iota(jnp.int32, shape, len(shape) - 1)


def earlier(block, amount):
    if amount == 0:
        return block
    samples = block.shape[-1]
    return jnp.where(lane_index(block.shape) < samples - amount, pltpu.roll(block, samples - amount, 1), 0.0)


def folds(trial_dev, samples):
    return trial_dev >= 4 * samples


def channel_limits(trial_dev, blocks, samples):
    limits = []
    for block in range(blocks):
        limit, rows = CHANS, NDM
        while (block * trial_dev * rows // NDM + 1) // 2 >= samples:
            limit, rows = limit // 2, rows // 2
        limits.append(limit)
    return limits


def entry_kernel(x_hbm, mask_ref, out_ref, x_ref, in_sem, send, send_sem, recv_sem, own_sem):
    blocks, beams, bands, samples = send.shape
    groups = lax.axis_size("beam")
    beam_dev = beams // groups
    width = x_ref.shape[1]
    group = width // (bands * blocks)
    trial_dev = NDM // blocks
    row_total = float(beams * samples)
    fold = folds(trial_dev, samples)
    limits = channel_limits(trial_dev, blocks, samples)
    my_block = lax.axis_index("freq")
    my_group = lax.axis_index("beam")
    my_place = my_block * groups + my_group
    devices = blocks * groups

    barrier = pltpu.get_barrier_semaphore()
    for step in range(1, devices):
        peer = (my_place + step) % devices
        pl.semaphore_signal(
            barrier, inc=1, device_id={"freq": peer // groups, "beam": peer % groups},
            device_id_type=pl.DeviceIdType.MESH,
        )

    chunks = in_sem.shape[0]
    span = width // chunks
    loads = [
        pltpu.make_async_copy(
            x_hbm.at[:, pl.ds(c * span, span)], x_ref.at[:, pl.ds(c * span, span)], in_sem.at[c]
        )
        for c in range(chunks)
    ]
    for load in loads:
        load.start()
    means, scales = [], []
    for c in range(chunks):
        loads[c].wait()
        total = jnp.zeros((span, samples), jnp.float32)
        squares = jnp.zeros((span, samples), jnp.float32)
        for beam in range(beams):
            wide = x_ref[beam, c * span:(c + 1) * span].astype(jnp.float32)
            total = total + wide
            squares = squares + wide * wide
        mean = jnp.sum(total, axis=1, keepdims=True) / row_total
        var = jnp.sum(squares, axis=1, keepdims=True) / row_total - mean * mean
        means.append(mean)
        scales.append(lax.rsqrt(var + epsilon))
    channel_mean = jnp.concatenate(means, axis=0)
    channel_scale = jnp.concatenate(scales, axis=0)
    out_row = lax.broadcasted_iota(jnp.int32, (blocks * bands, width), 0)
    channel = lax.broadcasted_iota(jnp.int32, (blocks * bands, width), 1)
    band = out_row % bands
    if fold:
        half = bands // 2
        band = (band % half) * 2 + band // half
    wanted = band * blocks + out_row // bands
    clean = mask_ref[:, pl.ds(pl.multiple_of(my_group * width, width), width)].astype(jnp.float32)
    chosen = jnp.where(channel // group == wanted, clean, 0.0).astype(jnp.bfloat16)
    upper = my_block * 2 >= blocks

    def message(block, slot, beam, rows):
        return pltpu.make_async_remote_copy(
            src_ref=send.at[block, slot, pl.ds(0, rows)],
            dst_ref=out_ref.at[beam % beam_dev, my_place, pl.ds(0, rows)],
            send_sem=send_sem.at[block, slot],
            recv_sem=recv_sem.at[beam % beam_dev, my_place],
            device_id={"freq": block, "beam": beam // beam_dev},
            device_id_type=pl.DeviceIdType.MESH,
        )

    def own_copy(slot, part):
        return pltpu.make_async_copy(
            send.at[my_block, slot], out_ref.at[part, my_place], own_sem.at[part]
        )

    def every_message(action, slot):
        beam = (my_group * beam_dev + slot) % beams
        for block in range(blocks):
            goes = my_place * width < limits[block]
            if slot < beam_dev:
                goes = goes & (my_block != block)
            if fold:
                @pl.when(goes & upper)
                def _(block=block):
                    action(message(block, slot, beam, bands // 2))
                goes = goes & jnp.logical_not(upper)

            @pl.when(goes)
            def _(block=block):
                action(message(block, slot, beam, bands))

    for slot in range(beams):
        beam = (my_group * beam_dev + slot) % beams
        wide = x_ref[beam].astype(jnp.float32)
        normed = ((wide - channel_mean) * channel_scale).astype(jnp.bfloat16)
        sums = jnp.dot(chosen, normed, preferred_element_type=jnp.float32)
        tree = [[sums[i * bands:(i + 1) * bands]] for i in range(blocks)]
        while len(tree) > 1:
            merged = []
            for low, high in zip(tree[0::2], tree[1::2]):
                merged.append(
                    [low[m // 2] + earlier(high[m // 2], (m + 1) // 2) for m in range(2 * len(low))]
                )
            tree = merged
        for number, row in enumerate(tree[0]):
            if fold:
                both = row[:half] + row[half:]
                row = jnp.concatenate([jnp.where(upper, both, row[:half]), row[half:]], axis=0)
            send[number, slot] = row.astype(jnp.bfloat16)
        if slot == 0:
            pl.semaphore_wait(barrier, devices - 1)
        every_message(lambda copy: copy.start(), slot)
        if slot < beam_dev:
            own_copy(slot, slot).start()

    for slot in range(beam_dev):
        own_copy(slot, slot).wait()
    limit = sum(jnp.where(my_block == block, limits[block], 0) for block in range(blocks))
    for place in range(devices):
        for part in range(beam_dev):
            rows = bands // 2 if fold and 2 * place >= devices else bands
            target = out_ref.at[part, place, pl.ds(0, rows)]
            @pl.when((place * width < limit) & (place != my_place))
            def _(target=target, place=place, part=part):
                pltpu.make_async_remote_copy(
                    src_ref=target, dst_ref=target, send_sem=send_sem.at[0, 0],
                    recv_sem=recv_sem.at[part, place],
                    device_id={"freq": my_block, "beam": my_group},
                    device_id_type=pl.DeviceIdType.MESH,
                ).wait_recv()
    for slot in range(beams):
        every_message(lambda copy: copy.wait_send(), slot)


def entry_rows(intensity, channel_mask):
    beams, width, samples = intensity.shape
    blocks, groups = lax.axis_size("freq"), lax.axis_size("beam")
    bands = width * NDM // (CHANS * blocks)
    beam_dev, devices = beams // groups, blocks * groups
    return pl.pallas_call(
        entry_kernel,
        in_specs=[pl.BlockSpec(memory_space=pl.ANY), pl.BlockSpec(memory_space=pltpu.VMEM)],
        out_specs=pl.BlockSpec(memory_space=pl.ANY),
        scratch_shapes=[
            pltpu.VMEM((beams, width, samples), jnp.bfloat16),
            pltpu.SemaphoreType.DMA((4,)),
            pltpu.VMEM((blocks, beams, bands, samples), jnp.bfloat16),
            pltpu.SemaphoreType.DMA((blocks, beams)),
            pltpu.SemaphoreType.DMA((beam_dev, devices)),
            pltpu.SemaphoreType.DMA((beam_dev,)),
        ],
        out_shape=jax.ShapeDtypeStruct((beam_dev, devices, bands, samples), jnp.bfloat16),
        compiler_params=pltpu.CompilerParams(collective_id=0, has_side_effects=True),
    )(intensity, channel_mask.reshape(1, -1))


def advanced(pieces, amount):
    lanes = pieces[0].shape[-1]
    position = lane_index(pieces[0].shape)
    turn = (lanes - amount) & (lanes - 1)
    turned = [pltpu.roll(piece, turn, 1) for piece in pieces]
    return joined(turned, lambda limit: position < limit - amount)


def advanced_rows(pieces, amounts):
    lanes = pieces[0].shape[-1]
    position = lane_index(pieces[0].shape) + amounts
    picks = position & (lanes - 1)
    turned = [jnp.take_along_axis(piece, picks, axis=1, mode="promise_in_bounds") for piece in pieces]
    return joined(turned, lambda limit: position < limit)


def joined(turned, below):
    lanes = turned[0].shape[-1]
    near = [below((k + 1) * lanes) for k in range(len(turned))]
    result = []
    for number in range(len(turned)):
        value = jnp.zeros_like(turned[0])
        for ahead in reversed(range(len(turned) - number)):
            value = jnp.where(near[ahead], turned[number + ahead], value)
        result.append(value)
    return result


def trial_kernel(place_ref, widths_ref, x_ref, out_ref, first, even, odd, series, prefix):
    total, samples = out_ref.shape[2], x_ref.shape[3]
    tiles = total // LANE_ROWS
    tile_bits = tiles.bit_length() - 1
    lanes = prefix.shape[2]
    parts = samples // lanes
    pitch = first.shape[1] // LANE_ROWS
    block = place_ref[0]
    bands = x_ref.shape[2]
    fold = folds(total, samples)
    half_bands = bands // 2
    sources = x_ref.shape[1]
    for number in range(sources):
        high, start = divmod(number * bands, tiles)
        start += reverse_bits(high, LANE_ROWS.bit_length() - 1) * pitch
        for part in range(parts):
            cut = slice(part * lanes, (part + 1) * lanes)
            if fold and 2 * number >= sources:
                first[part, start:start + half_bands] = x_ref[0, number, :half_bands, cut].astype(jnp.float32)
                first[part, start + half_bands:start + bands] = jnp.zeros((half_bands, lanes), jnp.float32)
            else:
                first[part, start:start + bands] = x_ref[0, number, :, cut].astype(jnp.float32)
    for tile in range(tiles):
        spot = tile
        if fold:
            band = tile % bands
            spot = tile - band + (band % 2) * half_bands + band // 2
        for part in range(parts):
            even[reverse_bits(tile, tile_bits), :, part * lanes:(part + 1) * lanes] = first[
                part, pl.ds(spot, LANE_ROWS, stride=pitch)
            ]

    source, target = even, odd
    count = 1
    while count < tiles:
        half = tiles // count // 2

        def merge(j, source=source, target=target, count=count, half=half):
            flat = (half * LANE_ROWS, lanes)
            cut = [slice(part * lanes, (part + 1) * lanes) for part in range(parts)]
            low = [source[pl.ds(j * 2 * half, half), :, c].reshape(flat) for c in cut]
            high = [source[pl.ds(j * 2 * half + half, half), :, c].reshape(flat) for c in cut]
            for side in range(2):
                moved = advanced(high, block * count + j + side)
                for c, base, extra in zip(cut, low, moved):
                    target[pl.ds((2 * j + side) * half, half), :, c] = (base + extra).reshape(
                        half, LANE_ROWS, lanes
                    )

        if count <= 16:
            for j in range(count):
                merge(j)
        else:
            def step(i, carry, merge=merge):
                for k in range(32):
                    merge(i * 32 + k)
                return carry
            lax.fori_loop(0, count // 32, step, 0)
        source, target = target, source
        count = count * 2

    spot = lax.broadcasted_iota(jnp.int32, (LANE_ROWS, lanes), 0)
    bits = [spot >> 2 & 1, spot >> 1 & 1, spot & 1]
    clear = [bit == 0 for bit in bits]

    def final_rows(j):
        pieces = [source[j, :, part * lanes:(part + 1) * lanes] for part in range(parts)]
        row = spot * 0 + (block * tiles + j)
        for level, reach in enumerate((4, 2, 1)):
            low, high = [], []
            for piece in pieces:
                down = pltpu.roll(piece, reach, 0)
                up = down if 2 * reach == LANE_ROWS else pltpu.roll(piece, LANE_ROWS - reach, 0)
                low.append(jnp.where(clear[level], piece, down))
                high.append(jnp.where(clear[level], up, piece))
            moved = advanced_rows(high, row + bits[level])
            pieces = [base + extra for base, extra in zip(low, moved)]
            row = 2 * row + bits[level]
        return jnp.concatenate(pieces, axis=1)

    def finish(i, carry):
        for k in range(16):
            pair = i * 16 + k
            rows = jnp.concatenate([final_rows(2 * pair), final_rows(2 * pair + 1)], axis=0)
            coarse = rows.astype(jnp.bfloat16)
            place = pl.ds(pl.multiple_of(pair * 16, 16), 16)
            series[place, :samples] = coarse
            series[place, samples:] = (rows - coarse.astype(jnp.float32)).astype(jnp.bfloat16)
        return carry

    lax.fori_loop(0, tiles // 32, finish, 0)

    until = lax.broadcasted_iota(jnp.int32, (samples, 2 * samples), 0)
    time = lax.broadcasted_iota(jnp.int32, (samples, 2 * samples), 1) & (samples - 1)
    ladder = jnp.where(time <= until, 1.0, 0.0).astype(jnp.bfloat16)
    margin = prefix.shape[1] - samples - LANE_ROWS
    piece = 2 * lanes
    for part in range(total // piece):
        sums = lax.dot_general(
            ladder, series[part * piece:(part + 1) * piece], (((1,), (1,)), ((), ())),
            preferred_element_type=jnp.float32,
        )
        for side in range(2):
            column = 2 * part + side
            prefix[column, :LANE_ROWS] = jnp.zeros((LANE_ROWS, lanes), jnp.float32)
            prefix[column, LANE_ROWS:LANE_ROWS + samples] = sums[:, side * lanes:(side + 1) * lanes]
            prefix[column, LANE_ROWS + samples:] = jnp.full((margin, lanes), -jnp.inf, jnp.float32)
    for column in range(total // lanes):
        best = None
        for number in range(widths_ref.shape[0]):
            width = widths_ref[number]
            sums = (
                prefix[column, pl.ds(LANE_ROWS - 1 + width, samples)]
                - prefix[column, LANE_ROWS - 1:LANE_ROWS - 1 + samples]
            )
            norm = lax.rsqrt(jnp.full((1, lanes), width * CHANS, jnp.int32).astype(jnp.float32))
            peak = jnp.max(sums, axis=0, keepdims=True) * norm
            best = peak if best is None else jnp.maximum(best, peak)
        out_ref[0, :, column * lanes:(column + 1) * lanes] = best


def trial_peaks(rows, box_widths, place):
    beams, devices, bands, samples = rows.shape
    total = devices * bands
    tiles = total // LANE_ROWS
    return pl.pallas_call(
        trial_kernel,
        grid_spec=pltpu.PrefetchScalarGridSpec(
            num_scalar_prefetch=2,
            grid=(beams,),
            in_specs=[pl.BlockSpec((1, devices, bands, samples), lambda b, p, w: (b, 0, 0, 0))],
            out_specs=pl.BlockSpec((1, 1, total), lambda b, p, w: (b, 0, 0)),
            scratch_shapes=[
                pltpu.VMEM((samples // LANES, total + LANE_ROWS * LANE_ROWS, LANES), jnp.float32),
                pltpu.VMEM((tiles, LANE_ROWS, samples), jnp.float32),
                pltpu.VMEM((tiles, LANE_ROWS, samples), jnp.float32),
                pltpu.VMEM((total, 2 * samples), jnp.bfloat16),
                pltpu.VMEM((total // LANES, LANE_ROWS + samples + WIDEST, LANES), jnp.float32),
            ],
        ),
        out_shape=jax.ShapeDtypeStruct((beams, 1, total), jnp.float32),
    )(place, box_widths, rows)[:, 0]


def compact(samples, devices, blocks, groups, beams, width):
    return (
        samples == 2 * LANES and NDM == 16 * samples and blocks == 4 and beams == groups
        and devices * LANE_ROWS == samples and width * devices == CHANS
    )


def block_span(block):
    return ((0, 4), (0, 4), (1, 4), (1, 4))[block]


def late_span(place, whole):
    return (0, 8) if place < whole else (4, 8)


def band_mask(depth, width):
    rows = LANE_ROWS * (2 << depth)
    row = lax.broadcasted_iota(jnp.int32, (rows, width), 0)
    channel = lax.broadcasted_iota(jnp.int32, (rows, width), 1)
    inner, tile = row % LANE_ROWS, row // LANE_ROWS
    if depth == 0:
        wanted = inner * 2 + tile
    else:
        quarter = tile % 4
        band = inner * 4 + (quarter % 2) * 2 + quarter // 2
        wanted = band * (rows // (4 * LANE_ROWS)) + tile // 4
    return channel // (width // rows) == wanted


def stepped(pair, amount):
    if amount == 0:
        return list(pair)
    lane = lane_index(pair[1].shape)
    near = lane < LANES - amount
    turned = [None if piece is None else pltpu.roll(piece, LANES - amount, 1) for piece in pair]
    early = None if turned[0] is None else jnp.where(near, turned[0], turned[1])
    return [early, jnp.where(near, turned[1], 0.0)]


def plus(low, high):
    return [a + b for a, b in zip(low, high)]


def near_leaves(tiles):
    wide = [plus(tiles[0], tiles[2]), plus(tiles[1], tiles[3])] if len(tiles) == 4 else tiles
    return plus_late(wide) + plus(wide[0], wide[1])


def plus_late(pair):
    return plus(pair[0], stepped(pair[1], 1))


def double_leaves(tiles):
    pairs = [plus_late([tiles[a], tiles[2 + a]]) for a in range(2)]
    return [pair[part] for part in range(2) for pair in pairs]


def far_leaves(tiles):
    parts = [tiles[at:at + 4] for at in range(0, len(tiles), 4)]
    halves = parts if len(parts) == 2 else [[plus(a, b) for a, b in zip(*parts[at:at + 2])] for at in (0, 2)]
    out = {1: [plus(low, stepped(high, 1)) for low, high in zip(*halves)]}
    if len(parts) == 4:
        one, two = [[plus(a, stepped(b, 1)) for a, b in zip(*parts[at:at + 2])] for at in (0, 2)]
        for block in (2, 3):
            out[block] = [plus(low, stepped(high, block - 1)) for low, high in zip(one, two)]
    return {block: [pair[part] for part in range(2) for pair in pairs] for block, pairs in out.items()}


def search_kernel(
    x_hbm, mask_hbm, widths_hbm, out_ref, x_ref, unit_ref, mask_ref, widths_ref, in_sem, send, send_sem, recv, recv_sem,
    twice, twice_sem, taken, taken_sem, peaks, answered, answer_sem, ready_sem, far, far_sem, relay, relay_sem, onward_sem, first, work, mid, planes, double, lower, series, prefix,
):
    beams, width, samples = x_ref.shape
    blocks, groups = lax.axis_size("freq"), lax.axis_size("beam")
    devices = blocks * groups
    row_total = float(beams * samples)
    my_block = lax.axis_index("freq")
    my_group = lax.axis_index("beam")
    my_place = my_block * groups + my_group
    quarter = groups // 2

    chunks = in_sem.shape[0] - 2
    span = width // chunks
    loads = [
        pltpu.make_async_copy(
            x_hbm.at[:, pl.ds(c * span, span)], x_ref.at[:, pl.ds(c * span, span)], in_sem.at[c]
        )
        for c in range(chunks)
    ]
    mask_load = pltpu.make_async_copy(mask_hbm, mask_ref, in_sem.at[chunks])
    widths_load = pltpu.make_async_copy(widths_hbm, widths_ref, in_sem.at[chunks + 1])
    loads[0].start()
    mask_load.start()
    for load in loads[1:]:
        load.start()
    widths_load.start()

    def signal(semaphore, block, group):
        pl.semaphore_signal(
            semaphore, inc=1, device_id={"freq": block, "beam": group}, device_id_type=pl.DeviceIdType.MESH,
        )

    barrier = pltpu.get_barrier_semaphore()

    @pl.when(my_block == 0)
    def _():
        for block in (3, 1, 2):
            for group in range(groups):
                signal(barrier, block, group)
        for step in range(1, groups):
            signal(barrier, 0, (my_group + step) % groups)

    @pl.when(my_block == 1)
    def _():
        for group in range(groups):
            signal(barrier, 0, group)
        for step in range(1, groups):
            signal(barrier, 1, (my_group + step) % groups)

    @pl.when(my_block >= 2)
    def _():
        pl.semaphore_wait(barrier, groups)
        for group in range(groups):
            signal(ready_sem, 0, group)

    for column in range(prefix.shape[0]):
        prefix[column, :LANE_ROWS] = jnp.zeros((LANE_ROWS, LANES), jnp.float32)
        prefix[column, LANE_ROWS + samples:] = jnp.full((WIDEST, LANES), -jnp.inf, jnp.float32)

    lane = lax.broadcasted_iota(jnp.int32, (LANE_ROWS, LANES), 1)
    inner = lax.broadcasted_iota(jnp.int32, (LANE_ROWS, LANES), 0)
    unit_ref[...] = jnp.ones(unit_ref.shape, jnp.bfloat16)
    means, scales = [], []
    for c in range(chunks):
        loads[c].wait()
        if c == 0:
            mask_load.wait()
        unit = unit_ref[...].astype(jnp.float32)
        totals = []
        for column in range(span // LANES):
            found = [jnp.zeros((LANE_ROWS, LANES), jnp.float32) for _ in range(2)]
            for pair in range(LANES // (2 * LANE_ROWS)):
                at = c * span + column * LANES + pair * 2 * LANE_ROWS
                sums = [jnp.zeros((2 * LANE_ROWS, samples), jnp.float32) for _ in range(2)]
                for b in range(beams):
                    wide = x_ref[b, at:at + 2 * LANE_ROWS].astype(jnp.float32)
                    sums = [sums[0] + wide * unit, sums[1] + wide * wide]
                sums = [jnp.sum(value, axis=1, keepdims=True) for value in sums]
                for half in range(2):
                    spot = lane == inner + (2 * pair + half) * LANE_ROWS
                    cut = slice(half * LANE_ROWS, (half + 1) * LANE_ROWS)
                    found = [have + jnp.where(spot, value[cut], 0.0) for have, value in zip(found, sums)]
            totals.append([jnp.sum(value, axis=0, keepdims=True) for value in found])
        mean = jnp.concatenate([total[0] for total in totals], axis=1) / row_total
        var = jnp.concatenate([total[1] for total in totals], axis=1) / row_total - mean * mean
        place = pl.multiple_of(my_group * width + c * span, span)
        clean = mask_ref[:, pl.ds(place, span)].astype(jnp.float32)
        means.append(mean)
        scales.append(lax.rsqrt(var + epsilon) * clean)
    channel_mean = jnp.concatenate(means, axis=1)
    channel_scale = jnp.concatenate(scales, axis=1)
    coarse = channel_scale.astype(jnp.bfloat16).astype(jnp.float32)
    fine = (channel_scale - coarse).astype(jnp.bfloat16).astype(jnp.float32)
    offset = channel_mean * (coarse + fine)

    def summing(depth):
        chosen = band_mask(depth, width)
        count = chosen.shape[0]
        matrix = jnp.concatenate(
            [jnp.where(chosen, coarse, 0.0), jnp.where(chosen, fine, 0.0)], axis=0
        ).astype(jnp.bfloat16)
        shift = jnp.sum(jnp.where(chosen, offset, 0.0), axis=1, keepdims=True)

        def tiles(slot):
            both = jnp.dot(matrix, x_ref[(my_group + slot) % beams], preferred_element_type=jnp.float32)
            sums = both[:count] + both[count:] - shift
            return [
                [sums[t:t + LANE_ROWS, p * LANES:(p + 1) * LANES] for p in range(2)]
                for t in range(0, count, LANE_ROWS)
            ]

        return tiles

    def message(block, slot, begin, end):
        return pltpu.make_async_remote_copy(
            src_ref=send.at[block, slot, pl.ds(begin, end - begin)],
            dst_ref=recv.at[my_place, pl.ds(begin, end - begin)],
            send_sem=send_sem.at[block, slot],
            recv_sem=recv_sem.at[my_place],
            device_id={"freq": block, "beam": (my_group + slot) % beams},
            device_id_type=pl.DeviceIdType.MESH,
        )

    def near_messages(action, slot, narrow):
        if narrow:
            action(message(0, slot, *block_span(2)))
            return

        @pl.when((my_block == 1) | (slot > 0))
        def _():
            action(message(0, slot, *block_span(0)))

    def double_messages(action, slot):
        def message(begin):
            return pltpu.make_async_remote_copy(
                src_ref=twice.at[slot, pl.ds(begin, 4 - begin)],
                dst_ref=taken.at[my_place, pl.ds(begin, 4 - begin)],
                send_sem=twice_sem.at[slot],
                recv_sem=taken_sem.at[my_place],
                device_id={"freq": 1, "beam": (my_group + slot) % beams},
                device_id_type=pl.DeviceIdType.MESH,
            )

        @pl.when(my_block == 0)
        def _():
            action(message(0))
        if slot > 0:
            @pl.when(my_block == 1)
            def _():
                action(message(2))

    def answer():
        return pltpu.make_async_remote_copy(
            src_ref=peaks, dst_ref=answered, send_sem=answer_sem.at[0], recv_sem=answer_sem.at[1],
            device_id={"freq": 0, "beam": my_group}, device_id_type=pl.DeviceIdType.MESH,
        )

    def near_phase(narrow, begin, end):
        tiles = summing(0 if narrow else 1)
        batch = 4
        for start in range(begin, end, batch):
            slots = range(start, start + batch)
            for slot, summed in [(slot, tiles(slot)) for slot in slots]:
                for number, leaf in enumerate(near_leaves(summed)):
                    if not narrow or number > 0:
                        send[0, slot, number] = leaf.astype(jnp.bfloat16)
                if not narrow:
                    for number, leaf in enumerate(double_leaves(summed)):
                        twice[slot, number] = leaf.astype(jnp.bfloat16)
                if slot == 0 and not narrow:
                    @pl.when(my_block == 0)
                    def _():
                        recv[my_place, :4] = send[0, 0, :4]

                    @pl.when(my_block == 1)
                    def _():
                        taken[my_place] = twice[0]
            if narrow:
                for slot in slots:
                    near_messages(lambda copy: copy.start(), slot, narrow)

    def next_messages(action, slot, low):
        action(message(1, slot, 0 if low else 4, 8))

    def by_half(source, action):
        for half in range(2):
            @pl.when((source * 2 >= quarter) if half else (source * 2 < quarter))
            def _(half=half):
                action(4 * half)

    def passed(row, begin):
        return pltpu.make_async_remote_copy(
            src_ref=far.at[quarter + row, :, pl.ds(begin, 8 - begin)],
            dst_ref=relay.at[row, :, pl.ds(begin, 8 - begin)],
            send_sem=far_sem.at[quarter + row, 0],
            recv_sem=relay_sem.at[row],
            device_id={"freq": 0, "beam": (my_group + quarter) % groups},
            device_id_type=pl.DeviceIdType.MESH,
        )

    def direct(beam, block, begin):
        return pltpu.make_async_remote_copy(
            src_ref=far.at[beam, block - 2, pl.ds(begin, 8 - begin)],
            dst_ref=recv.at[my_place, pl.ds(begin, 8 - begin)],
            send_sem=far_sem.at[beam, block - 2],
            recv_sem=recv_sem.at[my_place],
            device_id={"freq": block, "beam": beam},
            device_id_type=pl.DeviceIdType.MESH,
        )

    def onward(row, block, begin):
        return pltpu.make_async_remote_copy(
            src_ref=relay.at[row, block - 2, pl.ds(begin, 8 - begin)],
            dst_ref=recv.at[my_place - quarter, pl.ds(begin, 8 - begin)],
            send_sem=onward_sem.at[row, block - 2],
            recv_sem=recv_sem.at[my_place - quarter],
            device_id={"freq": block, "beam": quarter + row},
            device_id_type=pl.DeviceIdType.MESH,
        )

    def far_phase(low):
        tiles = summing(3 if low else 2)
        batch = 2
        for begin in range(0, beams, batch):
            slots = range(begin, begin + batch)
            for slot, summed in [(slot, tiles(slot)) for slot in slots]:
                for block, leaves in far_leaves(summed).items():
                    for number, leaf in enumerate(leaves):
                        if block == 1:
                            send[block, slot, number] = leaf.astype(jnp.bfloat16)
                        else:
                            far[(my_group + slot) % beams, block - 2, number] = leaf.astype(jnp.bfloat16)
            if not low:
                for slot in slots:
                    next_messages(lambda copy: copy.start(), slot, low)

    def landed(target, semaphore):
        pltpu.make_async_remote_copy(
            src_ref=target, dst_ref=target, send_sem=send_sem.at[0, 0], recv_sem=semaphore,
            device_id={"freq": my_block, "beam": my_group}, device_id_type=pl.DeviceIdType.MESH,
        ).wait_recv()

    def arrival(place, begin, end):
        landed(recv.at[place, pl.ds(begin, end - begin)], recv_sem.at[place])

    args = (recv, first, work, mid, series)
    pitch = first.shape[1] // LANE_ROWS

    def wide_places(count, numbers_of):
        per = count // LANE_ROWS
        return [
            ((place // per) * pitch + (place % per) * (pitch - LANE_ROWS) // per + address, place, numbers)
            for place in range(count) for address, numbers in numbers_of(place)
        ]

    @pl.when(my_block < 2)
    def _():
        near_phase(False, 0, beams)

        @pl.when((my_block == 0) & (my_group < quarter))
        def _():
            far_phase(True)

        pl.semaphore_wait(barrier, 2 * groups - 1)
        for slot in range(beams):
            double_messages(lambda copy: copy.start(), slot)
        for slot in range(beams):
            near_messages(lambda copy: copy.start(), slot, False)

        @pl.when((my_block == 0) & (my_group < quarter))
        def _():
            by_half(my_group, lambda begin: [passed(row, begin).start() for row in range(quarter)])
            for slot in range(beams):
                next_messages(lambda copy: copy.start(), slot, True)

        @pl.when((my_block == 0) & (my_group >= quarter))
        def _():
            far_phase(False)

    @pl.when(my_block >= 2)
    def _():
        near_phase(True, 0, beams)

    widths_load.wait()

    @pl.when(my_block == 0)
    def _():
        for place in range(groups):
            @pl.when(place != my_group)
            def _(place=place):
                arrival(place, *block_span(0))
        both = ((2, 3), (0, 1))
        plane_rows(recv, first, mid, groups, [(planes.at[root], 0, root, (both[root],)) for root in range(2)])

        pl.semaphore_wait(ready_sem, 2 * groups)

        @pl.when(my_group < quarter)
        def _():
            by_half(my_group, lambda begin: [
                direct(beam, block, begin).start() for beam in range(quarter) for block in (3, 2)
            ])

        @pl.when(my_group >= quarter)
        def _():
            def pass_on(begin):
                for row in range(quarter):
                    landed(relay.at[row, :, pl.ds(begin, 8 - begin)], relay_sem.at[row])
                    for block in (3, 2):
                        onward(row, block, begin).start()

            by_half(my_group - quarter, pass_on)

        for place in range(groups, 2 * groups):
            arrival(place, *block_span(1))
        plane_rows(recv, first, mid, groups, [(planes.at[root], 1, root, (both[root],)) for root in range(2)])
        lower_rows(planes, lower)
        late = ((2, 3), (None, 1))
        for plane in range(2, blocks):
            for place in range(plane * groups, (plane + 1) * groups):
                arrival(place, *block_span(2))
            plane_rows(recv, first, mid, groups, [(planes.at[root], plane, root, (late[root],)) for root in range(2)])
        upper_rows(planes, lower, series)
        result = boxcar_rows(widths_ref, series, prefix, 2, 4)
        unfolded(result[:2], out_ref, 0)
        unfolded(result[2:], out_ref, 256)
        landed(answered, answer_sem.at[1])
        unpermuted([answered[column] for column in range(2)], out_ref, 512, 1, 4)

    @pl.when(my_block == 1)
    def _():
        for place in range(groups):
            landed(taken.at[place], taken_sem.at[place])
        plane_rows(taken, first, mid, groups, [(double, 0, 1, ((0, 2), (1, 3)))])
        for place in range(groups, 2 * groups):
            @pl.when(place != my_place)
            def _(place=place):
                landed(taken.at[place, pl.ds(2, 2)], taken_sem.at[place])
        plane_rows(taken, first, mid, groups, [(double, 1, 1, ((None, 2), (None, 3)))])
        double_rows(double, series, 256)
        for number, column in enumerate(boxcar_rows(widths_ref, series, prefix, 2, 2)):
            peaks[number] = column
        answer().start()
        for place in range(groups):
            arrival(place, *late_span(place, quarter))
        unit_rows(*args, 0, 1, 256, 2, wide_places(
            groups,
            lambda place: [
                (8 * (2 * (q % 2) + q // 2), (q if place < quarter else None, 4 + q)) for q in range(4)
            ],
        ))
        unpermuted(boxcar_rows(widths_ref, series, prefix, 0, 2), out_ref, 0, 2, 3)
        answer().wait_send()

    for late in (2, 3):
        @pl.when(my_block == late)
        def _(late=late):
            found = []
            for place in range(quarter):
                arrival(place, *late_span(place, quarter // 2))
                for q in range(4):
                    found.append((
                        (2 * (q % 2) + q // 2) * pitch + place * LANE_ROWS, place,
                        (q if 2 * place < quarter else None, 4 + q),
                    ))
            unit_rows(*args, 0, late, 128, 2, found)
            unpermuted(boxcar_rows(widths_ref, series, prefix, 0, 1), out_ref, 0, 3, 3)

    for slot in range(beams):
        for narrow in (True, False):
            @pl.when((my_block >= 2) == narrow)
            def _(narrow=narrow, slot=slot):
                near_messages(lambda copy: copy.wait_send(), slot, narrow)
                if not narrow:
                    double_messages(lambda copy: copy.wait_send(), slot)
        for low in (True, False):
            @pl.when((my_block == 0) & ((my_group < quarter) == low))
            def _(low=low, slot=slot):
                next_messages(lambda copy: copy.wait_send(), slot, low)

    @pl.when((my_block == 0) & (my_group < quarter))
    def _():
        by_half(my_group, lambda begin: [passed(row, begin).wait_send() for row in range(quarter)])
        by_half(my_group, lambda begin: [
            direct(beam, block, begin).wait_send() for beam in range(quarter) for block in (3, 2)
        ])

    @pl.when((my_block == 0) & (my_group >= quarter))
    def _():
        by_half(my_group - quarter, lambda begin: [
            onward(row, block, begin).wait_send() for row in range(quarter) for block in (3, 2)
        ])


def search(intensity, channel_mask, box_widths):
    beams, width, samples = intensity.shape
    blocks, groups = lax.axis_size("freq"), lax.axis_size("beam")
    devices = blocks * groups
    operands = (intensity, channel_mask.reshape(1, -1), box_widths)
    return pl.pallas_call(
        search_kernel,
        in_specs=[pl.BlockSpec(memory_space=pl.ANY)] * 3,
        out_specs=pl.BlockSpec(memory_space=pltpu.VMEM),
        scratch_shapes=[
            pltpu.VMEM((beams, width, samples), jnp.bfloat16),
            pltpu.VMEM((2 * LANE_ROWS, samples), jnp.bfloat16),
            pltpu.VMEM((1, width * groups), jnp.int32),
            pltpu.SMEM(box_widths.shape, jnp.int32),
            pltpu.SemaphoreType.DMA((6,)),
            pltpu.VMEM((2, beams, 8, LANE_ROWS, LANES), jnp.bfloat16),
            pltpu.SemaphoreType.DMA((2, beams)),
            pltpu.VMEM((devices, 8, LANE_ROWS, LANES), jnp.bfloat16),
            pltpu.SemaphoreType.DMA((devices,)),
            pltpu.VMEM((beams, 4, LANE_ROWS, LANES), jnp.bfloat16),
            pltpu.SemaphoreType.DMA((beams,)),
            pltpu.VMEM((2 * groups, 4, LANE_ROWS, LANES), jnp.bfloat16),
            pltpu.SemaphoreType.DMA((2 * groups,)),
            pltpu.VMEM((2, LANE_ROWS, LANES), jnp.float32),
            pltpu.VMEM((2, LANE_ROWS, LANES), jnp.float32),
            pltpu.SemaphoreType.DMA((2,)),
            pltpu.SemaphoreType.REGULAR,
            pltpu.VMEM((beams, 2, 8, LANE_ROWS, LANES), jnp.bfloat16),
            pltpu.SemaphoreType.DMA((beams, 2)),
            pltpu.VMEM((groups // 2, 2, 8, LANE_ROWS, LANES), jnp.bfloat16),
            pltpu.SemaphoreType.DMA((groups // 2,)),
            pltpu.SemaphoreType.DMA((groups // 2, 2)),
            pltpu.VMEM((2, samples + LANE_ROWS * LANE_ROWS, LANES), jnp.float32),
            pltpu.VMEM((2, samples, LANES), jnp.float32),
            pltpu.VMEM((2, samples, LANES), jnp.float32),
            pltpu.VMEM((2, blocks, 2, LANE_ROWS * LANE_ROWS, LANES), jnp.float32),
            pltpu.VMEM((2, 2, LANES, LANES), jnp.float32),
            pltpu.VMEM((2, 2, LANES, LANES), jnp.float32),
            pltpu.VMEM((3 * samples, 2 * samples), jnp.bfloat16),
            pltpu.VMEM((6, LANE_ROWS + samples + WIDEST, LANES), jnp.float32),
        ],
        out_shape=jax.ShapeDtypeStruct((1, NDM // blocks), jnp.float32),
        compiler_params=pltpu.CompilerParams(collective_id=0, has_side_effects=True, vmem_limit_bytes=32 << 20),
    )(*[pltpu.with_memory_space_constraint(value, pltpu.HBM) for value in operands])


def ramped(pair, start, stride, far, only_late=False):
    shape = pair[1].shape
    reach = (LANE_ROWS - 1) * stride
    place = lane_index(shape) + (start + reach - lax.broadcasted_iota(jnp.int32, shape, 0) * stride)
    turn = (-start - reach) % LANES

    def turned(piece):
        if turn + reach < LANES:
            return pltpu.roll(piece, turn, 1, stride=stride, stride_axis=0)
        return jnp.take_along_axis(piece, place & (LANES - 1), axis=1, mode="promise_in_bounds")

    late = turned(pair[1])
    if far:
        return [jnp.where(place < 2 * LANES, late, 0.0), None]
    near = place < LANES
    early = None if only_late else jnp.where(near, turned(pair[0]), late)
    return [early, jnp.where(near, late, 0.0)]


def joined_pair(low, high):
    return [a if b is None else (None if a is None else a + b) for a, b in zip(low, high)]


def unit_rows(recv, first, work, mid, series, base, root, leaves, kinds, found):
    tiles = leaves // LANE_ROWS
    pitch = first.shape[1] // LANE_ROWS
    for address, place, numbers in found:
        for part in range(2):
            if numbers[part] is not None:
                first[part, address:address + LANE_ROWS] = recv[place, numbers[part]].astype(jnp.float32)

    def leaf(tile, part):
        outer, kind = tile >> kinds, tile & ((1 << kinds) - 1)
        if leaves == LANE_ROWS * (pitch - LANE_ROWS):
            spot, step = ((outer >> 3 << kinds) + kind) * LANE_ROWS + (outer & 7), pitch
        else:
            spot, step = kind * pitch + outer, LANE_ROWS // 2
        return first[part, pl.ds(spot, LANE_ROWS, stride=step)]

    chunk = 8
    for c in range(tiles // chunk):
        tree = [[[leaf(c * chunk + k, part) for part in range(2)]] for k in range(chunk)]
        level_root = root
        while len(tree) > 1:
            tree = [
                [
                    plus(low[r // 2], stepped(high[r // 2], level_root + r // 2 + r % 2))
                    for r in range(2 * len(low))
                ]
                for low, high in zip(tree[0::2], tree[1::2])
            ]
            level_root = level_root * 2
        for j in range(chunk):
            for part in range(2):
                at = (j * (tiles // chunk) + c) * LANE_ROWS
                work[part, at:at + LANE_ROWS] = tree[0][j][part]
    chunks = tiles // chunk
    for j in range(chunk):
        tree = []
        for c in range(chunks):
            at = (j * chunks + c) * LANE_ROWS
            tree.append([[work[part, at:at + LANE_ROWS] for part in range(2)]])
        level_root = root * chunk + j
        while len(tree) > 1:
            tree = [
                [
                    plus(low[r // 2], stepped(high[r // 2], level_root + r // 2 + r % 2))
                    for r in range(2 * len(low))
                ]
                for low, high in zip(tree[0::2], tree[1::2])
            ]
            level_root = level_root * 2
        for k in range(chunks):
            for part in range(2):
                at = (j * chunks + k ^ LANE_ROWS - 1) * LANE_ROWS
                mid[part, at:at + LANE_ROWS] = tree[0][k][part]
    far = root > 0
    for g in range(tiles // LANE_ROWS):
        tree = []
        for s in range(LANE_ROWS):
            pair = [
                None if far and 2 * s >= LANE_ROWS and part == 0
                else mid[part, pl.ds(g * LANE_ROWS * LANE_ROWS + s, LANE_ROWS, stride=LANE_ROWS)]
                for part in range(2)
            ]
            tree.append([pair])
        rows = merged_rows(tree, root * tiles + g * LANE_ROWS, 1, far)
        for k in range(0, LANE_ROWS, 2):
            save_series(series, base + g * LANE_ROWS * LANE_ROWS + k * LANE_ROWS, rows[k:k + 2])


def merged_rows(tree, start, stride, far):
    while len(tree) > 1:
        tree = [
            [
                joined_pair(
                    low[r // 2],
                    ramped(
                        high[r // 2], start + r // 2 + r % 2, stride, far and len(tree) == 2,
                        high[r // 2][0] is None,
                    ),
                )
                for r in range(2 * len(low))
            ]
            for low, high in zip(tree[0::2], tree[1::2])
        ]
        start, stride = start * 2, stride * 2
    return tree[0]


def plane_rows(recv, first, mid, groups, jobs):
    flat = LANE_ROWS * LANE_ROWS
    origins, origin = [], 0
    for target, plane, root, numbers in jobs:
        origins.append(origin)
        origin += len(numbers) * flat
    used = [[part for part in range(2) if numbers[0][part] is not None] for _, _, _, numbers in jobs]
    for (target, plane, root, numbers), origin, parts in zip(jobs, origins, used):
        for place in range(groups):
            for kind in range(len(numbers)):
                for part in parts:
                    at = origin + kind * flat + place * LANE_ROWS
                    rows = recv[plane * groups + place, numbers[kind][part]]
                    first[part, at:at + LANE_ROWS] = rows.astype(jnp.float32)

    def pair_at(source, parts, start):
        return [source[part, pl.ds(start, LANE_ROWS, stride=LANE_ROWS)] if part in parts else None for part in range(2)]

    for (target, plane, root, numbers), origin, parts in zip(jobs, origins, used):
        kinds = len(numbers)
        tree = [
            [pair_at(first, parts, origin + (tile % kinds) * flat + tile // kinds)]
            for tile in range(kinds * LANE_ROWS)
        ]
        level_root = root
        while len(tree) > 1:
            tree = [
                [
                    joined_pair(low[r // 2], stepped(high[r // 2], level_root + r // 2 + r % 2))
                    for r in range(2 * len(low))
                ]
                for low, high in zip(tree[0::2], tree[1::2])
            ]
            level_root = level_root * 2
        for j, pair in enumerate(tree[0]):
            for part in parts:
                at = origin + (j ^ LANE_ROWS - 1) * LANE_ROWS
                mid[part, at:at + LANE_ROWS] = pair[part]
    for (target, plane, root, numbers), origin, parts in zip(jobs, origins, used):
        for g in range(len(numbers)):
            tree = [[pair_at(mid, parts, origin + g * flat + p)] for p in range(LANE_ROWS)]
            for k, pair in enumerate(merged_rows(tree, (root * len(numbers) + g) * LANE_ROWS, 1, False)):
                at = g * flat + k * LANE_ROWS
                for part in parts:
                    target[plane, part, at:at + LANE_ROWS] = pair[part]


def double_rows(target, series, base):
    for g in range(2):
        for k in range(LANE_ROWS):
            number = g * LANE_ROWS + k
            tree = [[plane_tile(target, 0, number, (0, 1))], [plane_tile(target, 1, number, (1,))]]
            rows = merged_rows(tree, LANES + g * LANE_ROWS * LANE_ROWS + k, LANE_ROWS, True)
            save_series(series, base + 2 * number * LANE_ROWS, rows)


def plane_tile(target, plane, k, parts):
    return [
        target[plane, part, k * LANE_ROWS:(k + 1) * LANE_ROWS] if part in parts else None for part in range(2)
    ]


def lower_rows(planes, lower):
    for k in range(LANE_ROWS):
        for root in range(2):
            tree = [[plane_tile(planes.at[root], plane, k, (0, 1))] for plane in range(2)]
            for q, pair in enumerate(merged_rows(tree, root * LANE_ROWS * LANE_ROWS + k, LANE_ROWS, False)):
                for part in range(2):
                    at = (2 * k + q) * LANE_ROWS
                    lower[root, part, at:at + LANE_ROWS] = pair[part]


def upper_rows(planes, lower, series):
    for root in range(2):
        parts = (0, 1) if root == 0 else (1,)
        for k in range(LANE_ROWS):
            begin = root * LANE_ROWS * LANE_ROWS + k
            tree = [[plane_tile(planes.at[root], plane, k, parts)] for plane in (2, 3)]
            high = merged_rows(tree, begin, LANE_ROWS, False)
            low = []
            for q in range(2):
                at = (2 * k + q) * LANE_ROWS
                low.append([lower[root, part, at:at + LANE_ROWS] for part in range(2)])
            rows = merged_rows([low, high], begin * 2, 2 * LANE_ROWS, root > 0)
            for number in range(0, 4, 2):
                at = (32 * (1 + root) + 4 * k + number) * LANE_ROWS
                save_series(series, at, rows[number:number + 2])


def save_series(series, at, pairs):
    rows = jnp.concatenate([jnp.concatenate(pair, axis=1) for pair in pairs], axis=0)
    coarse = rows.astype(jnp.bfloat16)
    samples = rows.shape[1]
    series[at:at + 2 * LANE_ROWS, :samples] = coarse
    series[at:at + 2 * LANE_ROWS, samples:] = (rows - coarse.astype(jnp.float32)).astype(jnp.bfloat16)


def unfolded(columns, out_ref, offset):
    lane = lane_index((LANE_ROWS, LANES))
    for number in range(2):
        picks = (lane & 15) * LANE_ROWS + (LANE_ROWS - 1) - (lane >> 5) - 4 * number
        spread = [jnp.take_along_axis(column, picks, axis=1, mode="promise_in_bounds") for column in columns]
        at = offset + number * LANES
        out_ref[:, at:at + LANES] = jnp.where(lane & 16 == 0, spread[0], spread[1])[:1]


def boxcar_rows(widths_ref, series, prefix, begin, count):
    lanes = prefix.shape[2]
    samples = series.shape[1] // 2
    until = lax.broadcasted_iota(jnp.int32, (samples, 2 * samples), 0)
    time = lax.broadcasted_iota(jnp.int32, (samples, 2 * samples), 1) & (samples - 1)
    ladder = jnp.where(time <= until, 1.0, 0.0).astype(jnp.bfloat16)
    piece = min(2, count)
    for start in range(begin, begin + count, piece):
        sums = lax.dot_general(
            ladder, series[start * lanes:(start + piece) * lanes], (((1,), (1,)), ((), ())),
            preferred_element_type=jnp.float32,
        )
        for side in range(piece):
            prefix[start + side, LANE_ROWS:LANE_ROWS + samples] = sums[:, side * lanes:(side + 1) * lanes]
    widths = [widths_ref[number] for number in range(widths_ref.shape[0])]
    norms = [
        lax.rsqrt(jnp.full((LANE_ROWS, lanes), width * CHANS, jnp.int32).astype(jnp.float32)) for width in widths
    ]
    result = []
    for column in range(begin, begin + count):
        ahead = [prefix[column, pl.ds(LANE_ROWS - 1 + width, samples)] for width in widths]
        base = prefix[column, LANE_ROWS - 1:LANE_ROWS - 1 + samples]
        best = [None] * len(widths)
        for at in range(0, samples, LANE_ROWS):
            before = base[at:at + LANE_ROWS]
            for number, after in enumerate(ahead):
                gain = after[at:at + LANE_ROWS] - before
                best[number] = gain if at == 0 else jnp.maximum(best[number], gain)
        peak = best[0] * norms[0]
        for value, norm in zip(best[1:], norms[1:]):
            peak = jnp.maximum(peak, value * norm)
        result.append(jnp.broadcast_to(jnp.max(peak, axis=0, keepdims=True), (LANE_ROWS, lanes)))
    return result


def unpermuted(columns, out_ref, offset, repeat_bits, bits):
    lane = lane_index((LANE_ROWS, LANES))
    for number in range(len(columns) << repeat_bits):
        row = (lane + number * LANES) >> repeat_bits
        row = row & (LANES - 1)
        block = LANE_ROWS << bits
        picks = (row & (LANES - block)) + (row & ((1 << bits) - 1)) * LANE_ROWS + (LANE_ROWS - 1) - ((row & (block - 1)) >> bits)
        column = columns[number >> repeat_bits]
        spread = jnp.take_along_axis(column, picks, axis=1, mode="promise_in_bounds")
        at = offset + number * LANES
        out_ref[:, at:at + LANES] = spread[:1]


def shards(intensity, channel_mask, box_widths):
    beams, width, samples = intensity.shape
    blocks, groups = lax.axis_size("freq"), lax.axis_size("beam")
    if compact(samples, blocks * groups, blocks, groups, beams, width):
        return search(intensity, channel_mask, box_widths)
    rows = entry_rows(intensity, channel_mask)
    return trial_peaks(rows, box_widths, lax.axis_index("freq").reshape(1))


def solution(mesh):
    in_specs = (P(None, ("freq", "beam"), None), P("freq"), P())
    out_specs = P("beam", "freq")
    return jax.shard_map(shards, mesh=mesh, in_specs=in_specs, out_specs=out_specs, check_vma=False)
```

```python
import jax
import jax.numpy as jnp
from jax import lax
from jax.experimental import pallas as pl
from jax.experimental.pallas import tpu as pltpu
from jax.sharding import PartitionSpec as P

CHANS = 16384
NDM = 4096
LANE_ROWS = 8
LANES = 128
WIDEST = 64

epsilon = 1e-05


def reverse_bits(number, count):
    result = 0
    for _ in range(count):
        result = result << 1 | number & 1
        number >>= 1
    return result


def lane_index(shape):
    return lax.broadcasted_iota(jnp.int32, shape, len(shape) - 1)


def earlier(block, amount):
    if amount == 0:
        return block
    samples = block.shape[-1]
    return jnp.where(lane_index(block.shape) < samples - amount, pltpu.roll(block, samples - amount, 1), 0.0)


def folds(trial_dev, samples):
    return trial_dev >= 4 * samples


def channel_limits(trial_dev, blocks, samples):
    limits = []
    for block in range(blocks):
        limit, rows = CHANS, NDM
        while (block * trial_dev * rows // NDM + 1) // 2 >= samples:
            limit, rows = limit // 2, rows // 2
        limits.append(limit)
    return limits


def entry_kernel(x_hbm, mask_ref, out_ref, x_ref, in_sem, send, send_sem, recv_sem, own_sem):
    blocks, beams, bands, samples = send.shape
    groups = lax.axis_size("beam")
    beam_dev = beams // groups
    width = x_ref.shape[1]
    group = width // (bands * blocks)
    trial_dev = NDM // blocks
    row_total = float(beams * samples)
    fold = folds(trial_dev, samples)
    limits = channel_limits(trial_dev, blocks, samples)
    my_block = lax.axis_index("freq")
    my_group = lax.axis_index("beam")
    my_place = my_block * groups + my_group
    devices = blocks * groups

    barrier = pltpu.get_barrier_semaphore()
    for step in range(1, devices):
        peer = (my_place + step) % devices
        pl.semaphore_signal(
            barrier, inc=1, device_id={"freq": peer // groups, "beam": peer % groups},
            device_id_type=pl.DeviceIdType.MESH,
        )

    chunks = in_sem.shape[0]
    span = width // chunks
    loads = [
        pltpu.make_async_copy(
            x_hbm.at[:, pl.ds(c * span, span)], x_ref.at[:, pl.ds(c * span, span)], in_sem.at[c]
        )
        for c in range(chunks)
    ]
    for load in loads:
        load.start()
    means, scales = [], []
    for c in range(chunks):
        loads[c].wait()
        total = jnp.zeros((span, samples), jnp.float32)
        squares = jnp.zeros((span, samples), jnp.float32)
        for beam in range(beams):
            wide = x_ref[beam, c * span:(c + 1) * span].astype(jnp.float32)
            total = total + wide
            squares = squares + wide * wide
        mean = jnp.sum(total, axis=1, keepdims=True) / row_total
        var = jnp.sum(squares, axis=1, keepdims=True) / row_total - mean * mean
        means.append(mean)
        scales.append(lax.rsqrt(var + epsilon))
    channel_mean = jnp.concatenate(means, axis=0)
    channel_scale = jnp.concatenate(scales, axis=0)
    out_row = lax.broadcasted_iota(jnp.int32, (blocks * bands, width), 0)
    channel = lax.broadcasted_iota(jnp.int32, (blocks * bands, width), 1)
    band = out_row % bands
    if fold:
        half = bands // 2
        band = (band % half) * 2 + band // half
    wanted = band * blocks + out_row // bands
    clean = mask_ref[:, pl.ds(pl.multiple_of(my_group * width, width), width)].astype(jnp.float32)
    chosen = jnp.where(channel // group == wanted, clean, 0.0).astype(jnp.bfloat16)
    upper = my_block * 2 >= blocks

    def message(block, slot, beam, rows):
        return pltpu.make_async_remote_copy(
            src_ref=send.at[block, slot, pl.ds(0, rows)],
            dst_ref=out_ref.at[beam % beam_dev, my_place, pl.ds(0, rows)],
            send_sem=send_sem.at[block, slot],
            recv_sem=recv_sem.at[beam % beam_dev, my_place],
            device_id={"freq": block, "beam": beam // beam_dev},
            device_id_type=pl.DeviceIdType.MESH,
        )

    def own_copy(slot, part):
        return pltpu.make_async_copy(
            send.at[my_block, slot], out_ref.at[part, my_place], own_sem.at[part]
        )

    def every_message(action, slot):
        beam = (my_group * beam_dev + slot) % beams
        for block in range(blocks):
            goes = my_place * width < limits[block]
            if slot < beam_dev:
                goes = goes & (my_block != block)
            if fold:
                @pl.when(goes & upper)
                def _(block=block):
                    action(message(block, slot, beam, bands // 2))
                goes = goes & jnp.logical_not(upper)

            @pl.when(goes)
            def _(block=block):
                action(message(block, slot, beam, bands))

    for slot in range(beams):
        beam = (my_group * beam_dev + slot) % beams
        wide = x_ref[beam].astype(jnp.float32)
        normed = ((wide - channel_mean) * channel_scale).astype(jnp.bfloat16)
        sums = jnp.dot(chosen, normed, preferred_element_type=jnp.float32)
        tree = [[sums[i * bands:(i + 1) * bands]] for i in range(blocks)]
        while len(tree) > 1:
            merged = []
            for low, high in zip(tree[0::2], tree[1::2]):
                merged.append(
                    [low[m // 2] + earlier(high[m // 2], (m + 1) // 2) for m in range(2 * len(low))]
                )
            tree = merged
        for number, row in enumerate(tree[0]):
            if fold:
                both = row[:half] + row[half:]
                row = jnp.concatenate([jnp.where(upper, both, row[:half]), row[half:]], axis=0)
            send[number, slot] = row.astype(jnp.bfloat16)
        if slot == 0:
            pl.semaphore_wait(barrier, devices - 1)
        every_message(lambda copy: copy.start(), slot)
        if slot < beam_dev:
            own_copy(slot, slot).start()

    for slot in range(beam_dev):
        own_copy(slot, slot).wait()
    limit = sum(jnp.where(my_block == block, limits[block], 0) for block in range(blocks))
    for place in range(devices):
        for part in range(beam_dev):
            rows = bands // 2 if fold and 2 * place >= devices else bands
            target = out_ref.at[part, place, pl.ds(0, rows)]
            @pl.when((place * width < limit) & (place != my_place))
            def _(target=target, place=place, part=part):
                pltpu.make_async_remote_copy(
                    src_ref=target, dst_ref=target, send_sem=send_sem.at[0, 0],
                    recv_sem=recv_sem.at[part, place],
                    device_id={"freq": my_block, "beam": my_group},
                    device_id_type=pl.DeviceIdType.MESH,
                ).wait_recv()
    for slot in range(beams):
        every_message(lambda copy: copy.wait_send(), slot)


def entry_rows(intensity, channel_mask):
    beams, width, samples = intensity.shape
    blocks, groups = lax.axis_size("freq"), lax.axis_size("beam")
    bands = width * NDM // (CHANS * blocks)
    beam_dev, devices = beams // groups, blocks * groups
    return pl.pallas_call(
        entry_kernel,
        in_specs=[pl.BlockSpec(memory_space=pl.ANY), pl.BlockSpec(memory_space=pltpu.VMEM)],
        out_specs=pl.BlockSpec(memory_space=pl.ANY),
        scratch_shapes=[
            pltpu.VMEM((beams, width, samples), jnp.bfloat16),
            pltpu.SemaphoreType.DMA((4,)),
            pltpu.VMEM((blocks, beams, bands, samples), jnp.bfloat16),
            pltpu.SemaphoreType.DMA((blocks, beams)),
            pltpu.SemaphoreType.DMA((beam_dev, devices)),
            pltpu.SemaphoreType.DMA((beam_dev,)),
        ],
        out_shape=jax.ShapeDtypeStruct((beam_dev, devices, bands, samples), jnp.bfloat16),
        compiler_params=pltpu.CompilerParams(collective_id=0, has_side_effects=True),
    )(intensity, channel_mask.reshape(1, -1))


def advanced(pieces, amount):
    lanes = pieces[0].shape[-1]
    position = lane_index(pieces[0].shape)
    turn = (lanes - amount) & (lanes - 1)
    turned = [pltpu.roll(piece, turn, 1) for piece in pieces]
    return joined(turned, lambda limit: position < limit - amount)


def advanced_rows(pieces, amounts):
    lanes = pieces[0].shape[-1]
    position = lane_index(pieces[0].shape) + amounts
    picks = position & (lanes - 1)
    turned = [jnp.take_along_axis(piece, picks, axis=1, mode="promise_in_bounds") for piece in pieces]
    return joined(turned, lambda limit: position < limit)


def joined(turned, below):
    lanes = turned[0].shape[-1]
    near = [below((k + 1) * lanes) for k in range(len(turned))]
    result = []
    for number in range(len(turned)):
        value = jnp.zeros_like(turned[0])
        for ahead in reversed(range(len(turned) - number)):
            value = jnp.where(near[ahead], turned[number + ahead], value)
        result.append(value)
    return result


def trial_kernel(place_ref, widths_ref, x_ref, out_ref, first, even, odd, series, prefix):
    total, samples = out_ref.shape[2], x_ref.shape[3]
    tiles = total // LANE_ROWS
    tile_bits = tiles.bit_length() - 1
    lanes = prefix.shape[2]
    parts = samples // lanes
    pitch = first.shape[1] // LANE_ROWS
    block = place_ref[0]
    bands = x_ref.shape[2]
    fold = folds(total, samples)
    half_bands = bands // 2
    sources = x_ref.shape[1]
    for number in range(sources):
        high, start = divmod(number * bands, tiles)
        start += reverse_bits(high, LANE_ROWS.bit_length() - 1) * pitch
        for part in range(parts):
            cut = slice(part * lanes, (part + 1) * lanes)
            if fold and 2 * number >= sources:
                first[part, start:start + half_bands] = x_ref[0, number, :half_bands, cut].astype(jnp.float32)
                first[part, start + half_bands:start + bands] = jnp.zeros((half_bands, lanes), jnp.float32)
            else:
                first[part, start:start + bands] = x_ref[0, number, :, cut].astype(jnp.float32)
    for tile in range(tiles):
        spot = tile
        if fold:
            band = tile % bands
            spot = tile - band + (band % 2) * half_bands + band // 2
        for part in range(parts):
            even[reverse_bits(tile, tile_bits), :, part * lanes:(part + 1) * lanes] = first[
                part, pl.ds(spot, LANE_ROWS, stride=pitch)
            ]

    source, target = even, odd
    count = 1
    while count < tiles:
        half = tiles // count // 2

        def merge(j, source=source, target=target, count=count, half=half):
            flat = (half * LANE_ROWS, lanes)
            cut = [slice(part * lanes, (part + 1) * lanes) for part in range(parts)]
            low = [source[pl.ds(j * 2 * half, half), :, c].reshape(flat) for c in cut]
            high = [source[pl.ds(j * 2 * half + half, half), :, c].reshape(flat) for c in cut]
            for side in range(2):
                moved = advanced(high, block * count + j + side)
                for c, base, extra in zip(cut, low, moved):
                    target[pl.ds((2 * j + side) * half, half), :, c] = (base + extra).reshape(
                        half, LANE_ROWS, lanes
                    )

        if count <= 16:
            for j in range(count):
                merge(j)
        else:
            def step(i, carry, merge=merge):
                for k in range(32):
                    merge(i * 32 + k)
                return carry
            lax.fori_loop(0, count // 32, step, 0)
        source, target = target, source
        count = count * 2

    spot = lax.broadcasted_iota(jnp.int32, (LANE_ROWS, lanes), 0)
    bits = [spot >> 2 & 1, spot >> 1 & 1, spot & 1]
    clear = [bit == 0 for bit in bits]

    def final_rows(j):
        pieces = [source[j, :, part * lanes:(part + 1) * lanes] for part in range(parts)]
        row = spot * 0 + (block * tiles + j)
        for level, reach in enumerate((4, 2, 1)):
            low, high = [], []
            for piece in pieces:
                down = pltpu.roll(piece, reach, 0)
                up = down if 2 * reach == LANE_ROWS else pltpu.roll(piece, LANE_ROWS - reach, 0)
                low.append(jnp.where(clear[level], piece, down))
                high.append(jnp.where(clear[level], up, piece))
            moved = advanced_rows(high, row + bits[level])
            pieces = [base + extra for base, extra in zip(low, moved)]
            row = 2 * row + bits[level]
        return jnp.concatenate(pieces, axis=1)

    def finish(i, carry):
        for k in range(16):
            pair = i * 16 + k
            rows = jnp.concatenate([final_rows(2 * pair), final_rows(2 * pair + 1)], axis=0)
            coarse = rows.astype(jnp.bfloat16)
            place = pl.ds(pl.multiple_of(pair * 16, 16), 16)
            series[place, :samples] = coarse
            series[place, samples:] = (rows - coarse.astype(jnp.float32)).astype(jnp.bfloat16)
        return carry

    lax.fori_loop(0, tiles // 32, finish, 0)

    until = lax.broadcasted_iota(jnp.int32, (samples, 2 * samples), 0)
    time = lax.broadcasted_iota(jnp.int32, (samples, 2 * samples), 1) & (samples - 1)
    ladder = jnp.where(time <= until, 1.0, 0.0).astype(jnp.bfloat16)
    margin = prefix.shape[1] - samples - LANE_ROWS
    piece = 2 * lanes
    for part in range(total // piece):
        sums = lax.dot_general(
            ladder, series[part * piece:(part + 1) * piece], (((1,), (1,)), ((), ())),
            preferred_element_type=jnp.float32,
        )
        for side in range(2):
            column = 2 * part + side
            prefix[column, :LANE_ROWS] = jnp.zeros((LANE_ROWS, lanes), jnp.float32)
            prefix[column, LANE_ROWS:LANE_ROWS + samples] = sums[:, side * lanes:(side + 1) * lanes]
            prefix[column, LANE_ROWS + samples:] = jnp.full((margin, lanes), -jnp.inf, jnp.float32)
    for column in range(total // lanes):
        best = None
        for number in range(widths_ref.shape[0]):
            width = widths_ref[number]
            sums = (
                prefix[column, pl.ds(LANE_ROWS - 1 + width, samples)]
                - prefix[column, LANE_ROWS - 1:LANE_ROWS - 1 + samples]
            )
            norm = lax.rsqrt(jnp.full((1, lanes), width * CHANS, jnp.int32).astype(jnp.float32))
            peak = jnp.max(sums, axis=0, keepdims=True) * norm
            best = peak if best is None else jnp.maximum(best, peak)
        out_ref[0, :, column * lanes:(column + 1) * lanes] = best


def trial_peaks(rows, box_widths, place):
    beams, devices, bands, samples = rows.shape
    total = devices * bands
    tiles = total // LANE_ROWS
    return pl.pallas_call(
        trial_kernel,
        grid_spec=pltpu.PrefetchScalarGridSpec(
            num_scalar_prefetch=2,
            grid=(beams,),
            in_specs=[pl.BlockSpec((1, devices, bands, samples), lambda b, p, w: (b, 0, 0, 0))],
            out_specs=pl.BlockSpec((1, 1, total), lambda b, p, w: (b, 0, 0)),
            scratch_shapes=[
                pltpu.VMEM((samples // LANES, total + LANE_ROWS * LANE_ROWS, LANES), jnp.float32),
                pltpu.VMEM((tiles, LANE_ROWS, samples), jnp.float32),
                pltpu.VMEM((tiles, LANE_ROWS, samples), jnp.float32),
                pltpu.VMEM((total, 2 * samples), jnp.bfloat16),
                pltpu.VMEM((total // LANES, LANE_ROWS + samples + WIDEST, LANES), jnp.float32),
            ],
        ),
        out_shape=jax.ShapeDtypeStruct((beams, 1, total), jnp.float32),
    )(place, box_widths, rows)[:, 0]


def compact(samples, devices, blocks, groups, beams, width):
    return (
        samples == 2 * LANES and NDM == 16 * samples and blocks == 4 and beams == groups
        and devices * LANE_ROWS == samples and width * devices == CHANS
    )


def block_span(block):
    return ((0, 4), (0, 4), (1, 4), (1, 4))[block]


def late_span(place, whole):
    return (0, 8) if place < whole else (4, 8)


def band_mask(depth, width):
    rows = LANE_ROWS * (2 << depth)
    row = lax.broadcasted_iota(jnp.int32, (rows, width), 0)
    channel = lax.broadcasted_iota(jnp.int32, (rows, width), 1)
    inner, tile = row % LANE_ROWS, row // LANE_ROWS
    if depth == 0:
        wanted = inner * 2 + tile
    else:
        quarter = tile % 4
        band = inner * 4 + (quarter % 2) * 2 + quarter // 2
        wanted = band * (rows // (4 * LANE_ROWS)) + tile // 4
    return channel // (width // rows) == wanted


def stepped(pair, amount):
    if amount == 0:
        return list(pair)
    lane = lane_index(pair[1].shape)
    near = lane < LANES - amount
    turned = [None if piece is None else pltpu.roll(piece, LANES - amount, 1) for piece in pair]
    early = None if turned[0] is None else jnp.where(near, turned[0], turned[1])
    return [early, jnp.where(near, turned[1], 0.0)]


def plus(low, high):
    return [a + b for a, b in zip(low, high)]


def near_leaves(tiles):
    wide = [plus(tiles[0], tiles[2]), plus(tiles[1], tiles[3])] if len(tiles) == 4 else tiles
    return plus_late(wide) + plus(wide[0], wide[1])


def plus_late(pair):
    return plus(pair[0], stepped(pair[1], 1))


def double_leaves(tiles):
    pairs = [plus_late([tiles[a], tiles[2 + a]]) for a in range(2)]
    return [pair[part] for part in range(2) for pair in pairs]


def far_leaves(tiles):
    parts = [tiles[at:at + 4] for at in range(0, len(tiles), 4)]
    halves = parts if len(parts) == 2 else [[plus(a, b) for a, b in zip(*parts[at:at + 2])] for at in (0, 2)]
    out = {1: [plus(low, stepped(high, 1)) for low, high in zip(*halves)]}
    if len(parts) == 4:
        one, two = [[plus(a, stepped(b, 1)) for a, b in zip(*parts[at:at + 2])] for at in (0, 2)]
        for block in (2, 3):
            out[block] = [plus(low, stepped(high, block - 1)) for low, high in zip(one, two)]
    return {block: [pair[part] for part in range(2) for pair in pairs] for block, pairs in out.items()}


def search_kernel(
    x_hbm, mask_hbm, widths_hbm, out_ref, x_ref, unit_ref, mask_ref, widths_ref, in_sem, send, send_sem, recv, recv_sem,
    twice, twice_sem, taken, taken_sem, peaks, answered, answer_sem, ready_sem, far, far_sem, relay, relay_sem, onward_sem, first, work, mid, planes, double, lower, series, prefix,
):
    beams, width, samples = x_ref.shape
    blocks, groups = lax.axis_size("freq"), lax.axis_size("beam")
    devices = blocks * groups
    row_total = float(beams * samples)
    my_block = lax.axis_index("freq")
    my_group = lax.axis_index("beam")
    my_place = my_block * groups + my_group
    quarter = groups // 2

    chunks = in_sem.shape[0] - 2
    span = width // chunks
    loads = [
        pltpu.make_async_copy(
            x_hbm.at[:, pl.ds(c * span, span)], x_ref.at[:, pl.ds(c * span, span)], in_sem.at[c]
        )
        for c in range(chunks)
    ]
    mask_load = pltpu.make_async_copy(mask_hbm, mask_ref, in_sem.at[chunks])
    widths_load = pltpu.make_async_copy(widths_hbm, widths_ref, in_sem.at[chunks + 1])
    loads[0].start()
    mask_load.start()
    for load in loads[1:]:
        load.start()
    widths_load.start()

    def signal(semaphore, block, group):
        pl.semaphore_signal(
            semaphore, inc=1, device_id={"freq": block, "beam": group}, device_id_type=pl.DeviceIdType.MESH,
        )

    barrier = pltpu.get_barrier_semaphore()

    @pl.when(my_block == 0)
    def _():
        for block in (3, 1, 2):
            for group in range(groups):
                signal(barrier, block, group)
        for step in range(1, groups):
            signal(barrier, 0, (my_group + step) % groups)

    @pl.when(my_block == 1)
    def _():
        for group in range(groups):
            signal(barrier, 0, group)
        for step in range(1, groups):
            signal(barrier, 1, (my_group + step) % groups)

    @pl.when(my_block >= 2)
    def _():
        pl.semaphore_wait(barrier, groups)
        for group in range(groups):
            signal(ready_sem, 0, group)

    for column in range(prefix.shape[0]):
        prefix[column, :LANE_ROWS] = jnp.zeros((LANE_ROWS, LANES), jnp.float32)
        prefix[column, LANE_ROWS + samples:] = jnp.full((WIDEST, LANES), -jnp.inf, jnp.float32)

    lane = lax.broadcasted_iota(jnp.int32, (LANE_ROWS, LANES), 1)
    inner = lax.broadcasted_iota(jnp.int32, (LANE_ROWS, LANES), 0)
    unit_ref[...] = jnp.ones(unit_ref.shape, jnp.bfloat16)
    means, scales = [], []
    for c in range(chunks):
        loads[c].wait()
        if c == 0:
            mask_load.wait()
        unit = unit_ref[...].astype(jnp.float32)
        totals = []
        for column in range(span // LANES):
            found = [jnp.zeros((LANE_ROWS, LANES), jnp.float32) for _ in range(2)]
            for pair in range(LANES // (2 * LANE_ROWS)):
                at = c * span + column * LANES + pair * 2 * LANE_ROWS
                sums = [jnp.zeros((2 * LANE_ROWS, samples), jnp.float32) for _ in range(2)]
                for b in range(beams):
                    wide = x_ref[b, at:at + 2 * LANE_ROWS].astype(jnp.float32)
                    sums = [sums[0] + wide * unit, sums[1] + wide * wide]
                sums = [jnp.sum(value, axis=1, keepdims=True) for value in sums]
                for half in range(2):
                    spot = lane == inner + (2 * pair + half) * LANE_ROWS
                    cut = slice(half * LANE_ROWS, (half + 1) * LANE_ROWS)
                    found = [have + jnp.where(spot, value[cut], 0.0) for have, value in zip(found, sums)]
            totals.append([jnp.sum(value, axis=0, keepdims=True) for value in found])
        mean = jnp.concatenate([total[0] for total in totals], axis=1) / row_total
        var = jnp.concatenate([total[1] for total in totals], axis=1) / row_total - mean * mean
        place = pl.multiple_of(my_group * width + c * span, span)
        clean = mask_ref[:, pl.ds(place, span)].astype(jnp.float32)
        means.append(mean)
        scales.append(lax.rsqrt(var + epsilon) * clean)
    channel_mean = jnp.concatenate(means, axis=1)
    channel_scale = jnp.concatenate(scales, axis=1)
    coarse = channel_scale.astype(jnp.bfloat16).astype(jnp.float32)
    fine = (channel_scale - coarse).astype(jnp.bfloat16).astype(jnp.float32)
    offset = channel_mean * (coarse + fine)

    def summing(depth):
        chosen = band_mask(depth, width)
        count = chosen.shape[0]
        matrix = jnp.concatenate(
            [jnp.where(chosen, coarse, 0.0), jnp.where(chosen, fine, 0.0)], axis=0
        ).astype(jnp.bfloat16)
        shift = jnp.sum(jnp.where(chosen, offset, 0.0), axis=1, keepdims=True)

        def tiles(slot):
            both = jnp.dot(matrix, x_ref[(my_group + slot) % beams], preferred_element_type=jnp.float32)
            sums = both[:count] + both[count:] - shift
            return [
                [sums[t:t + LANE_ROWS, p * LANES:(p + 1) * LANES] for p in range(2)]
                for t in range(0, count, LANE_ROWS)
            ]

        return tiles

    def message(block, slot, begin, end):
        return pltpu.make_async_remote_copy(
            src_ref=send.at[block, slot, pl.ds(begin, end - begin)],
            dst_ref=recv.at[my_place, pl.ds(begin, end - begin)],
            send_sem=send_sem.at[block, slot],
            recv_sem=recv_sem.at[my_place],
            device_id={"freq": block, "beam": (my_group + slot) % beams},
            device_id_type=pl.DeviceIdType.MESH,
        )

    def near_messages(action, slot, narrow):
        if narrow:
            action(message(0, slot, *block_span(2)))
            return

        @pl.when((my_block == 1) | (slot > 0))
        def _():
            action(message(0, slot, *block_span(0)))

    def double_messages(action, slot):
        def message(begin):
            return pltpu.make_async_remote_copy(
                src_ref=twice.at[slot, pl.ds(begin, 4 - begin)],
                dst_ref=taken.at[my_place, pl.ds(begin, 4 - begin)],
                send_sem=twice_sem.at[slot],
                recv_sem=taken_sem.at[my_place],
                device_id={"freq": 1, "beam": (my_group + slot) % beams},
                device_id_type=pl.DeviceIdType.MESH,
            )

        @pl.when(my_block == 0)
        def _():
            action(message(0))
        if slot > 0:
            @pl.when(my_block == 1)
            def _():
                action(message(2))

    def answer():
        return pltpu.make_async_remote_copy(
            src_ref=peaks, dst_ref=answered, send_sem=answer_sem.at[0], recv_sem=answer_sem.at[1],
            device_id={"freq": 0, "beam": my_group}, device_id_type=pl.DeviceIdType.MESH,
        )

    def near_phase(narrow, begin, end):
        tiles = summing(0 if narrow else 1)
        batch = 4
        for start in range(begin, end, batch):
            slots = range(start, start + batch)
            for slot, summed in [(slot, tiles(slot)) for slot in slots]:
                for number, leaf in enumerate(near_leaves(summed)):
                    if not narrow or number > 0:
                        send[0, slot, number] = leaf.astype(jnp.bfloat16)
                if not narrow:
                    for number, leaf in enumerate(double_leaves(summed)):
                        twice[slot, number] = leaf.astype(jnp.bfloat16)
                if slot == 0 and not narrow:
                    @pl.when(my_block == 0)
                    def _():
                        recv[my_place, :4] = send[0, 0, :4]

                    @pl.when(my_block == 1)
                    def _():
                        taken[my_place] = twice[0]
            if narrow:
                for slot in slots:
                    near_messages(lambda copy: copy.start(), slot, narrow)

    def next_messages(action, slot, low):
        action(message(1, slot, 0 if low else 4, 8))

    def by_half(source, action):
        for half in range(2):
            @pl.when((source * 2 >= quarter) if half else (source * 2 < quarter))
            def _(half=half):
                action(4 * half)

    def passed(row, begin):
        return pltpu.make_async_remote_copy(
            src_ref=far.at[quarter + row, :, pl.ds(begin, 8 - begin)],
            dst_ref=relay.at[row, :, pl.ds(begin, 8 - begin)],
            send_sem=far_sem.at[quarter + row, 0],
            recv_sem=relay_sem.at[row],
            device_id={"freq": 0, "beam": (my_group + quarter) % groups},
            device_id_type=pl.DeviceIdType.MESH,
        )

    def direct(beam, block, begin):
        return pltpu.make_async_remote_copy(
            src_ref=far.at[beam, block - 2, pl.ds(begin, 8 - begin)],
            dst_ref=recv.at[my_place, pl.ds(begin, 8 - begin)],
            send_sem=far_sem.at[beam, block - 2],
            recv_sem=recv_sem.at[my_place],
            device_id={"freq": block, "beam": beam},
            device_id_type=pl.DeviceIdType.MESH,
        )

    def onward(row, block, begin):
        return pltpu.make_async_remote_copy(
            src_ref=relay.at[row, block - 2, pl.ds(begin, 8 - begin)],
            dst_ref=recv.at[my_place - quarter, pl.ds(begin, 8 - begin)],
            send_sem=onward_sem.at[row, block - 2],
            recv_sem=recv_sem.at[my_place - quarter],
            device_id={"freq": block, "beam": quarter + row},
            device_id_type=pl.DeviceIdType.MESH,
        )

    def far_phase(low):
        tiles = summing(3 if low else 2)
        batch = 2
        for begin in range(0, beams, batch):
            slots = range(begin, begin + batch)
            for slot, summed in [(slot, tiles(slot)) for slot in slots]:
                for block, leaves in far_leaves(summed).items():
                    for number, leaf in enumerate(leaves):
                        if block == 1:
                            send[block, slot, number] = leaf.astype(jnp.bfloat16)
                        else:
                            far[(my_group + slot) % beams, block - 2, number] = leaf.astype(jnp.bfloat16)
            if not low:
                for slot in slots:
                    next_messages(lambda copy: copy.start(), slot, low)

    def landed(target, semaphore):
        pltpu.make_async_remote_copy(
            src_ref=target, dst_ref=target, send_sem=send_sem.at[0, 0], recv_sem=semaphore,
            device_id={"freq": my_block, "beam": my_group}, device_id_type=pl.DeviceIdType.MESH,
        ).wait_recv()

    def arrival(place, begin, end):
        landed(recv.at[place, pl.ds(begin, end - begin)], recv_sem.at[place])

    args = (recv, first, work, mid, series)
    pitch = first.shape[1] // LANE_ROWS

    def wide_places(count, numbers_of):
        per = count // LANE_ROWS
        return [
            ((place // per) * pitch + (place % per) * (pitch - LANE_ROWS) // per + address, place, numbers)
            for place in range(count) for address, numbers in numbers_of(place)
        ]

    @pl.when(my_block < 2)
    def _():
        near_phase(False, 0, beams)

        @pl.when((my_block == 0) & (my_group < quarter))
        def _():
            far_phase(True)

        pl.semaphore_wait(barrier, 2 * groups - 1)
        for slot in range(beams):
            double_messages(lambda copy: copy.start(), slot)
        for slot in range(beams):
            near_messages(lambda copy: copy.start(), slot, False)

        @pl.when((my_block == 0) & (my_group < quarter))
        def _():
            by_half(my_group, lambda begin: [passed(row, begin).start() for row in range(quarter)])
            for slot in range(beams):
                next_messages(lambda copy: copy.start(), slot, True)

        @pl.when((my_block == 0) & (my_group >= quarter))
        def _():
            far_phase(False)

    @pl.when(my_block >= 2)
    def _():
        near_phase(True, 0, beams)

    widths_load.wait()

    @pl.when(my_block == 0)
    def _():
        for place in range(groups):
            @pl.when(place != my_group)
            def _(place=place):
                arrival(place, *block_span(0))
        both = ((2, 3), (0, 1))
        plane_rows(recv, first, mid, groups, [(planes.at[root], 0, root, (both[root],)) for root in range(2)])

        pl.semaphore_wait(ready_sem, 2 * groups)

        @pl.when(my_group < quarter)
        def _():
            by_half(my_group, lambda begin: [
                direct(beam, block, begin).start() for beam in range(quarter) for block in (3, 2)
            ])

        @pl.when(my_group >= quarter)
        def _():
            def pass_on(begin):
                for row in range(quarter):
                    landed(relay.at[row, :, pl.ds(begin, 8 - begin)], relay_sem.at[row])
                    for block in (3, 2):
                        onward(row, block, begin).start()

            by_half(my_group - quarter, pass_on)

        for place in range(groups, 2 * groups):
            arrival(place, *block_span(1))
        plane_rows(recv, first, mid, groups, [(planes.at[root], 1, root, (both[root],)) for root in range(2)])
        lower_rows(planes, lower)
        late = ((2, 3), (None, 1))
        for plane in range(2, blocks):
            for place in range(plane * groups, (plane + 1) * groups):
                arrival(place, *block_span(2))
            plane_rows(recv, first, mid, groups, [(planes.at[root], plane, root, (late[root],)) for root in range(2)])
        upper_rows(planes, lower, series)
        result = boxcar_rows(widths_ref, series, prefix, 2, 4)
        unfolded(result[:2], out_ref, 0)
        unfolded(result[2:], out_ref, 256)
        landed(answered, answer_sem.at[1])
        unpermuted([answered[column] for column in range(2)], out_ref, 512, 1, 4)

    @pl.when(my_block == 1)
    def _():
        for place in range(groups, 2 * groups):
            @pl.when(place != my_place)
            def _(place=place):
                landed(taken.at[place, pl.ds(2, 2)], taken_sem.at[place])
        plane_rows(taken, first, mid, groups, [(double, 1, 1, ((None, 2), (None, 3)))])
        for place in range(groups):
            landed(taken.at[place], taken_sem.at[place])
        plane_rows(taken, first, mid, groups, [(double, 0, 1, ((0, 2), (1, 3)))])
        double_rows(double, series, 256)
        for number, column in enumerate(boxcar_rows(widths_ref, series, prefix, 2, 2)):
            peaks[number] = column
        answer().start()
        for place in range(groups):
            arrival(place, *late_span(place, quarter))
        unit_rows(*args, 0, 1, 256, 2, wide_places(
            groups,
            lambda place: [
                (8 * (2 * (q % 2) + q // 2), (q if place < quarter else None, 4 + q)) for q in range(4)
            ],
        ))
        unpermuted(boxcar_rows(widths_ref, series, prefix, 0, 2), out_ref, 0, 2, 3)
        answer().wait_send()

    for late in (2, 3):
        @pl.when(my_block == late)
        def _(late=late):
            found = []
            for place in range(quarter):
                arrival(place, *late_span(place, quarter // 2))
                for q in range(4):
                    found.append((
                        (2 * (q % 2) + q // 2) * pitch + place * LANE_ROWS, place,
                        (q if 2 * place < quarter else None, 4 + q),
                    ))
            unit_rows(*args, 0, late, 128, 2, found)
            unpermuted(boxcar_rows(widths_ref, series, prefix, 0, 1), out_ref, 0, 3, 3)

    for slot in range(beams):
        for narrow in (True, False):
            @pl.when((my_block >= 2) == narrow)
            def _(narrow=narrow, slot=slot):
                near_messages(lambda copy: copy.wait_send(), slot, narrow)
                if not narrow:
                    double_messages(lambda copy: copy.wait_send(), slot)
        for low in (True, False):
            @pl.when((my_block == 0) & ((my_group < quarter) == low))
            def _(low=low, slot=slot):
                next_messages(lambda copy: copy.wait_send(), slot, low)

    @pl.when((my_block == 0) & (my_group < quarter))
    def _():
        by_half(my_group, lambda begin: [passed(row, begin).wait_send() for row in range(quarter)])
        by_half(my_group, lambda begin: [
            direct(beam, block, begin).wait_send() for beam in range(quarter) for block in (3, 2)
        ])

    @pl.when((my_block == 0) & (my_group >= quarter))
    def _():
        by_half(my_group - quarter, lambda begin: [
            onward(row, block, begin).wait_send() for row in range(quarter) for block in (3, 2)
        ])


def search(intensity, channel_mask, box_widths):
    beams, width, samples = intensity.shape
    blocks, groups = lax.axis_size("freq"), lax.axis_size("beam")
    devices = blocks * groups
    operands = (intensity, channel_mask.reshape(1, -1), box_widths)
    return pl.pallas_call(
        search_kernel,
        in_specs=[pl.BlockSpec(memory_space=pl.ANY)] * 3,
        out_specs=pl.BlockSpec(memory_space=pltpu.VMEM),
        scratch_shapes=[
            pltpu.VMEM((beams, width, samples), jnp.bfloat16),
            pltpu.VMEM((2 * LANE_ROWS, samples), jnp.bfloat16),
            pltpu.VMEM((1, width * groups), jnp.int32),
            pltpu.SMEM(box_widths.shape, jnp.int32),
            pltpu.SemaphoreType.DMA((6,)),
            pltpu.VMEM((2, beams, 8, LANE_ROWS, LANES), jnp.bfloat16),
            pltpu.SemaphoreType.DMA((2, beams)),
            pltpu.VMEM((devices, 8, LANE_ROWS, LANES), jnp.bfloat16),
            pltpu.SemaphoreType.DMA((devices,)),
            pltpu.VMEM((beams, 4, LANE_ROWS, LANES), jnp.bfloat16),
            pltpu.SemaphoreType.DMA((beams,)),
            pltpu.VMEM((2 * groups, 4, LANE_ROWS, LANES), jnp.bfloat16),
            pltpu.SemaphoreType.DMA((2 * groups,)),
            pltpu.VMEM((2, LANE_ROWS, LANES), jnp.float32),
            pltpu.VMEM((2, LANE_ROWS, LANES), jnp.float32),
            pltpu.SemaphoreType.DMA((2,)),
            pltpu.SemaphoreType.REGULAR,
            pltpu.VMEM((beams, 2, 8, LANE_ROWS, LANES), jnp.bfloat16),
            pltpu.SemaphoreType.DMA((beams, 2)),
            pltpu.VMEM((groups // 2, 2, 8, LANE_ROWS, LANES), jnp.bfloat16),
            pltpu.SemaphoreType.DMA((groups // 2,)),
            pltpu.SemaphoreType.DMA((groups // 2, 2)),
            pltpu.VMEM((2, samples + LANE_ROWS * LANE_ROWS, LANES), jnp.float32),
            pltpu.VMEM((2, samples, LANES), jnp.float32),
            pltpu.VMEM((2, samples, LANES), jnp.float32),
            pltpu.VMEM((2, blocks, 2, LANE_ROWS * LANE_ROWS, LANES), jnp.float32),
            pltpu.VMEM((2, 2, LANES, LANES), jnp.float32),
            pltpu.VMEM((2, 2, LANES, LANES), jnp.float32),
            pltpu.VMEM((3 * samples, 2 * samples), jnp.bfloat16),
            pltpu.VMEM((6, LANE_ROWS + samples + WIDEST, LANES), jnp.float32),
        ],
        out_shape=jax.ShapeDtypeStruct((1, NDM // blocks), jnp.float32),
        compiler_params=pltpu.CompilerParams(collective_id=0, has_side_effects=True, vmem_limit_bytes=32 << 20),
    )(*[pltpu.with_memory_space_constraint(value, pltpu.HBM) for value in operands])


def ramped(pair, start, stride, far, only_late=False):
    shape = pair[1].shape
    reach = (LANE_ROWS - 1) * stride
    place = lane_index(shape) + (start + reach - lax.broadcasted_iota(jnp.int32, shape, 0) * stride)
    turn = (-start - reach) % LANES

    def turned(piece):
        if turn + reach < LANES:
            return pltpu.roll(piece, turn, 1, stride=stride, stride_axis=0)
        return jnp.take_along_axis(piece, place & (LANES - 1), axis=1, mode="promise_in_bounds")

    late = turned(pair[1])
    if far:
        return [jnp.where(place < 2 * LANES, late, 0.0), None]
    near = place < LANES
    early = None if only_late else jnp.where(near, turned(pair[0]), late)
    return [early, jnp.where(near, late, 0.0)]


def joined_pair(low, high):
    return [a if b is None else (None if a is None else a + b) for a, b in zip(low, high)]


def unit_rows(recv, first, work, mid, series, base, root, leaves, kinds, found):
    tiles = leaves // LANE_ROWS
    pitch = first.shape[1] // LANE_ROWS
    for address, place, numbers in found:
        for part in range(2):
            if numbers[part] is not None:
                first[part, address:address + LANE_ROWS] = recv[place, numbers[part]].astype(jnp.float32)

    def leaf(tile, part):
        outer, kind = tile >> kinds, tile & ((1 << kinds) - 1)
        if leaves == LANE_ROWS * (pitch - LANE_ROWS):
            spot, step = ((outer >> 3 << kinds) + kind) * LANE_ROWS + (outer & 7), pitch
        else:
            spot, step = kind * pitch + outer, LANE_ROWS // 2
        return first[part, pl.ds(spot, LANE_ROWS, stride=step)]

    chunk = 8
    for c in range(tiles // chunk):
        tree = [[[leaf(c * chunk + k, part) for part in range(2)]] for k in range(chunk)]
        level_root = root
        while len(tree) > 1:
            tree = [
                [
                    plus(low[r // 2], stepped(high[r // 2], level_root + r // 2 + r % 2))
                    for r in range(2 * len(low))
                ]
                for low, high in zip(tree[0::2], tree[1::2])
            ]
            level_root = level_root * 2
        for j in range(chunk):
            for part in range(2):
                at = (j * (tiles // chunk) + c) * LANE_ROWS
                work[part, at:at + LANE_ROWS] = tree[0][j][part]
    chunks = tiles // chunk
    for j in range(chunk):
        tree = []
        for c in range(chunks):
            at = (j * chunks + c) * LANE_ROWS
            tree.append([[work[part, at:at + LANE_ROWS] for part in range(2)]])
        level_root = root * chunk + j
        while len(tree) > 1:
            tree = [
                [
                    plus(low[r // 2], stepped(high[r // 2], level_root + r // 2 + r % 2))
                    for r in range(2 * len(low))
                ]
                for low, high in zip(tree[0::2], tree[1::2])
            ]
            level_root = level_root * 2
        for k in range(chunks):
            for part in range(2):
                at = (j * chunks + k ^ LANE_ROWS - 1) * LANE_ROWS
                mid[part, at:at + LANE_ROWS] = tree[0][k][part]
    far = root > 0
    for g in range(tiles // LANE_ROWS):
        tree = []
        for s in range(LANE_ROWS):
            pair = [
                None if far and 2 * s >= LANE_ROWS and part == 0
                else mid[part, pl.ds(g * LANE_ROWS * LANE_ROWS + s, LANE_ROWS, stride=LANE_ROWS)]
                for part in range(2)
            ]
            tree.append([pair])
        rows = merged_rows(tree, root * tiles + g * LANE_ROWS, 1, far)
        for k in range(0, LANE_ROWS, 2):
            save_series(series, base + g * LANE_ROWS * LANE_ROWS + k * LANE_ROWS, rows[k:k + 2])


def merged_rows(tree, start, stride, far):
    while len(tree) > 1:
        tree = [
            [
                joined_pair(
                    low[r // 2],
                    ramped(
                        high[r // 2], start + r // 2 + r % 2, stride, far and len(tree) == 2,
                        high[r // 2][0] is None,
                    ),
                )
                for r in range(2 * len(low))
            ]
            for low, high in zip(tree[0::2], tree[1::2])
        ]
        start, stride = start * 2, stride * 2
    return tree[0]


def plane_rows(recv, first, mid, groups, jobs):
    flat = LANE_ROWS * LANE_ROWS
    origins, origin = [], 0
    for target, plane, root, numbers in jobs:
        origins.append(origin)
        origin += len(numbers) * flat
    used = [[part for part in range(2) if numbers[0][part] is not None] for _, _, _, numbers in jobs]
    for (target, plane, root, numbers), origin, parts in zip(jobs, origins, used):
        for place in range(groups):
            for kind in range(len(numbers)):
                for part in parts:
                    at = origin + kind * flat + place * LANE_ROWS
                    rows = recv[plane * groups + place, numbers[kind][part]]
                    first[part, at:at + LANE_ROWS] = rows.astype(jnp.float32)

    def pair_at(source, parts, start):
        return [source[part, pl.ds(start, LANE_ROWS, stride=LANE_ROWS)] if part in parts else None for part in range(2)]

    for (target, plane, root, numbers), origin, parts in zip(jobs, origins, used):
        kinds = len(numbers)
        tree = [
            [pair_at(first, parts, origin + (tile % kinds) * flat + tile // kinds)]
            for tile in range(kinds * LANE_ROWS)
        ]
        level_root = root
        while len(tree) > 1:
            tree = [
                [
                    joined_pair(low[r // 2], stepped(high[r // 2], level_root + r // 2 + r % 2))
                    for r in range(2 * len(low))
                ]
                for low, high in zip(tree[0::2], tree[1::2])
            ]
            level_root = level_root * 2
        for j, pair in enumerate(tree[0]):
            for part in parts:
                at = origin + (j ^ LANE_ROWS - 1) * LANE_ROWS
                mid[part, at:at + LANE_ROWS] = pair[part]
    for (target, plane, root, numbers), origin, parts in zip(jobs, origins, used):
        for g in range(len(numbers)):
            tree = [[pair_at(mid, parts, origin + g * flat + p)] for p in range(LANE_ROWS)]
            for k, pair in enumerate(merged_rows(tree, (root * len(numbers) + g) * LANE_ROWS, 1, False)):
                at = g * flat + k * LANE_ROWS
                for part in parts:
                    target[plane, part, at:at + LANE_ROWS] = pair[part]


def double_rows(target, series, base):
    for g in range(2):
        for k in range(LANE_ROWS):
            number = g * LANE_ROWS + k
            tree = [[plane_tile(target, 0, number, (0, 1))], [plane_tile(target, 1, number, (1,))]]
            rows = merged_rows(tree, LANES + g * LANE_ROWS * LANE_ROWS + k, LANE_ROWS, True)
            save_series(series, base + 2 * number * LANE_ROWS, rows)


def plane_tile(target, plane, k, parts):
    return [
        target[plane, part, k * LANE_ROWS:(k + 1) * LANE_ROWS] if part in parts else None for part in range(2)
    ]


def lower_rows(planes, lower):
    for k in range(LANE_ROWS):
        for root in range(2):
            tree = [[plane_tile(planes.at[root], plane, k, (0, 1))] for plane in range(2)]
            for q, pair in enumerate(merged_rows(tree, root * LANE_ROWS * LANE_ROWS + k, LANE_ROWS, False)):
                for part in range(2):
                    at = (2 * k + q) * LANE_ROWS
                    lower[root, part, at:at + LANE_ROWS] = pair[part]


def upper_rows(planes, lower, series):
    for root in range(2):
        parts = (0, 1) if root == 0 else (1,)
        for k in range(LANE_ROWS):
            begin = root * LANE_ROWS * LANE_ROWS + k
            tree = [[plane_tile(planes.at[root], plane, k, parts)] for plane in (2, 3)]
            high = merged_rows(tree, begin, LANE_ROWS, False)
            low = []
            for q in range(2):
                at = (2 * k + q) * LANE_ROWS
                low.append([lower[root, part, at:at + LANE_ROWS] for part in range(2)])
            rows = merged_rows([low, high], begin * 2, 2 * LANE_ROWS, root > 0)
            for number in range(0, 4, 2):
                at = (32 * (1 + root) + 4 * k + number) * LANE_ROWS
                save_series(series, at, rows[number:number + 2])


def save_series(series, at, pairs):
    rows = jnp.concatenate([jnp.concatenate(pair, axis=1) for pair in pairs], axis=0)
    coarse = rows.astype(jnp.bfloat16)
    samples = rows.shape[1]
    series[at:at + 2 * LANE_ROWS, :samples] = coarse
    series[at:at + 2 * LANE_ROWS, samples:] = (rows - coarse.astype(jnp.float32)).astype(jnp.bfloat16)


def unfolded(columns, out_ref, offset):
    lane = lane_index((LANE_ROWS, LANES))
    for number in range(2):
        picks = (lane & 15) * LANE_ROWS + (LANE_ROWS - 1) - (lane >> 5) - 4 * number
        spread = [jnp.take_along_axis(column, picks, axis=1, mode="promise_in_bounds") for column in columns]
        at = offset + number * LANES
        out_ref[:, at:at + LANES] = jnp.where(lane & 16 == 0, spread[0], spread[1])[:1]


def boxcar_rows(widths_ref, series, prefix, begin, count):
    lanes = prefix.shape[2]
    samples = series.shape[1] // 2
    until = lax.broadcasted_iota(jnp.int32, (samples, 2 * samples), 0)
    time = lax.broadcasted_iota(jnp.int32, (samples, 2 * samples), 1) & (samples - 1)
    ladder = jnp.where(time <= until, 1.0, 0.0).astype(jnp.bfloat16)
    piece = min(2, count)
    for start in range(begin, begin + count, piece):
        sums = lax.dot_general(
            ladder, series[start * lanes:(start + piece) * lanes], (((1,), (1,)), ((), ())),
            preferred_element_type=jnp.float32,
        )
        for side in range(piece):
            prefix[start + side, LANE_ROWS:LANE_ROWS + samples] = sums[:, side * lanes:(side + 1) * lanes]
    widths = [widths_ref[number] for number in range(widths_ref.shape[0])]
    norms = [
        lax.rsqrt(jnp.full((LANE_ROWS, lanes), width * CHANS, jnp.int32).astype(jnp.float32)) for width in widths
    ]
    result = []
    for column in range(begin, begin + count):
        ahead = [prefix[column, pl.ds(LANE_ROWS - 1 + width, samples)] for width in widths]
        base = prefix[column, LANE_ROWS - 1:LANE_ROWS - 1 + samples]
        best = [None] * len(widths)
        for at in range(0, samples, LANE_ROWS):
            before = base[at:at + LANE_ROWS]
            for number, after in enumerate(ahead):
                gain = after[at:at + LANE_ROWS] - before
                best[number] = gain if at == 0 else jnp.maximum(best[number], gain)
        peak = best[0] * norms[0]
        for value, norm in zip(best[1:], norms[1:]):
            peak = jnp.maximum(peak, value * norm)
        result.append(jnp.broadcast_to(jnp.max(peak, axis=0, keepdims=True), (LANE_ROWS, lanes)))
    return result


def unpermuted(columns, out_ref, offset, repeat_bits, bits):
    lane = lane_index((LANE_ROWS, LANES))
    for number in range(len(columns) << repeat_bits):
        row = (lane + number * LANES) >> repeat_bits
        row = row & (LANES - 1)
        block = LANE_ROWS << bits
        picks = (row & (LANES - block)) + (row & ((1 << bits) - 1)) * LANE_ROWS + (LANE_ROWS - 1) - ((row & (block - 1)) >> bits)
        column = columns[number >> repeat_bits]
        spread = jnp.take_along_axis(column, picks, axis=1, mode="promise_in_bounds")
        at = offset + number * LANES
        out_ref[:, at:at + LANES] = spread[:1]


def shards(intensity, channel_mask, box_widths):
    beams, width, samples = intensity.shape
    blocks, groups = lax.axis_size("freq"), lax.axis_size("beam")
    if compact(samples, blocks * groups, blocks, groups, beams, width):
        return search(intensity, channel_mask, box_widths)
    rows = entry_rows(intensity, channel_mask)
    return trial_peaks(rows, box_widths, lax.axis_index("freq").reshape(1))


def solution(mesh):
    in_specs = (P(None, ("freq", "beam"), None), P("freq"), P())
    out_specs = P("beam", "freq")
    return jax.shard_map(shards, mesh=mesh, in_specs=in_specs, out_specs=out_specs, check_vma=False)
```
